256 devices in a mesh: sweep: 16 (over z, y_hi), cross: 16 (over y_lo, x, core).
Axes of the slice: x: 4, y: 4 (y_hi: 2, y_lo: 2; y = y_hi * 2 + y_lo), z: 8, core: 2. Of those that a mesh axis runs over, the one named last changes fastest.
Arguments:
- right_side: bfloat16 [32, 64, 320, 128], P('sweep', 'cross'), may hold values from -6 to 6
- diag_inv: bfloat16 [32, 64, 320, 320], P('sweep', 'cross')
- diag_blk: bfloat16 [32, 64, 320, 320], P('sweep', 'cross')
- lower_blk: bfloat16 [32, 64, 320, 320], P('sweep', 'cross')
- upper_blk: bfloat16 [32, 64, 320, 320], P('sweep', 'cross')
- cross_minus: bfloat16 [32, 64, 320, 320], P('sweep', 'cross')
- cross_plus: bfloat16 [32, 64, 320, 320], P('sweep', 'cross')
- elem_slot: int32 [32, 64], P('sweep', 'cross'), may hold values from 0 to 7, as said below
Outputs:
- precond: bfloat16 [32, 64, 320, 128], P('sweep', 'cross')
- jacobian_prod: bfloat16 [32, 64, 320, 128], P('sweep', 'cross')
The draws below stay inside these ranges and needn't reach their ends.
Inputs may be any that keep to these rules, and one draw needn't show every extreme that they name: `elem_slot`: within each aligned block of 2 slabs by 4 pencils the entries are a permutation of 0 to 7.
All inputs are finite; a program needn't handle non-finite values.
Results may differ from the reference program's by a relative error of at most 0.0083.
Values may be sent and summed in bfloat16 or wider, within the bound.
No kernel may reach another device: no remote copies, remote signals or barrier semaphores. Data moves between devices by JAX's collectives and lax.ppermute only.
A program may use at most 256 MiB of HBM per device.

```python
import math
import jax
import jax.numpy as jnp
from jax import lax

BLOCK = 320
COLS = 128
SLABS = 2
PENCILS = 4
NSLAB = 32
NPENCIL = 64


def coupling_block(key, diag_low, diag_high, sign_value, spread):
    key_diag, key_rest = jax.random.split(key)
    block_shape = (NSLAB, NPENCIL, BLOCK)
    diagonal_vals = jnp.exp(jax.random.uniform(key_diag, block_shape, jnp.float32, math.log(diag_low), math.log(diag_high)))
    jitter = jax.random.normal(key_rest, block_shape + (BLOCK,), jnp.float32)
    identity_mat = jnp.eye(BLOCK, dtype=jnp.float32)
    result = sign_value * diagonal_vals[..., None] * identity_mat + jitter * (spread / math.sqrt(BLOCK))
    return result.astype(jnp.bfloat16)


def draw_diag_inv(key, part):
    return coupling_block(jax.random.fold_in(key, 11), 0.93, 1.0, 1.0, 0.19)


def draw_diag_blk(key, part):
    return coupling_block(jax.random.fold_in(key, 12), 1.0, 2.5, 1.0, 0.3)


def draw_lower_blk(key, part):
    return coupling_block(jax.random.fold_in(key, 13), 0.72, 0.96, -1.0, 0.17)


def draw_upper_blk(key, part):
    return coupling_block(jax.random.fold_in(key, 14), 0.72, 0.96, -1.0, 0.17)


def draw_cross_minus(key, part):
    return coupling_block(jax.random.fold_in(key, 15), 0.2, 0.6, -1.0, 0.15)


def draw_cross_plus(key, part):
    return coupling_block(jax.random.fold_in(key, 16), 0.2, 0.6, -1.0, 0.15)


def draw_elem_slot(key, part):
    groups = NSLAB // SLABS * (NPENCIL // PENCILS)
    keys_all = jax.random.split(jax.random.fold_in(key, 71), groups)
    orders = jax.vmap(lambda one_key: jax.random.permutation(one_key, SLABS * PENCILS))(keys_all)
    orders = orders.reshape(NSLAB // SLABS, NPENCIL // PENCILS, SLABS, PENCILS)
    orders = orders.transpose(0, 2, 1, 3).reshape(NSLAB, NPENCIL)
    return orders.astype(jnp.int32)


def levels(own_key, extent, shards, low, high):
    factor_of = 1.0
    for position, shards_of in shards:
        heights = jax.random.uniform(jax.random.fold_in(jax.random.fold_in(own_key, 6), position), (shards_of,), jnp.float32, low / len(shards), high / len(shards))
        factor_of = factor_of * jnp.repeat(jnp.exp(heights), extent[position] // shards_of).reshape((-1,) + (1,) * (len(extent) - 1 - position))
    return factor_of


def normal_values(stream_key, extent, scale, most, cuts=(), kind=jnp.bfloat16):
    factor_of = levels(stream_key, extent, cuts, -0.22, 0.18) if cuts else 1.0
    entries = jax.random.normal(stream_key, extent, jnp.float32) * scale * factor_of
    return jnp.minimum(jnp.maximum(entries, -most), most).astype(kind)


def setup_inputs(seed: int = 0) -> dict:
    seeds = jax.random.split(jax.random.key(seed), 9)
    right_side = normal_values(seeds[0], (NSLAB, NPENCIL, BLOCK, COLS), 1.0, 6.0, ((0, 16), (1, 16)))
    diag_inv = draw_diag_inv(jax.random.fold_in(seeds[8], 71), 0)
    diag_blk = draw_diag_blk(jax.random.fold_in(seeds[8], 71), 0)
    lower_blk = draw_lower_blk(jax.random.fold_in(seeds[8], 71), 0)
    upper_blk = draw_upper_blk(jax.random.fold_in(seeds[8], 71), 0)
    cross_minus = draw_cross_minus(jax.random.fold_in(seeds[8], 71), 0)
    cross_plus = draw_cross_plus(jax.random.fold_in(seeds[8], 71), 0)
    elem_slot = draw_elem_slot(jax.random.fold_in(seeds[8], 71), 0)
    return {"right_side": right_side, "diag_inv": diag_inv, "diag_blk": diag_blk, "lower_blk": lower_blk, "upper_blk": upper_blk, "cross_minus": cross_minus, "cross_plus": cross_plus, "elem_slot": elem_slot}


def apply_blocks(blocks, vectors):
    return jnp.einsum("pij,pjr->pir", blocks.astype(jnp.float32), vectors.astype(jnp.float32), precision=lax.Precision.HIGHEST)


def storage_place(elem_slot):
    slab_ids = jnp.arange(NSLAB, dtype=jnp.int32)[:, None]
    pencil_ids = jnp.arange(NPENCIL, dtype=jnp.int32)[None, :]
    store_rows = SLABS * (slab_ids // SLABS) + elem_slot // PENCILS
    store_cols = PENCILS * (pencil_ids // PENCILS) + elem_slot % PENCILS
    return store_rows.astype(jnp.int32), store_cols.astype(jnp.int32)


def reference(right_side, diag_inv, diag_blk, lower_blk, upper_blk, cross_minus, cross_plus, elem_slot):
    store_rows, store_cols = storage_place(elem_slot)
    slab_list = jnp.arange(NSLAB, dtype=jnp.int32)
    zero_front = jnp.zeros((NPENCIL, BLOCK, COLS), jnp.float32)

    def forward(front_in, slab):
        where_rows = store_rows[slab]
        where_cols = store_cols[slab]
        inverse = diag_inv[where_rows, where_cols]
        lower = lower_blk[where_rows, where_cols]
        source = right_side[where_rows, where_cols].astype(jnp.float32)
        value = apply_blocks(inverse, source - apply_blocks(lower, front_in))
        return value, value

    _, forward_vals = lax.scan(forward, zero_front, slab_list)

    def backward(front_in, inputs):
        slab, value = inputs
        where_rows = store_rows[slab]
        where_cols = store_cols[slab]
        inverse = diag_inv[where_rows, where_cols]
        upper = upper_blk[where_rows, where_cols]
        solved = value - apply_blocks(inverse, apply_blocks(upper, front_in))
        return solved, solved

    _, solved_vals = lax.scan(backward, zero_front, (slab_list, forward_vals), reverse=True)
    precond_sorted = solved_vals.astype(jnp.bfloat16)
    padded = jnp.pad(precond_sorted, ((1, 1), (1, 1), (0, 0), (0, 0)))

    def jacobian(slab):
        where_rows = store_rows[slab]
        where_cols = store_cols[slab]
        center = lax.dynamic_index_in_dim(padded, slab + 1, 0, keepdims=False)
        below = lax.dynamic_index_in_dim(padded, slab, 0, keepdims=False)
        above = lax.dynamic_index_in_dim(padded, slab + 2, 0, keepdims=False)
        total = apply_blocks(diag_blk[where_rows, where_cols], center[1:-1])
        total = total + apply_blocks(lower_blk[where_rows, where_cols], below[1:-1])
        total = total + apply_blocks(upper_blk[where_rows, where_cols], above[1:-1])
        total = total + apply_blocks(cross_minus[where_rows, where_cols], center[:-2])
        total = total + apply_blocks(cross_plus[where_rows, where_cols], center[2:])
        return total.astype(jnp.bfloat16)

    jac_sorted = lax.map(jacobian, slab_list)
    precond = jnp.zeros_like(right_side).at[store_rows, store_cols].set(precond_sorted)
    jacobian_prod = jnp.zeros_like(right_side).at[store_rows, store_cols].set(jac_sorted)
    return (precond, jacobian_prod)
```

```python
import jax
import jax.numpy as jnp
from jax import lax
from jax.experimental import pallas as pl
from jax.experimental.pallas import tpu as pltpu
from jax.sharding import PartitionSpec as P

BF = jnp.bfloat16
F32 = jnp.float32
GROUP = 4
VMEM_LIMIT = 48 << 20


def mm(a, b):
    return jnp.dot(a, b, preferred_element_type=F32)


def packed_rows(n):
    return 2 * n + n // 2


def pack(ref, base, mat):
    n = mat.shape[0]
    half = n // 2
    ref[base : base + n, :] = mat[:, 0:128]
    ref[base + n : base + 2 * n, :] = mat[:, 128:256]
    ref[base + 2 * n : base + 2 * n + half, 0:64] = mat[0:half, 256:320]
    ref[base + 2 * n : base + 2 * n + half, 64:128] = mat[half:n, 256:320]


def unpack(ref, base, n):
    half = n // 2
    tail = ref[base + 2 * n : base + 2 * n + half, :]
    last = jnp.concatenate([tail[:, 0:64], tail[:, 64:128]], axis=0)
    return jnp.concatenate(
        [ref[base : base + n, :], ref[base + n : base + 2 * n, :], last], axis=1
    )


def local_maps_kernel(
    slots, d0, d1, l0, l1, u0, u1, r0, r1, maps, e0_out, a_out, h0_out, h1_out, y0_out, c_out
):
    n = d0.shape[0]
    rows = packed_rows(n)
    inv0, inv1 = d0[...], d1[...]
    e0 = mm(inv0, l0[...]).astype(BF)
    e1 = mm(inv1, l1[...]).astype(BF)
    h0 = mm(inv0, u0[...]).astype(BF)
    h1 = mm(inv1, u1[...]).astype(BF)
    y0 = mm(inv0, r0[...])
    y1 = mm(inv1, r1[...])
    a = mm(e1, e0).astype(BF)
    b = mm(h0, h1).astype(BF)
    c = y1 - mm(e1, y0.astype(BF))
    cb = c.astype(BF)
    g = -(e0.astype(F32) + mm(h0, a))
    h = y0 - mm(h0, cb)
    pack(maps, 0, a)
    pack(maps, rows, b)
    pack(maps, 2 * rows, g.astype(BF))
    maps[3 * rows : 3 * rows + n, :] = cb
    maps[3 * rows + n : 3 * rows + 2 * n, :] = h.astype(BF)
    e0_out[...] = e0
    a_out[...] = a
    h0_out[...] = h0
    h1_out[...] = h1
    y0_out[...] = y0
    c_out[...] = c


def local_maps(slots, diag_inv, lower, upper, source):
    n = diag_inv.shape[-1]
    cols = source.shape[-1]
    rows = 3 * packed_rows(n) + 2 * n

    def block(slab, width):
        return pl.BlockSpec((None, n, width), lambda p, sl: (sl[slab * GROUP + p], 0, 0))

    def out(width, height=n):
        return pl.BlockSpec((None, height, width), lambda p, sl: (p, 0, 0))

    shape = jax.ShapeDtypeStruct
    return pl.pallas_call(
        local_maps_kernel,
        grid_spec=pltpu.PrefetchScalarGridSpec(
            num_scalar_prefetch=1,
            grid=(GROUP,),
            in_specs=[
                block(0, n), block(1, n), block(0, n), block(1, n),
                block(0, n), block(1, n), block(0, cols), block(1, cols),
            ],
            out_specs=[out(cols, rows), out(n), out(n), out(n), out(n), out(cols), out(cols)],
        ),
        out_shape=[
            shape((GROUP, rows, cols), BF),
            shape((GROUP, n, n), BF),
            shape((GROUP, n, n), BF),
            shape((GROUP, n, n), BF),
            shape((GROUP, n, n), BF),
            shape((GROUP, n, cols), F32),
            shape((GROUP, n, cols), F32),
        ],
        compiler_params=pltpu.CompilerParams(vmem_limit_bytes=VMEM_LIMIT),
        name="local_maps",
    )(slots, diag_inv, diag_inv, lower, lower, upper, upper, source, source)


def joined(left, right):
    a_l, b_l, g_l, c_l, h_l = left
    a_r, b_r, g_r, c_r, h_r = right
    a = mm(a_r, a_l).astype(BF)
    b = mm(b_l, b_r).astype(BF)
    cb = c_l.astype(BF)
    c = mm(a_r, cb) + c_r
    g = (mm(b_l, mm(g_r, a_l).astype(BF)) + g_l.astype(F32)).astype(BF)
    h = mm(b_l, (mm(g_r, cb) + h_r).astype(BF)) + h_l
    return a, b, g, c, h


def segment(maps, j, n):
    rows = packed_rows(n)
    one = maps.at[j]
    return (
        unpack(one, 0, n),
        unpack(one, rows, n),
        unpack(one, 2 * rows, n),
        one[3 * rows : 3 * rows + n, :].astype(F32),
        one[3 * rows + n : 3 * rows + 2 * n, :].astype(F32),
    )


def group_map_kernel(group, maps, a_out, b_out, g_out, c_out, h_out, send):
    n = a_out.shape[0]
    a, b, g, c, h = joined(
        joined(segment(maps, 0, n), segment(maps, 1, n)),
        joined(segment(maps, 2, n), segment(maps, 3, n)),
    )
    a_out[...] = a
    b_out[...] = b
    g_out[...] = g
    c_out[...] = c
    h_out[...] = h
    send[0:n, :] = jnp.where(group[0] == 0, c, h).astype(BF)
    pack(send, n, g)


def forward_one_kernel(a, c, incoming, send):
    n = a.shape[0]
    send[...] = (mm(a[...], incoming[0:n, :]) + c[...]).astype(BF)


def turn_kernel(a, b, g, c, h, far, incoming, send, front_out, back_in):
    n = a.shape[0]
    front = incoming[...]
    ahead = (mm(a[...], front) + c[...]).astype(BF)
    back = (mm(unpack(far, n, n), ahead) + far[0:n, :].astype(F32)).astype(BF)
    send[...] = (mm(b[...], back) + mm(g[...], front) + h[...]).astype(BF)
    front_out[...] = ahead
    back_in[...] = back


def backward_one_kernel(group, b, g, h, far, incoming, ahead, send):
    n = b.shape[0]
    back = mm(b[...], incoming[...]) + mm(g[...], far[0:n, :]) + h[...]
    send[...] = jnp.where(group[0] == 1, back.astype(BF), ahead[...])


def interfaces_kernel(group, maps, far, hop2, hop3, back2, hop4, out):
    n = hop2.shape[0]
    rows = packed_rows(n)
    which = group[0]
    zero = jnp.zeros_like(hop2[...])
    front = jnp.where(
        which == 0, zero,
        jnp.where(which == 1, far[0:n, :], jnp.where(which == 2, hop2[...], hop4[...])),
    )
    back = jnp.where(
        which == 0, hop4[...],
        jnp.where(which == 1, hop3[...], jnp.where(which == 2, back2[...], zero)),
    )
    fronts = [front]
    for j in range(GROUP - 1):
        shift = maps[j, 3 * rows : 3 * rows + n, :].astype(F32)
        front = (mm(unpack(maps.at[j], 0, n), front) + shift).astype(BF)
        fronts.append(front)
    for j in reversed(range(GROUP)):
        out[j, 0:n, :] = fronts[j]
        out[j, n : 2 * n, :] = back
        if j:
            shift = maps[j, 3 * rows + n : 3 * rows + 2 * n, :].astype(F32)
            back = (
                mm(unpack(maps.at[j], rows, n), back)
                + (mm(unpack(maps.at[j], 2 * rows, n), fronts[j]) + shift)
            ).astype(BF)


def whole_call(kernel, outs, scalars, *operands, name):
    specs = [pl.BlockSpec(memory_space=pltpu.SMEM)] * len(scalars)
    specs += [pl.BlockSpec(memory_space=pltpu.VMEM)] * len(operands)
    return pl.pallas_call(
        kernel,
        in_specs=specs,
        out_specs=[pl.BlockSpec(memory_space=pltpu.VMEM)] * len(outs),
        out_shape=[jax.ShapeDtypeStruct(s, d) for s, d in outs],
        compiler_params=pltpu.CompilerParams(vmem_limit_bytes=VMEM_LIMIT),
        name=name,
    )(*scalars, *operands)


def finish_kernel(ends, e0, a, h0, h1, y0, c, p0, p1, first, last):
    n = e0.shape[0]
    pencil = pl.program_id(0)
    front = ends[0:n, :]
    back = ends[n : 2 * n, :]
    b1 = (c[...] + mm(a[...], front) - mm(h1[...], back)).astype(BF)
    b0 = (y0[...] - mm(e0[...], front) - mm(h0[...], b1)).astype(BF)
    p0[...] = b0
    p1[...] = b1

    @pl.when(pencil == 0)
    def _():
        first[0] = b0
        first[1] = b1

    @pl.when(pencil == GROUP - 1)
    def _():
        last[0] = b0
        last[1] = b1


def finish(ends, e0, a, h0, h1, y0, c):
    n, cols = y0.shape[1:]

    def per(height, width):
        return pl.BlockSpec((None, height, width), lambda p: (p, 0, 0))

    kept = pl.BlockSpec((2, n, cols), lambda p: (0, 0, 0))
    shape = jax.ShapeDtypeStruct
    return pl.pallas_call(
        finish_kernel,
        grid=(GROUP,),
        in_specs=[
            per(2 * n, cols), per(n, n), per(n, n), per(n, n), per(n, n),
            per(n, cols), per(n, cols),
        ],
        out_specs=[per(n, cols), per(n, cols), kept, kept],
        out_shape=[
            shape((GROUP, n, cols), BF), shape((GROUP, n, cols), BF),
            shape((2, n, cols), BF), shape((2, n, cols), BF),
        ],
        compiler_params=pltpu.CompilerParams(vmem_limit_bytes=VMEM_LIMIT),
        name="finish",
    )(ends, e0, a, h0, h1, y0, c)


def jacobian_kernel(
    slots, place, diag, lower, upper, minus, plus, p0, p1, ends, below, low, high, precond, jac, grid_vals
):
    n = diag.shape[0]
    element = pl.program_id(0)
    slab = element // GROUP
    pencil = element % GROUP

    @pl.when(element == 0)
    def _():
        zero = jnp.zeros((n, p0.shape[2]), BF)
        for p in range(GROUP):
            grid_vals[0, p + 1] = jnp.where(place[0] == 0, zero, below[p])
            grid_vals[1, p + 1] = p0[p]
            grid_vals[2, p + 1] = p1[p]
            grid_vals[3, p + 1] = ends[p, n : 2 * n, :]
        for s in range(2):
            grid_vals[s + 1, 0] = jnp.where(place[1] == 0, zero, low[s])
            grid_vals[s + 1, GROUP + 1] = jnp.where(place[1] == place[2] - 1, zero, high[s])

    own = grid_vals[slab + 1, pencil + 1]
    total = mm(diag[...], own)
    total = total + mm(lower[...], grid_vals[slab, pencil + 1])
    total = total + mm(upper[...], grid_vals[slab + 2, pencil + 1])
    total = total + mm(minus[...], grid_vals[slab + 1, pencil])
    total = total + mm(plus[...], grid_vals[slab + 1, pencil + 2])
    precond[...] = own
    jac[...] = total.astype(BF)


def jacobian(slots, place, blocks, p0, p1, ends, below, low, high):
    n, cols = p0.shape[1:]
    block = pl.BlockSpec((None, n, n), lambda e, sl, pc: (sl[e], 0, 0))
    out = pl.BlockSpec((None, n, cols), lambda e, sl, pc: (sl[e], 0, 0))

    def whole(array):
        return pl.BlockSpec(array.shape, lambda e, sl, pc: (0, 0, 0))

    vectors = (p0, p1, ends, below, low, high)
    shape = jax.ShapeDtypeStruct((2 * GROUP, n, cols), BF)
    return pl.pallas_call(
        jacobian_kernel,
        grid_spec=pltpu.PrefetchScalarGridSpec(
            num_scalar_prefetch=2,
            grid=(2 * GROUP,),
            in_specs=[block] * 5 + [whole(v) for v in vectors],
            out_specs=[out, out],
            scratch_shapes=[pltpu.VMEM((4, GROUP + 2, n, cols), BF)],
        ),
        out_shape=[shape, shape],
        compiler_params=pltpu.CompilerParams(vmem_limit_bytes=VMEM_LIMIT),
        name="jacobian",
    )(slots, place, *blocks, *vectors)


def local(right_side, diag_inv, diag_blk, lower_blk, upper_blk, cross_minus, cross_plus, elem_slot):
    n, cols = right_side.shape[2:]

    def flat(values):
        return values.reshape((-1,) + values.shape[2:])

    slots = elem_slot.reshape(-1)
    count = lax.axis_size("sweep")
    across = lax.axis_size("cross")
    sweep_at = lax.axis_index("sweep")
    group = (sweep_at // GROUP).astype(jnp.int32).reshape(1)
    place = jnp.stack([sweep_at, lax.axis_index("cross"), jnp.int32(across)]).astype(jnp.int32)
    groups = [list(range(g, g + GROUP)) for g in range(0, count, GROUP)]

    def exchange(values):
        return lax.all_to_all(values, "sweep", 0, 0, axis_index_groups=groups)

    def swap(values, order):
        pairs = [(g * GROUP + k, order[g] * GROUP + k) for g in range(GROUP) for k in range(GROUP)]
        return lax.ppermute(values, "sweep", pairs)

    outer, inner = (1, 0, 3, 2), (3, 2, 1, 0)

    maps, e0, a_loc, h0, h1, y0, c_loc = local_maps(
        slots, flat(diag_inv), flat(lower_blk), flat(upper_blk), flat(right_side)
    )
    maps = exchange(maps)
    mat, vec, vec32 = ((n, n), BF), ((n, cols), BF), ((n, cols), F32)
    a, b, g, c, h, send = whole_call(
        group_map_kernel,
        [mat, mat, mat, vec32, vec32, ((n + packed_rows(n), cols), BF)],
        [group], maps, name="group_map",
    )
    far = swap(send, outer)
    (send,) = whole_call(forward_one_kernel, [vec], [], a, c, far, name="forward_one")
    hop2 = swap(send, inner)
    send, ahead, back2 = whole_call(
        turn_kernel, [vec, vec, vec], [], a, b, g, c, h, far, hop2, name="turn"
    )
    hop3 = swap(send, inner)
    (send,) = whole_call(
        backward_one_kernel, [vec], [group], b, g, h, far, hop3, ahead, name="backward_one"
    )
    hop4 = swap(send, outer)
    (ends,) = whole_call(
        interfaces_kernel, [((GROUP, 2 * n, cols), BF)], [group],
        maps, far, hop2, hop3, back2, hop4, name="interfaces",
    )
    ends = exchange(ends)
    p0, p1, first, last = finish(ends, e0, a_loc, h0, h1, y0, c_loc)
    below = lax.ppermute(p1, "sweep", [(i, (i + 1) % count) for i in range(count)])
    low = lax.ppermute(last, "cross", [(i, (i + 1) % across) for i in range(across)])
    high = lax.ppermute(first, "cross", [((i + 1) % across, i) for i in range(across)])
    blocks = [flat(x) for x in (diag_blk, lower_blk, upper_blk, cross_minus, cross_plus)]
    precond, jac = jacobian(slots, place, blocks, p0, p1, ends, below, low, high)
    return precond.reshape(right_side.shape), jac.reshape(right_side.shape)


def solution(mesh):
    blocks = P("sweep", "cross", None, None)
    in_specs = (blocks,) * 7 + (P("sweep", "cross"),)
    return jax.shard_map(
        local, mesh=mesh, in_specs=in_specs, out_specs=(blocks, blocks), check_vma=False
    )
```

```python
import jax
import jax.numpy as jnp
from jax import lax
from jax.experimental import pallas as pl
from jax.experimental.pallas import tpu as pltpu
from jax.sharding import PartitionSpec as P

BF = jnp.bfloat16
F32 = jnp.float32
GROUP = 4
VMEM_LIMIT = 48 << 20


def mm(a, b):
    return jnp.dot(a, b, preferred_element_type=F32)


def mm_fine(a, x):
    width = x.shape[1]
    top = x.astype(BF)
    rest = (x - top.astype(F32)).astype(BF)
    both = mm(a, jnp.concatenate([top, rest], axis=1))
    return both[:, :width] + both[:, width:]


def packed_rows(n):
    return 2 * n + n // 2


def pack(ref, base, mat):
    n = mat.shape[0]
    half = n // 2
    ref[base : base + n, :] = mat[:, 0:128]
    ref[base + n : base + 2 * n, :] = mat[:, 128:256]
    ref[base + 2 * n : base + 2 * n + half, 0:64] = mat[0:half, 256:320]
    ref[base + 2 * n : base + 2 * n + half, 64:128] = mat[half:n, 256:320]


def unpack(ref, base, n):
    half = n // 2
    tail = ref[base + 2 * n : base + 2 * n + half, :]
    last = jnp.concatenate([tail[:, 0:64], tail[:, 64:128]], axis=0)
    return jnp.concatenate(
        [ref[base : base + n, :], ref[base + n : base + 2 * n, :], last], axis=1
    )


def front_maps_kernel(slots, d0, d1, l0, l1, r0, r1, maps, c_out):
    n = d0.shape[0]
    rows = packed_rows(n)
    e0 = mm(d0[...], l0[...]).astype(BF)
    e1 = mm(d1[...], l1[...]).astype(BF)
    y0 = mm(d0[...], r0[...])
    y1 = mm(d1[...], r1[...])
    c = y1 - mm_fine(e1, y0)
    pack(maps, 0, mm(e1, e0).astype(BF))
    maps[rows : rows + n, :] = c.astype(BF)
    c_out[...] = c


def back_maps_kernel(slots, d0, d1, l0, u0, u1, r0, front, c, maps):
    n = d0.shape[0]
    rows = packed_rows(n)
    e0 = mm(d0[...], l0[...])
    h0 = mm(d0[...], u0[...]).astype(BF)
    h1 = mm(d1[...], u1[...]).astype(BF)
    y0 = mm(d0[...], r0[...])
    pack(maps, 0, mm(h0, h1).astype(BF))
    g = -(e0 + mm(h0, unpack(front, 0, n)))
    pack(maps, rows, g.astype(BF))
    maps[2 * rows : 2 * rows + n, :] = (y0 - mm_fine(h0, c[...])).astype(BF)


def stored(slab, height, width):
    return pl.BlockSpec((None, height, width), lambda p, sl: (sl[slab, p], 0, 0))


def in_order(height, width):
    return pl.BlockSpec((None, height, width), lambda p, sl: (p, 0, 0))


def pencil_call(kernel, in_specs, out_specs, out_shape, slots, *operands, name):
    return pl.pallas_call(
        kernel,
        grid_spec=pltpu.PrefetchScalarGridSpec(
            num_scalar_prefetch=1, grid=(GROUP,), in_specs=in_specs, out_specs=out_specs
        ),
        out_shape=out_shape,
        compiler_params=pltpu.CompilerParams(vmem_limit_bytes=VMEM_LIMIT),
        name=name,
    )(slots, *operands)


def front_maps(slots, diag_inv, lower, source):
    n, cols = source.shape[1:]
    rows = packed_rows(n) + n
    shape = jax.ShapeDtypeStruct
    return pencil_call(
        front_maps_kernel,
        [stored(s, n, n) for s in (0, 1, 0, 1)] + [stored(s, n, cols) for s in (0, 1)],
        [in_order(rows, cols), in_order(n, cols)],
        [shape((GROUP, rows, cols), BF), shape((GROUP, n, cols), F32)],
        slots, diag_inv, diag_inv, lower, lower, source, source, name="front_maps",
    )


def back_maps(slots, diag_inv, lower, upper, source, front, c):
    n, cols = source.shape[1:]
    rows = 2 * packed_rows(n) + n
    return pencil_call(
        back_maps_kernel,
        [stored(s, n, n) for s in (0, 1, 0, 0, 1)]
        + [stored(0, n, cols), in_order(front.shape[1], cols), in_order(n, cols)],
        in_order(rows, cols),
        jax.ShapeDtypeStruct((GROUP, rows, cols), BF),
        slots, diag_inv, diag_inv, lower, upper, upper, source, front, c, name="back_maps",
    )


def forward_through(maps, front, n):
    rows = packed_rows(n)
    fronts = []
    for j in range(GROUP):
        fronts.append(front)
        shift = maps[j, rows : rows + n, :].astype(F32)
        front = mm_fine(unpack(maps.at[j], 0, n), front) + shift
    return fronts, front


def backward_through(maps, shifts, back, n):
    backs = [None] * GROUP
    for j in reversed(range(GROUP)):
        backs[j] = back
        back = mm_fine(unpack(maps.at[j], 0, n), back) + shifts[j]
    return backs, back


def forward_first_kernel(maps, send):
    n = send.shape[0]
    rows = packed_rows(n)
    front = maps[0, rows : rows + n, :].astype(F32)
    for j in range(1, GROUP):
        shift = maps[j, rows : rows + n, :].astype(F32)
        front = mm_fine(unpack(maps.at[j], 0, n), front) + shift
    send[...] = front.astype(BF)


def forward_kernel(maps, incoming, send):
    n = send.shape[0]
    _, front = forward_through(maps, incoming[...].astype(F32), n)
    send[...] = front.astype(BF)


def turn_kernel(group, front_maps, back_maps, hop1, hop2, hop3, send, fronts_out, shifts_out):
    n = send.shape[0]
    rows = packed_rows(n)
    which = group[0]
    zero = jnp.zeros_like(hop1[...])
    front = jnp.where(
        which == 0, zero,
        jnp.where(which == 1, hop1[...], jnp.where(which == 2, hop2[...], hop3[...])),
    )
    fronts, _ = forward_through(front_maps, front.astype(F32), n)
    shifts = []
    for j in range(GROUP):
        shift = back_maps[j, 2 * rows : 2 * rows + n, :].astype(F32)
        shifts.append(mm_fine(unpack(back_maps.at[j], rows, n), fronts[j]) + shift)
        shifts_out[j] = shifts[j]
        fronts_out[j] = fronts[j].astype(BF)
    back = shifts[GROUP - 1]
    for j in reversed(range(GROUP - 1)):
        back = mm_fine(unpack(back_maps.at[j], 0, n), back) + shifts[j]
    send[...] = back.astype(BF)


def backward_kernel(maps, shifts, incoming, send):
    n = send.shape[0]
    _, back = backward_through(maps, shifts, incoming[...].astype(F32), n)
    send[...] = back.astype(BF)


def interfaces_kernel(group, maps, shifts, fronts, hop4, hop5, hop6, out):
    n = hop4.shape[0]
    which = group[0]
    zero = jnp.zeros_like(hop4[...])
    back = jnp.where(
        which == 0, hop6[...],
        jnp.where(which == 1, hop5[...], jnp.where(which == 2, hop4[...], zero)),
    )
    backs, _ = backward_through(maps, shifts, back.astype(F32), n)
    for j in range(GROUP):
        out[j, 0:n, :] = fronts[j]
        out[j, n : 2 * n, :] = backs[j].astype(BF)


def whole_call(kernel, outs, scalars, *operands, name):
    specs = [pl.BlockSpec(memory_space=pltpu.SMEM)] * len(scalars)
    specs += [pl.BlockSpec(memory_space=pltpu.VMEM)] * len(operands)
    return pl.pallas_call(
        kernel,
        in_specs=specs,
        out_specs=[pl.BlockSpec(memory_space=pltpu.VMEM)] * len(outs),
        out_shape=[jax.ShapeDtypeStruct(s, d) for s, d in outs],
        compiler_params=pltpu.CompilerParams(vmem_limit_bytes=VMEM_LIMIT),
        name=name,
    )(*scalars, *operands)


def finish_kernel(slots, ends, d0, d1, l0, l1, u0, u1, r0, r1, p0, p1, first, last):
    n = d0.shape[0]
    pencil = pl.program_id(0)
    front = ends[0:n, :]
    back = ends[n : 2 * n, :]
    f0 = mm_fine(d0[...], r0[...].astype(F32) - mm(l0[...], front))
    f1 = mm_fine(d1[...], r1[...].astype(F32) - mm_fine(l1[...], f0))
    x1 = f1 - mm_fine(d1[...], mm(u1[...], back))
    x0 = f0 - mm_fine(d0[...], mm_fine(u0[...], x1))
    b0 = x0.astype(BF)
    b1 = x1.astype(BF)
    p0[...] = b0
    p1[...] = b1

    @pl.when(pencil == 0)
    def _():
        first[0] = b0
        first[1] = b1

    @pl.when(pencil == GROUP - 1)
    def _():
        last[0] = b0
        last[1] = b1


def finish(slots, ends, diag_inv, lower, upper, source):
    n, cols = source.shape[1:]
    kept = pl.BlockSpec((2, n, cols), lambda p, sl: (0, 0, 0))
    shape = jax.ShapeDtypeStruct
    return pencil_call(
        finish_kernel,
        [in_order(2 * n, cols)]
        + [stored(s, n, n) for s in (0, 1, 0, 1, 0, 1)]
        + [stored(s, n, cols) for s in (0, 1)],
        [in_order(n, cols), in_order(n, cols), kept, kept],
        [
            shape((GROUP, n, cols), BF), shape((GROUP, n, cols), BF),
            shape((2, n, cols), BF), shape((2, n, cols), BF),
        ],
        slots, ends, diag_inv, diag_inv, lower, lower, upper, upper, source, source,
        name="finish",
    )


def inner_jacobian_kernel(
    slots, diag, lower, upper, minus, plus, p0, p1, ends, precond, partial, vals
):
    n = diag.shape[0]
    element = pl.program_id(0)
    slab = element // GROUP
    pencil = element % GROUP

    @pl.when(element == 0)
    def _():
        zero = jnp.zeros((n, p0.shape[2]), BF)
        for p in range(GROUP):
            vals[0, p + 1] = zero
            vals[1, p + 1] = p0[p]
            vals[2, p + 1] = p1[p]
            vals[3, p + 1] = ends[p, n : 2 * n, :]
        for s in range(2):
            vals[s + 1, 0] = zero
            vals[s + 1, GROUP + 1] = zero

    own = vals[slab + 1, pencil + 1]
    total = mm(diag[...], own)
    total = total + mm(lower[...], vals[slab, pencil + 1])
    total = total + mm(upper[...], vals[slab + 2, pencil + 1])
    total = total + mm(minus[...], vals[slab + 1, pencil])
    total = total + mm(plus[...], vals[slab + 1, pencil + 2])
    precond[...] = own
    partial[...] = total


def inner_jacobian(slots, blocks, p0, p1, ends):
    n, cols = p0.shape[1:]
    block = pl.BlockSpec((None, n, n), lambda e, sl: (sl[e // GROUP, e % GROUP], 0, 0))
    out = pl.BlockSpec((None, n, cols), lambda e, sl: (sl[e // GROUP, e % GROUP], 0, 0))
    seq = pl.BlockSpec((None, n, cols), lambda e, sl: (e, 0, 0))

    def whole(array):
        return pl.BlockSpec(array.shape, lambda e, sl: (0, 0, 0))

    vectors = (p0, p1, ends)
    shape = (2 * GROUP, n, cols)
    return pl.pallas_call(
        inner_jacobian_kernel,
        grid_spec=pltpu.PrefetchScalarGridSpec(
            num_scalar_prefetch=1,
            grid=(2 * GROUP,),
            in_specs=[block] * 5 + [whole(v) for v in vectors],
            out_specs=[out, seq],
            scratch_shapes=[pltpu.VMEM((4, GROUP + 2, n, cols), BF)],
        ),
        out_shape=[jax.ShapeDtypeStruct(shape, BF), jax.ShapeDtypeStruct(shape, F32)],
        compiler_params=pltpu.CompilerParams(vmem_limit_bytes=VMEM_LIMIT),
        name="inner_jacobian",
    )(slots, *blocks, *vectors)


def edge_jacobian_kernel(slots, place, *refs):
    lowers, minuses, pluses = refs[0:4], refs[4:6], refs[6:8]
    partial, below, low, high, jac = refs[8:]
    left = jnp.where(place[1] == 0, 0.0, 1.0).astype(F32)
    right = jnp.where(place[1] == place[2] - 1, 0.0, 1.0).astype(F32)
    start = jnp.where(place[0] == 0, 0.0, 1.0).astype(F32)
    for s in range(2):
        for p in range(GROUP):
            total = partial[s * GROUP + p]
            if s == 0:
                total = total + start * mm(lowers[p][...], below[p])
            if p == 0:
                total = total + left * mm(minuses[s][...], low[s])
            if p == GROUP - 1:
                total = total + right * mm(pluses[s][...], high[s])
            jac[slots[s, p]] = total.astype(BF)


def edge_jacobian(slots, place, lower, minus, plus, partial, below, low, high):
    n, cols = below.shape[1:]

    def block(s, p):
        return pl.BlockSpec((None, n, n), lambda i, sl, pc: (sl[s, p], 0, 0))

    def whole(shape):
        return pl.BlockSpec(shape, lambda i, sl, pc: (0, 0, 0))

    vectors = (partial, below, low, high)
    return pl.pallas_call(
        edge_jacobian_kernel,
        grid_spec=pltpu.PrefetchScalarGridSpec(
            num_scalar_prefetch=2,
            grid=(1,),
            in_specs=[block(0, p) for p in range(GROUP)]
            + [block(s, 0) for s in range(2)]
            + [block(s, GROUP - 1) for s in range(2)]
            + [whole(v.shape) for v in vectors],
            out_specs=whole((2 * GROUP, n, cols)),
        ),
        out_shape=jax.ShapeDtypeStruct((2 * GROUP, n, cols), BF),
        compiler_params=pltpu.CompilerParams(vmem_limit_bytes=VMEM_LIMIT),
        name="edge_jacobian",
    )(slots, place, *([lower] * GROUP), minus, minus, plus, plus, *vectors)


def local(right_side, diag_inv, diag_blk, lower_blk, upper_blk, cross_minus, cross_plus, elem_slot):
    n, cols = right_side.shape[2:]
    source, inverse, diagonal, lower, upper, minus, plus = (
        values.reshape((-1,) + values.shape[2:])
        for values in (
            right_side, diag_inv, diag_blk, lower_blk, upper_blk, cross_minus, cross_plus
        )
    )
    count = lax.axis_size("sweep")
    across = lax.axis_size("cross")
    sweep_at = lax.axis_index("sweep")
    group = (sweep_at // GROUP).astype(jnp.int32).reshape(1)
    place = jnp.stack([sweep_at, lax.axis_index("cross"), jnp.int32(across)]).astype(jnp.int32)
    groups = [list(range(g, g + GROUP)) for g in range(0, count, GROUP)]

    def exchange(values):
        return lax.all_to_all(values, "sweep", 0, 0, axis_index_groups=groups)

    def swap(values, order):
        pairs = [(g * GROUP + k, order[g] * GROUP + k) for g in range(GROUP) for k in range(GROUP)]
        return lax.ppermute(values, "sweep", pairs)

    outer, inner = (1, 0, 3, 2), (3, 2, 1, 0)
    vec = ((n, cols), BF)
    vecs, vecs32 = ((GROUP, n, cols), BF), ((GROUP, n, cols), F32)

    front, c = front_maps(elem_slot, inverse, lower, source)
    fronts = exchange(front)
    back = back_maps(elem_slot, inverse, lower, upper, source, front, c)
    backs = exchange(back)
    (send,) = whole_call(forward_first_kernel, [vec], [], fronts, name="forward_first")
    hop1 = swap(send, outer)
    (send,) = whole_call(forward_kernel, [vec], [], fronts, hop1, name="forward_second")
    hop2 = swap(send, inner)
    (send,) = whole_call(forward_kernel, [vec], [], fronts, hop2, name="forward_third")
    hop3 = swap(send, outer)
    send, entering, shifts = whole_call(
        turn_kernel, [vec, vecs, vecs32], [group], fronts, backs, hop1, hop2, hop3, name="turn"
    )
    hop4 = swap(send, outer)
    (send,) = whole_call(backward_kernel, [vec], [], backs, shifts, hop4, name="backward_third")
    hop5 = swap(send, inner)
    (send,) = whole_call(backward_kernel, [vec], [], backs, shifts, hop5, name="backward_second")
    hop6 = swap(send, outer)
    (ends,) = whole_call(
        interfaces_kernel, [((GROUP, 2 * n, cols), BF)], [group],
        backs, shifts, entering, hop4, hop5, hop6, name="interfaces",
    )
    ends = exchange(ends)
    p0, p1, first, last = finish(elem_slot, ends, inverse, lower, upper, source)
    low = lax.ppermute(last, "cross", [(i, (i + 1) % across) for i in range(across)])
    high = lax.ppermute(first, "cross", [((i + 1) % across, i) for i in range(across)])
    below = lax.ppermute(p1, "sweep", [(i, (i + 1) % count) for i in range(count)])
    precond, partial = inner_jacobian(elem_slot, (diagonal, lower, upper, minus, plus), p0, p1, ends)
    jac = edge_jacobian(elem_slot, place, lower, minus, plus, partial, below, low, high)
    return precond.reshape(right_side.shape), jac.reshape(right_side.shape)


def solution(mesh):
    blocks = P("sweep", "cross", None, None)
    in_specs = (blocks,) * 7 + (P("sweep", "cross"),)
    return jax.shard_map(
        local, mesh=mesh, in_specs=in_specs, out_specs=(blocks, blocks), check_vma=False
    )
```

```python
import jax
import jax.numpy as jnp
from jax import lax
from jax.experimental import pallas as pl
from jax.experimental.pallas import tpu as pltpu
from jax.sharding import PartitionSpec as P

BF = jnp.bfloat16
F32 = jnp.float32
GROUP = 4
VMEM_LIMIT = 48 << 20


def mm(a, b):
    return jnp.dot(a, b, preferred_element_type=F32)


def mm_fine(a, x):
    width = x.shape[1]
    top = x.astype(BF)
    rest = (x - top.astype(F32)).astype(BF)
    both = mm(a, jnp.concatenate([top, rest], axis=1))
    return both[:, :width] + both[:, width:]


def packed_rows(n):
    return 2 * n + n // 2


def pack(ref, base, mat):
    n = mat.shape[0]
    half = n // 2
    ref[base : base + n, :] = mat[:, 0:128]
    ref[base + n : base + 2 * n, :] = mat[:, 128:256]
    ref[base + 2 * n : base + 2 * n + half, 0:64] = mat[0:half, 256:320]
    ref[base + 2 * n : base + 2 * n + half, 64:128] = mat[half:n, 256:320]


def unpack(ref, base, n):
    half = n // 2
    tail = ref[base + 2 * n : base + 2 * n + half, :]
    last = jnp.concatenate([tail[:, 0:64], tail[:, 64:128]], axis=0)
    return jnp.concatenate(
        [ref[base : base + n, :], ref[base + n : base + 2 * n, :], last], axis=1
    )


def map_rows(n):
    return 3 * packed_rows(n) + 2 * n


def local_map_kernel(slots, place, d0, d1, l0, l1, u0, u1, r0, r1, out):
    n = d0.shape[0]
    rows = packed_rows(n)
    inv0, inv1 = d0[...], d1[...]
    e0 = mm(inv0, l0[...])
    e1 = mm(inv1, l1[...]).astype(BF)
    h0 = mm(inv0, u0[...]).astype(BF)
    h1 = mm(inv1, u1[...]).astype(BF)
    y0 = mm(inv0, r0[...])
    y1 = mm(inv1, r1[...])
    a = mm(e1, e0.astype(BF)).astype(BF)
    c = y1 - mm_fine(e1, y0)
    b = mm(h0, h1).astype(BF)
    g = -(e0 + mm(h0, a))
    h = y0 - mm_fine(h0, c)
    pack(out, 0, a)
    pack(out, rows, b)
    pack(out, 2 * rows, g.astype(BF))
    out[3 * rows : 3 * rows + n, :] = c.astype(BF)
    out[3 * rows + n : 3 * rows + 2 * n, :] = h.astype(BF)


def stored(slab, pencil, height, width):
    return pl.BlockSpec(
        (None, height, width), lambda i, sl, at: (sl[slab, pencil(at)], 0, 0)
    )


def constant(shape):
    return pl.BlockSpec(shape, lambda i, sl, at: (0,) * len(shape))


def element_call(kernel, in_specs, out_shape, slots, place, *operands, name):
    return pl.pallas_call(
        kernel,
        grid_spec=pltpu.PrefetchScalarGridSpec(
            num_scalar_prefetch=2,
            grid=(1,),
            in_specs=in_specs,
            out_specs=[constant(o.shape) for o in out_shape],
        ),
        out_shape=out_shape,
        compiler_params=pltpu.CompilerParams(vmem_limit_bytes=VMEM_LIMIT),
        name=name,
    )(slots, place, *operands)


def local_map(slots, place, diag_inv, lower, upper, source, distance):
    n, cols = source.shape[1:]

    def pencil(at):
        return lax.bitwise_xor(at[3], jnp.int32(distance))

    (out,) = element_call(
        local_map_kernel,
        [stored(s, pencil, n, n) for s in (0, 1, 0, 1, 0, 1)]
        + [stored(s, pencil, n, cols) for s in (0, 1)],
        [jax.ShapeDtypeStruct((map_rows(n), cols), BF)],
        slots, place, diag_inv, diag_inv, lower, lower, upper, upper, source, source,
        name="local_map",
    )
    return out


def gather_maps(place, pieces, maps, sems):
    copies = []
    for distance, piece in enumerate(pieces):
        owner = lax.bitwise_xor(place[3], jnp.int32(distance))
        copy = pltpu.make_async_copy(piece, maps.at[owner], sems.at[distance])
        copy.start()
        copies.append(copy)
    for copy in copies:
        copy.wait()


def group_front_kernel(place, own, near, next_one, across, send, maps, sems):
    n = send.shape[0]
    rows = packed_rows(n)
    copies = []
    for distance, piece in enumerate((own, near, next_one, across)):
        owner = lax.bitwise_xor(place[3], jnp.int32(distance))
        for part, (start, size, to) in enumerate(((0, rows, 0), (3 * rows, n, rows))):
            copies.append(
                pltpu.make_async_copy(
                    piece.at[pl.ds(start, size)],
                    maps.at[owner, pl.ds(to, size)],
                    sems.at[distance, part],
                )
            )
            copies[-1].start()
    for copy in copies:
        copy.wait()
    front = maps[0, rows : rows + n, :].astype(F32)
    for j in range(1, GROUP):
        shift = maps[j, rows : rows + n, :].astype(F32)
        front = mm_fine(unpack(maps.at[j], 0, n), front) + shift
    send[...] = front.astype(BF)


def group_front(place, pieces, n, cols):
    return pl.pallas_call(
        group_front_kernel,
        in_specs=[pl.BlockSpec(memory_space=pltpu.SMEM)]
        + [pl.BlockSpec(memory_space=pl.ANY)] * GROUP,
        out_specs=pl.BlockSpec(memory_space=pltpu.VMEM),
        out_shape=jax.ShapeDtypeStruct((n, cols), BF),
        scratch_shapes=[
            pltpu.VMEM((GROUP, packed_rows(n) + n, cols), BF),
            pltpu.SemaphoreType.DMA((GROUP, 2)),
        ],
        compiler_params=pltpu.CompilerParams(vmem_limit_bytes=VMEM_LIMIT),
        name="group_front",
    )(place, *pieces)


def joined(left, right):
    a_l, b_l, g_l, c_l, h_l = left
    a_r, b_r, g_r, c_r, h_r = right
    a = mm(a_r, a_l).astype(BF)
    b = mm(b_l, b_r).astype(BF)
    g = (mm(b_l, mm(g_r, a_l).astype(BF)) + g_l.astype(F32)).astype(BF)
    c = mm_fine(a_r, c_l) + c_r
    h = mm_fine(b_l, mm_fine(g_r, c_l) + h_r) + h_l
    return a, b, g, c, h


def segment(maps, j, n):
    rows = packed_rows(n)
    one = maps.at[j]
    return (
        unpack(one, 0, n),
        unpack(one, rows, n),
        unpack(one, 2 * rows, n),
        one[3 * rows : 3 * rows + n, :].astype(F32),
        one[3 * rows + n : 3 * rows + 2 * n, :].astype(F32),
    )


def group_map_kernel(
    place, after, own, near, next_one, across, a_out, b_out, g_out, c_out, h_out, send_far, maps, sems
):
    n = a_out.shape[0]
    gather_maps(place, (own, near, next_one, across), maps, sems)
    a, b, g, c, h = joined(
        joined(segment(maps, 0, n), segment(maps, 1, n)),
        joined(segment(maps, 2, n), segment(maps, 3, n)),
    )
    a_out[...] = a
    b_out[...] = b
    g_out[...] = g
    c_out[...] = c
    h_out[...] = h
    send_far[0:n, :] = h.astype(BF)
    pack(send_far, n, g)


def group_map(place, after, pieces, n, cols):
    shapes = [
        ((n, n), BF), ((n, n), BF), ((n, n), BF), ((n, cols), F32), ((n, cols), F32),
        ((n + packed_rows(n), cols), BF),
    ]
    return pl.pallas_call(
        group_map_kernel,
        in_specs=[pl.BlockSpec(memory_space=pltpu.SMEM)]
        + [pl.BlockSpec(memory_space=pl.ANY)] * (GROUP + 1),
        out_specs=[pl.BlockSpec(memory_space=pltpu.VMEM)] * len(shapes),
        out_shape=[jax.ShapeDtypeStruct(s, d) for s, d in shapes],
        scratch_shapes=[
            pltpu.VMEM((GROUP, map_rows(n), cols), BF), pltpu.SemaphoreType.DMA((GROUP,))
        ],
        compiler_params=pltpu.CompilerParams(vmem_limit_bytes=VMEM_LIMIT),
        name="group_map",
    )(place, after, *pieces)


def forward_one_kernel(a, c, incoming, send):
    send[...] = (mm(a[...], incoming[...]) + c[...]).astype(BF)


def turn_kernel(a, b, g, c, h, far, incoming, send, front_out, back_in):
    n = a.shape[0]
    front = incoming[...]
    ahead = mm(a[...], front) + c[...]
    back = mm_fine(unpack(far, n, n), ahead) + far[0:n, :].astype(F32)
    send[...] = (mm_fine(b[...], back) + (mm(g[...], front) + h[...])).astype(BF)
    front_out[...] = ahead.astype(BF)
    back_in[...] = back.astype(BF)


def backward_one_kernel(place, b, g, h, hop1, incoming, ahead, send):
    back = mm(b[...], incoming[...]) + (mm(g[...], hop1[...]) + h[...])
    send[...] = jnp.where(place[4] == 1, back.astype(BF), ahead[...])


def interfaces_kernel(
    place, own, near, next_one, across, hop1, hop2, hop3, back2, hop4, out, maps, sems
):
    n = hop2.shape[0]
    rows = packed_rows(n)
    which = place[4]
    gather_maps(place, (own, near, next_one, across), maps, sems)
    zero = jnp.zeros_like(hop2[...])
    front = jnp.where(
        which == 0, zero,
        jnp.where(which == 1, hop1[...], jnp.where(which == 2, hop2[...], hop4[...])),
    ).astype(F32)
    back = jnp.where(
        which == 0, hop4[...],
        jnp.where(which == 1, hop3[...], jnp.where(which == 2, back2[...], zero)),
    ).astype(F32)
    fronts = [front]
    for j in range(GROUP - 1):
        shift = maps[j, 3 * rows : 3 * rows + n, :].astype(F32)
        front = mm_fine(unpack(maps.at[j], 0, n), front) + shift
        fronts.append(front)
    for j in reversed(range(GROUP)):
        out[j, 0:n, :] = fronts[j].astype(BF)
        out[j, n : 2 * n, :] = back.astype(BF)
        if j:
            shift = maps[j, 3 * rows + n : 3 * rows + 2 * n, :].astype(F32)
            inner = mm_fine(unpack(maps.at[j], 2 * rows, n), fronts[j]) + shift
            back = mm_fine(unpack(maps.at[j], rows, n), back) + inner


def interfaces(place, pieces, n, cols, *hops):
    return pl.pallas_call(
        interfaces_kernel,
        in_specs=[pl.BlockSpec(memory_space=pltpu.SMEM)]
        + [pl.BlockSpec(memory_space=pl.ANY)] * GROUP
        + [pl.BlockSpec(memory_space=pltpu.VMEM)] * len(hops),
        out_specs=pl.BlockSpec(memory_space=pltpu.VMEM),
        out_shape=jax.ShapeDtypeStruct((GROUP, 2 * n, cols), BF),
        scratch_shapes=[
            pltpu.VMEM((GROUP, map_rows(n), cols), BF), pltpu.SemaphoreType.DMA((GROUP,))
        ],
        compiler_params=pltpu.CompilerParams(vmem_limit_bytes=VMEM_LIMIT),
        name="interfaces",
    )(place, *pieces, *hops)


def whole_call(kernel, outs, scalars, *operands, name):
    specs = [pl.BlockSpec(memory_space=pltpu.SMEM)] * len(scalars)
    specs += [pl.BlockSpec(memory_space=pltpu.VMEM)] * len(operands)
    return pl.pallas_call(
        kernel,
        in_specs=specs,
        out_specs=[pl.BlockSpec(memory_space=pltpu.VMEM)] * len(outs),
        out_shape=[jax.ShapeDtypeStruct(s, d) for s, d in outs],
        compiler_params=pltpu.CompilerParams(vmem_limit_bytes=VMEM_LIMIT),
        name=name,
    )(*scalars, *operands)


def solve_pencils(ends, columns):
    n = ends[0].shape[0] // 2
    fronts = [e[0:n, :] for e in ends]
    backs = [e[n : 2 * n, :] for e in ends]
    both = range(len(ends))
    d0, d1, l0, l1, u0, u1, r0, r1 = zip(*columns)
    v = [mm(u1[i][...], backs[i]) for i in both]
    q = [r0[i][...].astype(F32) - mm(l0[i][...], fronts[i]) for i in both]
    f0 = [mm_fine(d0[i][...], q[i]) for i in both]
    v = [mm_fine(d1[i][...], v[i]) for i in both]
    q = [r1[i][...].astype(F32) - mm_fine(l1[i][...], f0[i]) for i in both]
    x1 = [mm_fine(d1[i][...], q[i]) - v[i] for i in both]
    q = [mm_fine(u0[i][...], x1[i]) for i in both]
    x0 = [f0[i] - mm_fine(d0[i][...], q[i]) for i in both]
    return [(x0[i].astype(BF), x1[i].astype(BF)) for i in both]


def outer_pencils_kernel(slots, place, ends, *refs):
    first, last = refs[16:]
    solved = solve_pencils([ends[0], ends[GROUP - 1]], [refs[0:8], refs[8:16]])
    for (x0, x1), out in zip(solved, (first, last)):
        out[0] = x0
        out[1] = x1


def inner_pencils_kernel(slots, place, ends, *refs):
    first, last, second, third, tops = refs[16:]
    solved = solve_pencils([ends[1], ends[2]], [refs[0:8], refs[8:16]])
    for (x0, x1), out, pencil in zip(solved, (second, third), (1, 2)):
        out[0] = x0
        out[1] = x1
        tops[pencil] = x1
    tops[0] = first[1]
    tops[GROUP - 1] = last[1]


def pencils(kernel, chosen, outs, slots, place, ends, diag_inv, lower, upper, source, *more, name):
    n, cols = source.shape[1:]
    specs, operands = [constant(ends.shape)], [ends]
    for p in chosen:
        for array in (diag_inv, lower, upper, source):
            for s in range(2):
                specs.append(stored(s, lambda at, p=p: p, n, array.shape[-1]))
                operands.append(array)
    specs += [constant(m.shape) for m in more]
    return element_call(
        kernel, specs, [jax.ShapeDtypeStruct(o, BF) for o in outs],
        slots, place, *operands, *more, name=name,
    )


def inner_jacobian_kernel(slots, *refs):
    blocks, (first, second, third, last, ends) = refs[0:10], refs[10:15]
    precond, partial, vals = refs[15:]
    n = first.shape[1]
    pencil = pl.program_id(0)

    @pl.when(pencil == 0)
    def _():
        zero = jnp.zeros(first.shape[1:], BF)
        for p, values in enumerate((first, second, third, last)):
            vals[0, p + 1] = zero
            vals[1, p + 1] = values[0]
            vals[2, p + 1] = values[1]
            vals[3, p + 1] = ends[p, n : 2 * n, :]
        for s in range(2):
            vals[s + 1, 0] = zero
            vals[s + 1, GROUP + 1] = zero

    both = range(2)
    near = [
        [
            vals[s + 1, pencil + 1], vals[s, pencil + 1], vals[s + 2, pencil + 1],
            vals[s + 1, pencil], vals[s + 1, pencil + 2],
        ]
        for s in both
    ]
    totals = [mm(blocks[5 * s][...], near[s][0]) for s in both]
    for t in range(1, 5):
        totals = [totals[s] + mm(blocks[5 * s + t][...], near[s][t]) for s in both]
    for s in both:
        precond[slots[s, pencil]] = near[s][0]
        partial[s] = totals[s]


def inner_jacobian(slots, blocks, vectors):
    n, cols = vectors[0].shape[1:]

    def whole(shape):
        return pl.BlockSpec(shape, lambda p, sl: (0, 0, 0))

    specs = [
        pl.BlockSpec((None, n, n), lambda p, sl, s=s: (sl[s, p], 0, 0))
        for s in range(2)
        for _ in blocks
    ]
    stored_shape = (2 * GROUP, n, cols)
    return pl.pallas_call(
        inner_jacobian_kernel,
        grid_spec=pltpu.PrefetchScalarGridSpec(
            num_scalar_prefetch=1,
            grid=(GROUP,),
            in_specs=specs + [whole(v.shape) for v in vectors],
            out_specs=[
                whole(stored_shape),
                pl.BlockSpec((None, 2, n, cols), lambda p, sl: (p, 0, 0, 0)),
            ],
            scratch_shapes=[pltpu.VMEM((4, GROUP + 2, n, cols), BF)],
        ),
        out_shape=[
            jax.ShapeDtypeStruct(stored_shape, BF),
            jax.ShapeDtypeStruct((GROUP, 2, n, cols), F32),
        ],
        compiler_params=pltpu.CompilerParams(vmem_limit_bytes=VMEM_LIMIT),
        name="inner_jacobian",
    )(slots, *blocks, *blocks, *vectors)


def edge_jacobian_kernel(slots, place, *refs):
    lowers, minuses, pluses = refs[0:4], refs[4:6], refs[6:8]
    partial, below, low, high, jac = refs[8:]
    left = jnp.where(place[1] == 0, 0.0, 1.0).astype(F32)
    right = jnp.where(place[1] == place[2] - 1, 0.0, 1.0).astype(F32)
    start = jnp.where(place[0] == 0, 0.0, 1.0).astype(F32)
    for s in range(2):
        for p in range(GROUP):
            total = partial[p, s]
            if s == 0:
                total = total + start * mm(lowers[p][...], below[p])
            if p == 0:
                total = total + left * mm(minuses[s][...], low[s])
            if p == GROUP - 1:
                total = total + right * mm(pluses[s][...], high[s])
            jac[slots[s, p]] = total.astype(BF)


def edge_jacobian(slots, place, lower, minus, plus, partial, below, low, high):
    n, cols = below.shape[1:]

    def block(s, p):
        return pl.BlockSpec((None, n, n), lambda i, sl, pc: (sl[s, p], 0, 0))

    def whole(shape):
        return pl.BlockSpec(shape, lambda i, sl, pc: (0,) * len(shape))

    vectors = (partial, below, low, high)
    return pl.pallas_call(
        edge_jacobian_kernel,
        grid_spec=pltpu.PrefetchScalarGridSpec(
            num_scalar_prefetch=2,
            grid=(1,),
            in_specs=[block(0, p) for p in range(GROUP)]
            + [block(s, 0) for s in range(2)]
            + [block(s, GROUP - 1) for s in range(2)]
            + [whole(v.shape) for v in vectors],
            out_specs=whole((2 * GROUP, n, cols)),
        ),
        out_shape=jax.ShapeDtypeStruct((2 * GROUP, n, cols), BF),
        compiler_params=pltpu.CompilerParams(vmem_limit_bytes=VMEM_LIMIT),
        name="edge_jacobian",
    )(slots, place, *([lower] * GROUP), minus, minus, plus, plus, *vectors)


def local(right_side, diag_inv, diag_blk, lower_blk, upper_blk, cross_minus, cross_plus, elem_slot):
    n, cols = right_side.shape[2:]
    source, inverse, diagonal, lower, upper, minus, plus = (
        pltpu.with_memory_space_constraint(
            values.reshape((-1,) + values.shape[2:]), pltpu.HBM
        )
        for values in (
            right_side, diag_inv, diag_blk, lower_blk, upper_blk, cross_minus, cross_plus
        )
    )
    count = lax.axis_size("sweep")
    across = lax.axis_size("cross")
    sweep_at = lax.axis_index("sweep")
    place = jnp.stack(
        [
            sweep_at, lax.axis_index("cross"), jnp.int32(across),
            lax.rem(sweep_at, GROUP), lax.div(sweep_at, GROUP),
        ]
    ).astype(jnp.int32)
    groups = [list(range(g, g + GROUP)) for g in range(0, count, GROUP)]

    def swap(values, order):
        pairs = [(g * GROUP + k, order[g] * GROUP + k) for g in range(GROUP) for k in range(GROUP)]
        return lax.ppermute(values, "sweep", pairs)

    def to_peer(values, distance):
        return lax.ppermute(values, "sweep", [(i, i ^ distance) for i in range(count)])

    outer, inner = (1, 0, 3, 2), (3, 2, 1, 0)
    maps = [None] * GROUP
    for distance in (3, 1, 2, 0):
        piece = local_map(elem_slot, place, inverse, lower, upper, source, distance)
        maps[distance] = to_peer(piece, distance) if distance else piece

    send = group_front(place, maps, n, cols)
    hop1 = swap(send, outer)
    a, b, g, c, h, send_far = group_map(place, send, maps, n, cols)
    far = swap(send_far, outer)
    vec = ((n, cols), BF)
    (send,) = whole_call(forward_one_kernel, [vec], [], a, c, hop1, name="forward_one")
    hop2 = swap(send, inner)
    send, ahead, back2 = whole_call(
        turn_kernel, [vec, vec, vec], [], a, b, g, c, h, far, hop2, name="turn"
    )
    hop3 = swap(send, inner)
    (send,) = whole_call(
        backward_one_kernel, [vec], [place], b, g, h, hop1, hop3, ahead, name="backward_one"
    )
    hop4 = swap(send, outer)
    ends = interfaces(place, maps, n, cols, hop1, hop2, hop3, back2, hop4)
    ends = lax.all_to_all(ends, "sweep", 0, 0, axis_index_groups=groups)

    pair, four = (2, n, cols), (GROUP, n, cols)
    first, last = pencils(
        outer_pencils_kernel, (0, GROUP - 1), [pair, pair],
        elem_slot, place, ends, inverse, lower, upper, source, name="outer_pencils",
    )
    low = lax.ppermute(last, "cross", [(i, (i + 1) % across) for i in range(across)])
    high = lax.ppermute(first, "cross", [((i + 1) % across, i) for i in range(across)])
    second, third, tops = pencils(
        inner_pencils_kernel, (1, 2), [pair, pair, four],
        elem_slot, place, ends, inverse, lower, upper, source, first, last, name="inner_pencils",
    )
    below = lax.ppermute(tops, "sweep", [(i, (i + 1) % count) for i in range(count)])
    precond, partial = inner_jacobian(
        elem_slot, (diagonal, lower, upper, minus, plus), (first, second, third, last, ends)
    )
    jac = edge_jacobian(elem_slot, place, lower, minus, plus, partial, below, low, high)
    return precond.reshape(right_side.shape), jac.reshape(right_side.shape)


def solution(mesh):
    blocks = P("sweep", "cross", None, None)
    in_specs = (blocks,) * 7 + (P("sweep", "cross"),)
    return jax.shard_map(
        local, mesh=mesh, in_specs=in_specs, out_specs=(blocks, blocks), check_vma=False
    )
```

```python
import functools

import jax
import jax.numpy as jnp
from jax import lax
from jax.experimental import pallas as pl
from jax.experimental.pallas import tpu as pltpu
from jax.sharding import PartitionSpec as P

BF = jnp.bfloat16
F32 = jnp.float32
GROUP = 4
VMEM_LIMIT = 48 << 20
LONG = pl.CostEstimate(flops=10**10, transcendentals=0, bytes_accessed=1024)
SHORT = pl.CostEstimate(flops=1024, transcendentals=0, bytes_accessed=1024)


def mm(a, b):
    return jnp.dot(a, b, preferred_element_type=F32)


def mm_fine(a, x):
    width = x.shape[1]
    top = x.astype(BF)
    rest = (x - top.astype(F32)).astype(BF)
    both = mm(a, jnp.concatenate([top, rest], axis=1))
    return both[:, :width] + both[:, width:]


def packed_rows(n):
    return 2 * n + n // 2


def pack(ref, base, mat):
    n = mat.shape[0]
    half = n // 2
    ref[base : base + n, :] = mat[:, 0:128]
    ref[base + n : base + 2 * n, :] = mat[:, 128:256]
    ref[base + 2 * n : base + 2 * n + half, 0:64] = mat[0:half, 256:320]
    ref[base + 2 * n : base + 2 * n + half, 64:128] = mat[half:n, 256:320]


def unpack(ref, base, n):
    half = n // 2
    tail = ref[base + 2 * n : base + 2 * n + half, :]
    last = jnp.concatenate([tail[:, 0:64], tail[:, 64:128]], axis=0)
    return jnp.concatenate(
        [ref[base : base + n, :], ref[base + n : base + 2 * n, :], last], axis=1
    )


def map_rows(n):
    return 3 * packed_rows(n) + 2 * n


def local_map_kernel(slots, place, d0, d1, l0, l1, u0, u1, r0, r1, out):
    n = d0.shape[0]
    rows = packed_rows(n)
    inv0, inv1 = d0[...], d1[...]
    e0 = mm(inv0, l0[...])
    e1 = mm(inv1, l1[...]).astype(BF)
    h0 = mm(inv0, u0[...]).astype(BF)
    h1 = mm(inv1, u1[...]).astype(BF)
    y0 = mm(inv0, r0[...])
    y1 = mm(inv1, r1[...])
    a = mm(e1, e0.astype(BF)).astype(BF)
    c = y1 - mm_fine(e1, y0)
    b = mm(h0, h1).astype(BF)
    g = -(e0 + mm(h0, a))
    h = y0 - mm_fine(h0, c)
    pack(out, 0, a)
    pack(out, rows, b)
    pack(out, 2 * rows, g.astype(BF))
    out[3 * rows : 3 * rows + n, :] = c.astype(BF)
    out[3 * rows + n : 3 * rows + 2 * n, :] = h.astype(BF)


def stored(slab, pencil, height, width):
    return pl.BlockSpec(
        (None, height, width), lambda i, sl, at: (sl[slab, pencil(at)], 0, 0)
    )


def constant(shape):
    return pl.BlockSpec(shape, lambda i, sl, at: (0,) * len(shape))


def element_call(kernel, in_specs, out_shape, slots, place, *operands, name, cost=SHORT):
    return pl.pallas_call(
        kernel,
        grid_spec=pltpu.PrefetchScalarGridSpec(
            num_scalar_prefetch=2,
            grid=(1,),
            in_specs=in_specs,
            out_specs=[constant(o.shape) for o in out_shape],
        ),
        out_shape=out_shape,
        compiler_params=pltpu.CompilerParams(vmem_limit_bytes=VMEM_LIMIT),
        cost_estimate=cost,
        name=name,
    )(slots, place, *operands)


def local_map(slots, place, diag_inv, lower, upper, source, distance):
    n, cols = source.shape[1:]

    def pencil(at):
        return lax.bitwise_xor(at[3], jnp.int32(distance))

    (out,) = element_call(
        local_map_kernel,
        [stored(s, pencil, n, n) for s in (0, 1, 0, 1, 0, 1)]
        + [stored(s, pencil, n, cols) for s in (0, 1)],
        [jax.ShapeDtypeStruct((map_rows(n), cols), BF)],
        slots, place, diag_inv, diag_inv, lower, lower, upper, upper, source, source,
        name="local_map",
    )
    return out


def per_owner(place, pieces, body):
    for owned in range(GROUP):

        @pl.when(place[3] == owned)
        def _(owned=owned):
            body([pieces[owned ^ j] for j in range(GROUP)])


def group_front_kernel(place, across, near, next_one, own, send):
    n = send.shape[0]
    rows = packed_rows(n)

    def body(maps):
        front = maps[0][3 * rows : 3 * rows + n, :].astype(F32)
        for one in maps[1:]:
            shift = one[3 * rows : 3 * rows + n, :].astype(F32)
            front = mm_fine(unpack(one, 0, n), front) + shift
        send[...] = front.astype(BF)

    per_owner(place, (own, near, next_one, across), body)


def joined(left, right):
    a_l, b_l, g_l, c_l, h_l = left
    a_r, b_r, g_r, c_r, h_r = right
    a = mm(a_r, a_l).astype(BF)
    b = mm(b_l, b_r).astype(BF)
    g = (mm(b_l, mm(g_r, a_l).astype(BF)) + g_l.astype(F32)).astype(BF)
    c = mm_fine(a_r, c_l) + c_r
    h = mm_fine(b_l, mm_fine(g_r, c_l) + h_r) + h_l
    return a, b, g, c, h


def segment(one, n):
    rows = packed_rows(n)
    return (
        unpack(one, 0, n),
        unpack(one, rows, n),
        unpack(one, 2 * rows, n),
        one[3 * rows : 3 * rows + n, :].astype(F32),
        one[3 * rows + n : 3 * rows + 2 * n, :].astype(F32),
    )


def group_map_kernel(
    place, across, near, next_one, own, a_out, b_out, g_out, c_out, h_out, send_far
):
    n = a_out.shape[0]

    def body(maps):
        segments = [segment(one, n) for one in maps]
        a, b, g, c, h = joined(joined(*segments[:2]), joined(*segments[2:]))
        a_out[...] = a
        b_out[...] = b
        g_out[...] = g
        c_out[...] = c
        h_out[...] = h
        send_far[0:n, :] = h.astype(BF)
        pack(send_far, n, g)

    per_owner(place, (own, near, next_one, across), body)


def forward_one_kernel(incoming, a, c, send):
    send[...] = (mm(a[...], incoming[...]) + c[...]).astype(BF)


def turn_kernel(incoming, far, a, b, g, c, h, send, front_out, back_in):
    n = a.shape[0]
    front = incoming[...]
    ahead = mm(a[...], front) + c[...]
    back = mm_fine(unpack(far, n, n), ahead) + far[0:n, :].astype(F32)
    send[...] = (mm_fine(b[...], back) + (mm(g[...], front) + h[...])).astype(BF)
    front_out[...] = ahead.astype(BF)
    back_in[...] = back.astype(BF)


def backward_one_kernel(place, b, g, h, hop1, incoming, ahead, send):
    back = mm(b[...], incoming[...]) + (mm(g[...], hop1[...]) + h[...])
    send[...] = jnp.where(place[4] == 1, back.astype(BF), ahead[...])


def interfaces_kernel(place, across, near, next_one, own, hop1, hop2, hop3, back2, hop4, out):
    n = hop2.shape[0]
    rows = packed_rows(n)
    which = place[4]
    zero = jnp.zeros_like(hop2[...])
    first = jnp.where(
        which == 0, zero,
        jnp.where(which == 1, hop1[...], jnp.where(which == 2, hop2[...], hop4[...])),
    ).astype(F32)
    last = jnp.where(
        which == 0, hop4[...],
        jnp.where(which == 1, hop3[...], jnp.where(which == 2, back2[...], zero)),
    ).astype(F32)

    def body(maps):
        fronts, back = [first], last
        for one in maps[:-1]:
            shift = one[3 * rows : 3 * rows + n, :].astype(F32)
            fronts.append(mm_fine(unpack(one, 0, n), fronts[-1]) + shift)
        for j in reversed(range(GROUP)):
            out[j, 0:n, :] = fronts[j].astype(BF)
            out[j, n : 2 * n, :] = back.astype(BF)
            if j:
                shift = maps[j][3 * rows + n : 3 * rows + 2 * n, :].astype(F32)
                inner = mm_fine(unpack(maps[j], 2 * rows, n), fronts[j]) + shift
                back = mm_fine(unpack(maps[j], rows, n), back) + inner

    per_owner(place, (own, near, next_one, across), body)


def whole_call(kernel, outs, scalars, *operands, name, cost=SHORT):
    specs = [pl.BlockSpec(memory_space=pltpu.SMEM)] * len(scalars)
    specs += [pl.BlockSpec(memory_space=pltpu.VMEM)] * len(operands)
    return pl.pallas_call(
        kernel,
        in_specs=specs,
        out_specs=[pl.BlockSpec(memory_space=pltpu.VMEM)] * len(outs),
        out_shape=[jax.ShapeDtypeStruct(s, d) for s, d in outs],
        compiler_params=pltpu.CompilerParams(vmem_limit_bytes=VMEM_LIMIT),
        cost_estimate=cost,
        name=name,
    )(*scalars, *operands)


def solve_pencils(ends, columns):
    n = ends[0].shape[0] // 2
    fronts = [e[0:n, :] for e in ends]
    backs = [e[n : 2 * n, :] for e in ends]
    both = range(len(ends))
    d0, d1, l0, l1, u0, u1, r0, r1 = zip(*columns)
    v = [mm(u1[i][...], backs[i]) for i in both]
    q = [r0[i][...].astype(F32) - mm(l0[i][...], fronts[i]) for i in both]
    f0 = [mm_fine(d0[i][...], q[i]) for i in both]
    v = [mm_fine(d1[i][...], v[i]) for i in both]
    q = [r1[i][...].astype(F32) - mm_fine(l1[i][...], f0[i]) for i in both]
    x1 = [mm_fine(d1[i][...], q[i]) - v[i] for i in both]
    q = [mm_fine(u0[i][...], x1[i]) for i in both]
    x0 = [f0[i] - mm_fine(d0[i][...], q[i]) for i in both]
    return [(x0[i].astype(BF), x1[i].astype(BF)) for i in both]


def two_pencils_kernel(chosen, slots, place, ends, *refs):
    outs, tops = refs[16:18], refs[18]
    solved = solve_pencils([ends[p] for p in chosen], [refs[0:8], refs[8:16]])
    for i, ((x0, x1), out) in enumerate(zip(solved, outs)):
        out[0] = x0
        out[1] = x1
        tops[i] = x1


def two_pencils(chosen, slots, place, ends, diag_inv, lower, upper, source):
    n, cols = source.shape[1:]
    specs, operands = [constant(ends.shape)], [ends]
    for p in chosen:
        for array in (diag_inv, lower, upper, source):
            for s in range(2):
                specs.append(stored(s, lambda at, p=p: p, n, array.shape[-1]))
                operands.append(array)
    return element_call(
        functools.partial(two_pencils_kernel, chosen), specs,
        [jax.ShapeDtypeStruct((2, n, cols), BF)] * 3, slots, place, *operands, name="two_pencils",
        cost=LONG if 0 in chosen else SHORT,
    )


def inner_jacobian_kernel(slots, *refs):
    blocks, (first, second, third, last, ends) = refs[0:10], refs[10:15]
    precond, partial, lowers, sides, vals = refs[15:]
    n = first.shape[1]
    pencil = pl.program_id(0)

    @pl.when(pencil == 0)
    def _():
        zero = jnp.zeros(first.shape[1:], BF)
        for p, values in enumerate((first, second, third, last)):
            vals[0, p + 1] = zero
            vals[1, p + 1] = values[0]
            vals[2, p + 1] = values[1]
            vals[3, p + 1] = ends[p, n : 2 * n, :]
        for s in range(2):
            vals[s + 1, 0] = zero
            vals[s + 1, GROUP + 1] = zero

    both = range(2)
    near = [
        [
            vals[s + 1, pencil + 1], vals[s, pencil + 1], vals[s + 2, pencil + 1],
            vals[s + 1, pencil], vals[s + 1, pencil + 2],
        ]
        for s in both
    ]
    totals = [mm(blocks[5 * s][...], near[s][0]) for s in both]
    for t in range(1, 5):
        totals = [totals[s] + mm(blocks[5 * s + t][...], near[s][t]) for s in both]
    for s in both:
        precond[slots[s, pencil]] = near[s][0]
        partial[s] = totals[s]
    lowers[...] = blocks[1][...]

    @pl.when(pencil == 0)
    def _():
        for s in both:
            sides[s] = blocks[5 * s + 3][...]

    @pl.when(pencil == GROUP - 1)
    def _():
        for s in both:
            sides[s + 2] = blocks[5 * s + 4][...]


def inner_jacobian(slots, blocks, vectors):
    n, cols = vectors[0].shape[1:]

    def whole(shape):
        return pl.BlockSpec(shape, lambda p, sl: (0, 0, 0))

    specs = [
        pl.BlockSpec((None, n, n), lambda p, sl, s=s: (sl[s, p], 0, 0))
        for s in range(2)
        for _ in blocks
    ]
    stored_shape = (2 * GROUP, n, cols)
    return pl.pallas_call(
        inner_jacobian_kernel,
        grid_spec=pltpu.PrefetchScalarGridSpec(
            num_scalar_prefetch=1,
            grid=(GROUP,),
            in_specs=specs + [whole(v.shape) for v in vectors],
            out_specs=[
                whole(stored_shape),
                pl.BlockSpec((None, 2, n, cols), lambda p, sl: (p, 0, 0, 0)),
                pl.BlockSpec((None, n, n), lambda p, sl: (p, 0, 0)),
                whole((4, n, n)),
            ],
            scratch_shapes=[pltpu.VMEM((4, GROUP + 2, n, cols), BF)],
        ),
        out_shape=[
            jax.ShapeDtypeStruct(stored_shape, BF),
            jax.ShapeDtypeStruct((GROUP, 2, n, cols), F32),
            jax.ShapeDtypeStruct((GROUP, n, n), BF),
            jax.ShapeDtypeStruct((4, n, n), BF),
        ],
        compiler_params=pltpu.CompilerParams(vmem_limit_bytes=VMEM_LIMIT),
        cost_estimate=SHORT,
        name="inner_jacobian",
    )(slots, *blocks, *blocks, *vectors)


def edge_jacobian_kernel(slots, place, low, high, below_outer, below_inner, partial, lowers, sides, jac):
    below = (below_outer.at[0], below_inner.at[0], below_inner.at[1], below_outer.at[1])
    left = jnp.where(place[1] == 0, 0.0, 1.0).astype(F32)
    right = jnp.where(place[1] == place[2] - 1, 0.0, 1.0).astype(F32)
    start = jnp.where(place[0] == 0, 0.0, 1.0).astype(F32)
    for s in range(2):
        for p in range(GROUP):
            total = partial[p, s]
            if s == 0:
                total = total + start * mm(lowers[p], below[p][...])
            if p == 0:
                total = total + left * mm(sides[s], low[s])
            if p == GROUP - 1:
                total = total + right * mm(sides[s + 2], high[s])
            jac[slots[s, p]] = total.astype(BF)


def local(right_side, diag_inv, diag_blk, lower_blk, upper_blk, cross_minus, cross_plus, elem_slot):
    n, cols = right_side.shape[2:]
    source, inverse, diagonal, lower, upper, minus, plus = (
        pltpu.with_memory_space_constraint(
            values.reshape((-1,) + values.shape[2:]), pltpu.HBM
        )
        for values in (
            right_side, diag_inv, diag_blk, lower_blk, upper_blk, cross_minus, cross_plus
        )
    )
    count = lax.axis_size("sweep")
    across = lax.axis_size("cross")
    sweep_at = lax.axis_index("sweep")
    place = jnp.stack(
        [
            sweep_at, lax.axis_index("cross"), jnp.int32(across),
            lax.rem(sweep_at, GROUP), lax.div(sweep_at, GROUP),
        ]
    ).astype(jnp.int32)
    groups = [list(range(g, g + GROUP)) for g in range(0, count, GROUP)]

    def swap(values, order):
        pairs = [(g * GROUP + k, order[g] * GROUP + k) for g in range(GROUP) for k in range(GROUP)]
        return lax.ppermute(values, "sweep", pairs)

    def to_peer(values, distance):
        return lax.ppermute(values, "sweep", [(i, i ^ distance) for i in range(count)])

    low_pair, high_pair, outer, inner = (1, 0, 2, 3), (0, 1, 3, 2), (1, 0, 3, 2), (0, 2, 1, 3)
    vec = ((n, cols), BF)
    maps = [None] * GROUP
    for distance in (3, 1, 2, 0):
        piece = local_map(elem_slot, place, inverse, lower, upper, source, distance)
        maps[distance] = to_peer(piece, distance) if distance else piece
    pieces = (maps[3], maps[1], maps[2], maps[0])

    (send,) = whole_call(group_front_kernel, [vec], [place], *pieces, name="group_front")
    hop1 = swap(send, low_pair)
    a, b, g, c, h, send_far = whole_call(
        group_map_kernel,
        [
            ((n, n), BF), ((n, n), BF), ((n, n), BF), ((n, cols), F32), ((n, cols), F32),
            ((n + packed_rows(n), cols), BF),
        ],
        [place], *pieces, name="group_map",
    )
    far = swap(send_far, high_pair)
    (send,) = whole_call(forward_one_kernel, [vec], [], hop1, a, c, name="forward_one", cost=LONG)
    hop2 = swap(send, inner)
    send, ahead, back2 = whole_call(
        turn_kernel, [vec, vec, vec], [], hop2, far, a, b, g, c, h, name="turn"
    )
    hop3 = swap(send, inner)
    (send,) = whole_call(
        backward_one_kernel, [vec], [place], b, g, h, hop1, hop3, ahead, name="backward_one"
    )
    hop4 = swap(send, outer)
    (ends,) = whole_call(
        interfaces_kernel, [((GROUP, 2 * n, cols), BF)], [place],
        *pieces, hop1, hop2, hop3, back2, hop4, name="interfaces",
    )
    ends = lax.all_to_all(ends, "sweep", 0, 0, axis_index_groups=groups)

    def solved(*chosen):
        return two_pencils(chosen, elem_slot, place, ends, inverse, lower, upper, source)

    def up(values):
        return lax.ppermute(values, "sweep", [(i, (i + 1) % count) for i in range(count)])

    first, last, tops = solved(0, GROUP - 1)
    low = lax.ppermute(last, "cross", [(i, (i + 1) % across) for i in range(across)])
    high = lax.ppermute(first, "cross", [((i + 1) % across, i) for i in range(across)])
    below_outer = up(tops)
    second, third, tops = solved(1, 2)
    below_inner = up(tops)
    precond, partial, lowers, sides = inner_jacobian(
        elem_slot, (diagonal, lower, upper, minus, plus), (first, second, third, last, ends)
    )
    (jac,) = whole_call(
        edge_jacobian_kernel, [((2 * GROUP, n, cols), BF)], [elem_slot, place],
        low, high, below_outer, below_inner, partial, lowers, sides, name="edge_jacobian",
    )
    return precond.reshape(right_side.shape), jac.reshape(right_side.shape)


def solution(mesh):
    blocks = P("sweep", "cross", None, None)
    in_specs = (blocks,) * 7 + (P("sweep", "cross"),)
    return jax.shard_map(
        local, mesh=mesh, in_specs=in_specs, out_specs=(blocks, blocks), check_vma=False
    )
```

```python
import functools

import jax
import jax.numpy as jnp
from jax import lax
from jax.experimental import pallas as pl
from jax.experimental.pallas import tpu as pltpu
from jax.sharding import PartitionSpec as P

BF = jnp.bfloat16
F32 = jnp.float32
GROUP = 4
VMEM_LIMIT = 28 << 20
LONG = pl.CostEstimate(flops=10**10, transcendentals=0, bytes_accessed=1024)
SHORT = pl.CostEstimate(flops=1024, transcendentals=0, bytes_accessed=1024)


def mm(a, b):
    return jnp.dot(a, b, preferred_element_type=F32)


def mm_fine(a, x):
    width = x.shape[1]
    top = x.astype(BF)
    rest = (x - top.astype(F32)).astype(BF)
    both = mm(a, jnp.concatenate([top, rest], axis=1))
    return both[:, :width] + both[:, width:]


def packed_rows(n):
    return 2 * n + n // 2


def pack(ref, base, mat):
    n = mat.shape[0]
    half = n // 2
    ref[base : base + n, :] = mat[:, 0:128]
    ref[base + n : base + 2 * n, :] = mat[:, 128:256]
    ref[base + 2 * n : base + 2 * n + half, 0:64] = mat[0:half, 256:320]
    ref[base + 2 * n : base + 2 * n + half, 64:128] = mat[half:n, 256:320]


def unpack(ref, base, n):
    half = n // 2
    tail = ref[base + 2 * n : base + 2 * n + half, :]
    last = jnp.concatenate([tail[:, 0:64], tail[:, 64:128]], axis=0)
    return jnp.concatenate(
        [ref[base : base + n, :], ref[base + n : base + 2 * n, :], last], axis=1
    )


def map_rows(n):
    return 3 * packed_rows(n) + 2 * n


def local_map_kernel(slots, place, d0, d1, l0, l1, u0, u1, r0, r1, out):
    n = d0.shape[0]
    rows = packed_rows(n)
    inv0, inv1 = d0[...], d1[...]
    e0 = mm(inv0, l0[...])
    e1 = mm(inv1, l1[...]).astype(BF)
    h0 = mm(inv0, u0[...]).astype(BF)
    h1 = mm(inv1, u1[...]).astype(BF)
    y0 = mm(inv0, r0[...])
    y1 = mm(inv1, r1[...])
    a = mm(e1, e0.astype(BF)).astype(BF)
    c = y1 - mm_fine(e1, y0)
    b = mm(h0, h1).astype(BF)
    g = -(e0 + mm(h0, a))
    h = y0 - mm_fine(h0, c)
    pack(out, 0, a)
    pack(out, rows, b)
    pack(out, 2 * rows, g.astype(BF))
    out[3 * rows : 3 * rows + n, :] = c.astype(BF)
    out[3 * rows + n : 3 * rows + 2 * n, :] = h.astype(BF)


def stored(slab, pencil, height, width):
    return pl.BlockSpec(
        (None, height, width), lambda i, sl, at: (sl[slab, pencil(at)], 0, 0)
    )


def constant(shape):
    return pl.BlockSpec(shape, lambda i, sl, at: (0,) * len(shape))


def element_call(kernel, in_specs, out_shape, slots, place, *operands, name, cost=SHORT):
    return pl.pallas_call(
        kernel,
        grid_spec=pltpu.PrefetchScalarGridSpec(
            num_scalar_prefetch=2,
            grid=(1,),
            in_specs=in_specs,
            out_specs=[constant(o.shape) for o in out_shape],
        ),
        out_shape=out_shape,
        compiler_params=pltpu.CompilerParams(vmem_limit_bytes=VMEM_LIMIT),
        cost_estimate=cost,
        name=name,
    )(slots, place, *operands)


def local_map(slots, place, diag_inv, lower, upper, source, distance):
    n, cols = source.shape[1:]

    def pencil(at):
        return lax.bitwise_xor(at[3], jnp.int32(distance))

    (out,) = element_call(
        local_map_kernel,
        [stored(s, pencil, n, n) for s in (0, 1, 0, 1, 0, 1)]
        + [stored(s, pencil, n, cols) for s in (0, 1)],
        [jax.ShapeDtypeStruct((map_rows(n), cols), BF)],
        slots, place, diag_inv, diag_inv, lower, lower, upper, upper, source, source,
        name="local_map",
    )
    return out


def halves(x):
    top = x.astype(BF)
    return top, (x - top.astype(F32)).astype(BF)


def prepare_kernel(
    slots, place, d0, d1, l0, l1, u0, u1, r0, r1, out, first_ops, second_ops, c_out, y_out
):
    n = d0.shape[0]
    rows = packed_rows(n)
    inv0, inv1 = d0[...], d1[...]
    e0 = mm(inv0, l0[...])
    e0_top, e0_rest = halves(e0)
    e1_top, e1_rest = halves(mm(inv1, l1[...]))
    h0_top, h0_rest = halves(mm(inv0, u0[...]))
    h1_top, h1_rest = halves(mm(inv1, u1[...]))
    y0 = mm(inv0, r0[...])
    a = mm(e1_top, e0_top) + (mm(e1_top, e0_rest) + mm(e1_rest, e0_top))
    c = mm(inv1, r1[...]) - (mm_fine(e1_top, y0) + mm(e1_rest, y0.astype(BF)))
    a_top, a_rest = halves(a)
    for t, part in enumerate((a_top, a_rest, -h1_top, -h1_rest)):
        first_ops[:, t * n : (t + 1) * n] = part
    for t, part in enumerate((-e0_top, -e0_rest, -h0_top, -h0_rest, -h0_top)):
        second_ops[:, t * n : (t + 1) * n] = part
    c_out[...] = c
    y_out[...] = y0

    @pl.when(pl.program_id(0) == place[3])
    def _():
        pack(out, 0, a_top)
        pack(out, rows, mm(h0_top, h1_top).astype(BF))
        pack(out, 2 * rows, (-(e0 + mm(h0_top, a_top))).astype(BF))
        out[3 * rows : 3 * rows + n, :] = c.astype(BF)
        out[3 * rows + n : 3 * rows + 2 * n, :] = (y0 - mm_fine(h0_top, c)).astype(BF)


def prepare(slots, place, diag_inv, lower, upper, source):
    n, cols = source.shape[1:]

    def block(slab, width):
        return pl.BlockSpec((None, n, width), lambda p, sl, at: (sl[slab, p], 0, 0))

    def per(width):
        return pl.BlockSpec((None, n, width), lambda p, sl, at: (p, 0, 0))

    shape = jax.ShapeDtypeStruct
    return pl.pallas_call(
        prepare_kernel,
        grid_spec=pltpu.PrefetchScalarGridSpec(
            num_scalar_prefetch=2,
            grid=(GROUP,),
            in_specs=[block(s, n) for s in (0, 1, 0, 1, 0, 1)] + [block(s, cols) for s in (0, 1)],
            out_specs=[
                pl.BlockSpec((map_rows(n), cols), lambda p, sl, at: (0, 0)),
                per(4 * n), per(5 * n), per(cols), per(cols),
            ],
        ),
        out_shape=[
            shape((map_rows(n), cols), BF),
            shape((GROUP, n, 4 * n), BF),
            shape((GROUP, n, 5 * n), BF),
            shape((GROUP, n, cols), F32),
            shape((GROUP, n, cols), F32),
        ],
        compiler_params=pltpu.CompilerParams(vmem_limit_bytes=VMEM_LIMIT),
        cost_estimate=SHORT,
        name="prepare",
    )(slots, place, diag_inv, diag_inv, lower, lower, upper, upper, source, source)


def per_owner(place, pieces, body):
    for owned in range(GROUP):

        @pl.when(place[3] == owned)
        def _(owned=owned):
            body([pieces[owned ^ j] for j in range(GROUP)])


def group_front_kernel(place, across, near, next_one, own, send):
    n = send.shape[0]
    rows = packed_rows(n)

    def body(maps):
        front = maps[0][3 * rows : 3 * rows + n, :].astype(F32)
        for one in maps[1:]:
            shift = one[3 * rows : 3 * rows + n, :].astype(F32)
            front = mm_fine(unpack(one, 0, n), front) + shift
        send[...] = front.astype(BF)

    per_owner(place, (own, near, next_one, across), body)


def joined(left, right):
    a_l, b_l, g_l, c_l, h_l = left
    a_r, b_r, g_r, c_r, h_r = right
    a = mm(a_r, a_l).astype(BF)
    b = mm(b_l, b_r).astype(BF)
    g = (mm(b_l, mm(g_r, a_l).astype(BF)) + g_l.astype(F32)).astype(BF)
    c = mm_fine(a_r, c_l) + c_r
    h = mm_fine(b_l, mm_fine(g_r, c_l) + h_r) + h_l
    return a, b, g, c, h


def segment(one, n):
    rows = packed_rows(n)
    return (
        unpack(one, 0, n),
        unpack(one, rows, n),
        unpack(one, 2 * rows, n),
        one[3 * rows : 3 * rows + n, :].astype(F32),
        one[3 * rows + n : 3 * rows + 2 * n, :].astype(F32),
    )


def group_map_kernel(
    place, across, near, next_one, own, a_out, b_out, g_out, c_out, h_out, send_far
):
    n = a_out.shape[0]

    def body(maps):
        segments = [segment(one, n) for one in maps]
        a, b, g, c, h = joined(joined(*segments[:2]), joined(*segments[2:]))
        a_out[...] = a
        b_out[...] = b
        g_out[...] = g
        c_out[...] = c
        h_out[...] = h
        send_far[0:n, :] = h.astype(BF)
        pack(send_far, n, g)

    per_owner(place, (own, near, next_one, across), body)


def forward_one_kernel(incoming, a, c, send):
    send[...] = (mm(a[...], incoming[...]) + c[...]).astype(BF)


def turn_kernel(incoming, far, a, b, g, c, h, send, front_out, back_in):
    n = a.shape[0]
    front = incoming[...]
    ahead = mm(a[...], front) + c[...]
    back = mm_fine(unpack(far, n, n), ahead) + far[0:n, :].astype(F32)
    send[...] = (mm_fine(b[...], back) + (mm(g[...], front) + h[...])).astype(BF)
    front_out[...] = ahead.astype(BF)
    back_in[...] = back.astype(BF)


def backward_one_kernel(place, b, g, h, hop1, incoming, ahead, send):
    back = mm(b[...], incoming[...]) + (mm(g[...], hop1[...]) + h[...])
    send[...] = jnp.where(place[4] == 1, back.astype(BF), ahead[...])


def interfaces_kernel(place, across, near, next_one, own, hop1, hop2, hop3, back2, hop4, out):
    n = hop2.shape[0]
    rows = packed_rows(n)
    which = place[4]
    zero = jnp.zeros_like(hop2[...])
    first = jnp.where(
        which == 0, zero,
        jnp.where(which == 1, hop1[...], jnp.where(which == 2, hop2[...], hop4[...])),
    ).astype(F32)
    last = jnp.where(
        which == 0, hop4[...],
        jnp.where(which == 1, hop3[...], jnp.where(which == 2, back2[...], zero)),
    ).astype(F32)

    def body(maps):
        fronts, back = [first], last
        for one in maps[:-1]:
            shift = one[3 * rows : 3 * rows + n, :].astype(F32)
            fronts.append(mm_fine(unpack(one, 0, n), fronts[-1]) + shift)
        for j in reversed(range(GROUP)):
            out[j, 0:n, :] = fronts[j].astype(BF)
            out[j, n : 2 * n, :] = back.astype(BF)
            if j:
                shift = maps[j][3 * rows + n : 3 * rows + 2 * n, :].astype(F32)
                inner = mm_fine(unpack(maps[j], 2 * rows, n), fronts[j]) + shift
                back = mm_fine(unpack(maps[j], rows, n), back) + inner

    per_owner(place, (own, near, next_one, across), body)


def whole_call(kernel, outs, scalars, *operands, name, cost=SHORT):
    specs = [pl.BlockSpec(memory_space=pltpu.SMEM)] * len(scalars)
    specs += [pl.BlockSpec(memory_space=pltpu.VMEM)] * len(operands)
    return pl.pallas_call(
        kernel,
        in_specs=specs,
        out_specs=[pl.BlockSpec(memory_space=pltpu.VMEM)] * len(outs),
        out_shape=[jax.ShapeDtypeStruct(s, d) for s, d in outs],
        compiler_params=pltpu.CompilerParams(vmem_limit_bytes=VMEM_LIMIT),
        cost_estimate=cost,
        name=name,
    )(*scalars, *operands)


def finish_kernel(place, ends, first_ops, second_ops, c, y0, within, beside, tops, solved):
    n = c.shape[1]
    every = range(GROUP)
    fronts = [ends[p, 0:n, :] for p in every]
    backs = [ends[p, n : 2 * n, :] for p in every]
    x1 = [
        c[p] + mm(first_ops[p], jnp.concatenate([fronts[p], fronts[p], backs[p], backs[p]], axis=0))
        for p in every
    ]
    for p in every:
        top, rest = halves(x1[p])
        x0 = y0[p] + mm(
            second_ops[p], jnp.concatenate([fronts[p], fronts[p], top, top, rest], axis=0)
        )
        solved[p, 0] = x0.astype(BF)
        solved[p, 1] = top
        tops[p] = top
    even = lax.rem(place[1], 2) == 0
    for s in range(2):
        first, last = solved[0, s], solved[GROUP - 1, s]
        within[s] = jnp.where(even, last, first)
        beside[s] = jnp.where(even, first, last)


def inner_jacobian_kernel(slots, *refs):
    blocks, (solved, ends) = refs[0:10], refs[10:12]
    precond, partial, lowers, sides, vals = refs[12:]
    n = solved.shape[2]
    pencil = pl.program_id(0)

    @pl.when(pencil == 0)
    def _():
        zero = jnp.zeros(solved.shape[2:], BF)
        for p in range(GROUP):
            vals[0, p + 1] = zero
            vals[1, p + 1] = solved[p, 0]
            vals[2, p + 1] = solved[p, 1]
            vals[3, p + 1] = ends[p, n : 2 * n, :]
        for s in range(2):
            vals[s + 1, 0] = zero
            vals[s + 1, GROUP + 1] = zero

    both = range(2)
    near = [
        [
            vals[s + 1, pencil + 1], vals[s, pencil + 1], vals[s + 2, pencil + 1],
            vals[s + 1, pencil], vals[s + 1, pencil + 2],
        ]
        for s in both
    ]
    totals = [mm(blocks[5 * s][...], near[s][0]) for s in both]
    for t in range(1, 5):
        totals = [totals[s] + mm(blocks[5 * s + t][...], near[s][t]) for s in both]
    for s in both:
        precond[slots[s, pencil]] = near[s][0]
        partial[s] = totals[s]
    lowers[...] = blocks[1][...]

    @pl.when(pencil == 0)
    def _():
        for s in both:
            sides[s] = blocks[5 * s + 3][...]

    @pl.when(pencil == GROUP - 1)
    def _():
        for s in both:
            sides[s + 2] = blocks[5 * s + 4][...]


def inner_jacobian(slots, blocks, vectors):
    n, cols = vectors[0].shape[2:]

    def whole(shape):
        return pl.BlockSpec(shape, lambda p, sl: (0,) * len(shape))

    specs = [
        pl.BlockSpec((None, n, n), lambda p, sl, s=s: (sl[s, p], 0, 0))
        for s in range(2)
        for _ in blocks
    ]
    stored_shape = (2 * GROUP, n, cols)
    return pl.pallas_call(
        inner_jacobian_kernel,
        grid_spec=pltpu.PrefetchScalarGridSpec(
            num_scalar_prefetch=1,
            grid=(GROUP,),
            in_specs=specs + [whole(v.shape) for v in vectors],
            out_specs=[
                whole(stored_shape),
                pl.BlockSpec((None, 2, n, cols), lambda p, sl: (p, 0, 0, 0)),
                pl.BlockSpec((None, n, n), lambda p, sl: (p, 0, 0)),
                whole((4, n, n)),
            ],
            scratch_shapes=[pltpu.VMEM((4, GROUP + 2, n, cols), BF)],
        ),
        out_shape=[
            jax.ShapeDtypeStruct(stored_shape, BF),
            jax.ShapeDtypeStruct((GROUP, 2, n, cols), F32),
            jax.ShapeDtypeStruct((GROUP, n, n), BF),
            jax.ShapeDtypeStruct((4, n, n), BF),
        ],
        compiler_params=pltpu.CompilerParams(vmem_limit_bytes=VMEM_LIMIT),
        cost_estimate=SHORT,
        name="inner_jacobian",
    )(slots, *blocks, *blocks, *vectors)


def edge_jacobian_kernel(slots, place, beside, below, within, partial, lowers, sides, jac):
    even = lax.rem(place[1], 2) == 0
    low = [jnp.where(even, beside[s], within[s]) for s in range(2)]
    high = [jnp.where(even, within[s], beside[s]) for s in range(2)]
    left = jnp.where(place[1] == 0, 0.0, 1.0).astype(F32)
    right = jnp.where(place[1] == place[2] - 1, 0.0, 1.0).astype(F32)
    start = jnp.where(place[0] == 0, 0.0, 1.0).astype(F32)
    for s in range(2):
        for p in range(GROUP):
            total = partial[p, s]
            if s == 0:
                total = total + start * mm(lowers[p], below[p])
            if p == 0:
                total = total + left * mm(sides[s], low[s])
            if p == GROUP - 1:
                total = total + right * mm(sides[s + 2], high[s])
            jac[slots[s, p]] = total.astype(BF)


def local(right_side, diag_inv, diag_blk, lower_blk, upper_blk, cross_minus, cross_plus, elem_slot):
    n, cols = right_side.shape[2:]
    source, inverse, diagonal, lower, upper, minus, plus = (
        pltpu.with_memory_space_constraint(
            values.reshape((-1,) + values.shape[2:]), pltpu.HBM
        )
        for values in (
            right_side, diag_inv, diag_blk, lower_blk, upper_blk, cross_minus, cross_plus
        )
    )
    count = lax.axis_size("sweep")
    across = lax.axis_size("cross")
    sweep_at = lax.axis_index("sweep")
    place = jnp.stack(
        [
            sweep_at, lax.axis_index("cross"), jnp.int32(across),
            lax.rem(sweep_at, GROUP), lax.div(sweep_at, GROUP),
        ]
    ).astype(jnp.int32)
    groups = [list(range(g, g + GROUP)) for g in range(0, count, GROUP)]

    def swap(values, order):
        pairs = [(g * GROUP + k, order[g] * GROUP + k) for g in range(GROUP) for k in range(GROUP)]
        return lax.ppermute(values, "sweep", pairs)

    def to_peer(values, distance):
        return lax.ppermute(values, "sweep", [(i, i ^ distance) for i in range(count)])

    low_pair, high_pair, outer, inner = (1, 0, 2, 3), (0, 1, 3, 2), (1, 0, 3, 2), (0, 2, 1, 3)
    vec = ((n, cols), BF)
    maps = [None] * GROUP
    for distance in (3, 1, 2):
        piece = local_map(elem_slot, place, inverse, lower, upper, source, distance)
        maps[distance] = to_peer(piece, distance)
    maps[0], first_ops, second_ops, c_own, y_own = prepare(
        elem_slot, place, inverse, lower, upper, source
    )
    pieces = (maps[3], maps[1], maps[2], maps[0])

    (send,) = whole_call(group_front_kernel, [vec], [place], *pieces, name="group_front")
    hop1 = swap(send, low_pair)
    a, b, g, c, h, send_far = whole_call(
        group_map_kernel,
        [
            ((n, n), BF), ((n, n), BF), ((n, n), BF), ((n, cols), F32), ((n, cols), F32),
            ((n + packed_rows(n), cols), BF),
        ],
        [place], *pieces, name="group_map",
    )
    far = swap(send_far, high_pair)
    (send,) = whole_call(forward_one_kernel, [vec], [], hop1, a, c, name="forward_one", cost=LONG)
    hop2 = swap(send, inner)
    send, ahead, back2 = whole_call(
        turn_kernel, [vec, vec, vec], [], hop2, far, a, b, g, c, h, name="turn"
    )
    hop3 = swap(send, inner)
    (send,) = whole_call(
        backward_one_kernel, [vec], [place], b, g, h, hop1, hop3, ahead, name="backward_one"
    )
    hop4 = swap(send, outer)
    (ends,) = whole_call(
        interfaces_kernel, [((GROUP, 2 * n, cols), BF)], [place],
        *pieces, hop1, hop2, hop3, back2, hop4, name="interfaces",
    )
    ends = lax.all_to_all(ends, "sweep", 0, 0, axis_index_groups=groups)

    pair = ((2, n, cols), BF)
    within, beside, tops, solved = whole_call(
        finish_kernel, [pair, pair, ((GROUP, n, cols), BF), ((GROUP, 2, n, cols), BF)], [place],
        ends, first_ops, second_ops, c_own, y_own, name="finish",
    )
    aside = [(across - 1, across - 1), (0, 0)]
    for i in range(1, across - 1, 2):
        aside += [(i, i + 1), (i + 1, i)]
    beside = lax.ppermute(beside, "cross", aside)
    below = lax.ppermute(tops, "sweep", [(i, (i + 1) % count) for i in range(count)])
    within = lax.ppermute(within, "cross", [(i, i ^ 1) for i in range(across)])
    precond, partial, lowers, sides = inner_jacobian(
        elem_slot, (diagonal, lower, upper, minus, plus), (solved, ends)
    )
    (jac,) = whole_call(
        edge_jacobian_kernel, [((2 * GROUP, n, cols), BF)], [elem_slot, place],
        beside, below, within, partial, lowers, sides, name="edge_jacobian",
    )
    return precond.reshape(right_side.shape), jac.reshape(right_side.shape)


def solution(mesh):
    blocks = P("sweep", "cross", None, None)
    in_specs = (blocks,) * 7 + (P("sweep", "cross"),)
    return jax.shard_map(
        local, mesh=mesh, in_specs=in_specs, out_specs=(blocks, blocks), check_vma=False
    )
```

```python
import functools

import jax
import jax.numpy as jnp
from jax import lax
from jax.experimental import pallas as pl
from jax.experimental.pallas import tpu as pltpu
from jax.sharding import PartitionSpec as P

BF = jnp.bfloat16
F32 = jnp.float32
GROUP = 4
VMEM_LIMIT = 28 << 20
LONG = pl.CostEstimate(flops=10**10, transcendentals=0, bytes_accessed=1024)
SHORT = pl.CostEstimate(flops=1024, transcendentals=0, bytes_accessed=1024)


def mm(a, b):
    return jnp.dot(a, b, preferred_element_type=F32)


def mm_fine(a, x):
    width = x.shape[1]
    top = x.astype(BF)
    rest = (x - top.astype(F32)).astype(BF)
    both = mm(a, jnp.concatenate([top, rest], axis=1))
    return both[:, :width] + both[:, width:]


def packed_rows(n):
    return 2 * n + n // 2


def pack(ref, base, mat):
    n = mat.shape[0]
    half = n // 2
    ref[base : base + n, :] = mat[:, 0:128]
    ref[base + n : base + 2 * n, :] = mat[:, 128:256]
    ref[base + 2 * n : base + 2 * n + half, 0:64] = mat[0:half, 256:320]
    ref[base + 2 * n : base + 2 * n + half, 64:128] = mat[half:n, 256:320]


def unpack(ref, base, n):
    half = n // 2
    tail = ref[base + 2 * n : base + 2 * n + half, :]
    last = jnp.concatenate([tail[:, 0:64], tail[:, 64:128]], axis=0)
    return jnp.concatenate(
        [ref[base : base + n, :], ref[base + n : base + 2 * n, :], last], axis=1
    )


def map_rows(n):
    return 3 * packed_rows(n) + 2 * n


def local_map_kernel(slots, place, d0, d1, l0, l1, u0, u1, r0, r1, out):
    n = d0.shape[0]
    rows = packed_rows(n)
    inv0, inv1 = d0[...], d1[...]
    e0 = mm(inv0, l0[...])
    e1 = mm(inv1, l1[...]).astype(BF)
    h0 = mm(inv0, u0[...]).astype(BF)
    h1 = mm(inv1, u1[...]).astype(BF)
    y0 = mm(inv0, r0[...])
    y1 = mm(inv1, r1[...])
    a = mm(e1, e0.astype(BF)).astype(BF)
    c = y1 - mm_fine(e1, y0)
    b = mm(h0, h1).astype(BF)
    g = -(e0 + mm(h0, a))
    h = y0 - mm_fine(h0, c)
    pack(out, 0, a)
    pack(out, rows, b)
    pack(out, 2 * rows, g.astype(BF))
    out[3 * rows : 3 * rows + n, :] = c.astype(BF)
    out[3 * rows + n : 3 * rows + 2 * n, :] = h.astype(BF)


def stored(slab, pencil, height, width):
    return pl.BlockSpec(
        (None, height, width), lambda i, sl, at: (sl[slab, pencil(at)], 0, 0)
    )


def constant(shape):
    return pl.BlockSpec(shape, lambda i, sl, at: (0,) * len(shape))


def element_call(kernel, in_specs, out_shape, slots, place, *operands, name, cost=SHORT):
    return pl.pallas_call(
        kernel,
        grid_spec=pltpu.PrefetchScalarGridSpec(
            num_scalar_prefetch=2,
            grid=(1,),
            in_specs=in_specs,
            out_specs=[constant(o.shape) for o in out_shape],
        ),
        out_shape=out_shape,
        compiler_params=pltpu.CompilerParams(vmem_limit_bytes=VMEM_LIMIT),
        cost_estimate=cost,
        name=name,
    )(slots, place, *operands)


def local_map(slots, place, diag_inv, lower, upper, source, distance):
    n, cols = source.shape[1:]

    def pencil(at):
        return lax.bitwise_xor(at[3], jnp.int32(distance))

    (out,) = element_call(
        local_map_kernel,
        [stored(s, pencil, n, n) for s in (0, 1, 0, 1, 0, 1)]
        + [stored(s, pencil, n, cols) for s in (0, 1)],
        [jax.ShapeDtypeStruct((map_rows(n), cols), BF)],
        slots, place, diag_inv, diag_inv, lower, lower, upper, upper, source, source,
        name="local_map",
    )
    return out


def halves(x):
    top = x.astype(BF)
    return top, (x - top.astype(F32)).astype(BF)


def prepare_kernel(slots, place, *refs):
    d0, d1, l0, l1, u0, u1, r0, r1 = refs[0:8]
    diags, minuses, pluses = refs[8:10], refs[10:12], refs[12:14]
    out, first_ops, second_ops, c_out, y_out, rows_out, lowers, sides = refs[14:]
    n = d0.shape[0]
    pencil = pl.program_id(0)
    for s in range(2):
        row = (diags[s], (l0, l1)[s], (u0, u1)[s], minuses[s], pluses[s])
        for t, block in enumerate(row):
            rows_out[s, :, t * n : (t + 1) * n] = block[...]
    lowers[...] = l0[...]

    @pl.when(pencil == 0)
    def _():
        for s in range(2):
            sides[s] = minuses[s][...]

    @pl.when(pencil == GROUP - 1)
    def _():
        for s in range(2):
            sides[s + 2] = pluses[s][...]

    rows = packed_rows(n)
    inv0, inv1 = d0[...], d1[...]
    e0 = mm(inv0, l0[...])
    e0_top, e0_rest = halves(e0)
    e1_top, e1_rest = halves(mm(inv1, l1[...]))
    h0_top, h0_rest = halves(mm(inv0, u0[...]))
    h1_top, h1_rest = halves(mm(inv1, u1[...]))
    y0 = mm(inv0, r0[...])
    a = mm(e1_top, e0_top) + (mm(e1_top, e0_rest) + mm(e1_rest, e0_top))
    c = mm(inv1, r1[...]) - (mm_fine(e1_top, y0) + mm(e1_rest, y0.astype(BF)))
    a_top, a_rest = halves(a)
    for t, part in enumerate((a_top, a_rest, -h1_top, -h1_rest)):
        first_ops[:, t * n : (t + 1) * n] = part
    for t, part in enumerate((-e0_top, -e0_rest, -h0_top, -h0_rest, -h0_top)):
        second_ops[:, t * n : (t + 1) * n] = part
    c_out[...] = c
    y_out[...] = y0

    @pl.when(pencil == place[3])
    def _():
        pack(out, 0, a_top)
        pack(out, rows, mm(h0_top, h1_top).astype(BF))
        pack(out, 2 * rows, (-(e0 + mm(h0_top, a_top))).astype(BF))
        out[3 * rows : 3 * rows + n, :] = c.astype(BF)
        out[3 * rows + n : 3 * rows + 2 * n, :] = (y0 - mm_fine(h0_top, c)).astype(BF)


def prepare(slots, place, diag_inv, lower, upper, source, diagonal, minus, plus):
    n, cols = source.shape[1:]

    def block(slab, width):
        return pl.BlockSpec((None, n, width), lambda p, sl, at: (sl[slab, p], 0, 0))

    def per(width):
        return pl.BlockSpec((None, n, width), lambda p, sl, at: (p, 0, 0))

    shape = jax.ShapeDtypeStruct
    return pl.pallas_call(
        prepare_kernel,
        grid_spec=pltpu.PrefetchScalarGridSpec(
            num_scalar_prefetch=2,
            grid=(GROUP,),
            in_specs=[block(s, n) for s in (0, 1) * 3]
            + [block(s, cols) for s in (0, 1)]
            + [block(s, n) for s in (0, 1) * 3],
            out_specs=[
                pl.BlockSpec((map_rows(n), cols), lambda p, sl, at: (0, 0)),
                per(4 * n), per(5 * n), per(cols), per(cols),
                pl.BlockSpec((None, 2, n, 5 * n), lambda p, sl, at: (p, 0, 0, 0)),
                per(n),
                pl.BlockSpec((4, n, n), lambda p, sl, at: (0, 0, 0)),
            ],
        ),
        out_shape=[
            shape((map_rows(n), cols), BF),
            shape((GROUP, n, 4 * n), BF),
            shape((GROUP, n, 5 * n), BF),
            shape((GROUP, n, cols), F32),
            shape((GROUP, n, cols), F32),
            shape((GROUP, 2, n, 5 * n), BF),
            shape((GROUP, n, n), BF),
            shape((4, n, n), BF),
        ],
        compiler_params=pltpu.CompilerParams(vmem_limit_bytes=VMEM_LIMIT),
        cost_estimate=SHORT,
        name="prepare",
    )(
        slots, place, diag_inv, diag_inv, lower, lower, upper, upper, source, source,
        diagonal, diagonal, minus, minus, plus, plus,
    )


def per_owner(place, pieces, body):
    for owned in range(GROUP):

        @pl.when(place[3] == owned)
        def _(owned=owned):
            body([pieces[owned ^ j] for j in range(GROUP)])


def segment(one, n):
    rows = packed_rows(n)
    return (
        unpack(one, 0, n),
        unpack(one, rows, n),
        unpack(one, 2 * rows, n),
        one[3 * rows : 3 * rows + n, :].astype(F32),
        one[3 * rows + n : 3 * rows + 2 * n, :].astype(F32),
    )


def group_back_kernel(
    place, across, near, next_one, own, a_low, b_low, c_low, g_out, h_out, send_far
):
    n = a_low.shape[0]

    def body(maps):
        (a0, b0, g0, c0, h0), (a1, b1, g1, c1, h1), (a2, b2, g2, c2, h2), (_, _, g3, _, h3) = (
            segment(one, n) for one in maps
        )
        a = mm(a1, a0).astype(BF)
        b = mm(b0, b1).astype(BF)
        c = mm_fine(a1, c0) + c1
        low_g = mm(b0, mm(g1, a0).astype(BF)) + g0.astype(F32)
        high_g = (mm(b2, mm(g3, a2).astype(BF)) + g2.astype(F32)).astype(BF)
        g = (mm(b, mm(high_g, a).astype(BF)) + low_g).astype(BF)
        low_h = mm_fine(b0, mm_fine(g1, c0) + h1) + h0
        high_h = mm_fine(b2, mm_fine(g3, c2) + h3) + h2
        h = mm_fine(b, mm_fine(high_g, c) + high_h) + low_h
        a_low[...] = a
        b_low[...] = b
        c_low[...] = c
        g_out[...] = g
        h_out[...] = h
        send_far[0:n, :] = h.astype(BF)
        pack(send_far, n, g)

    per_owner(place, (own, near, next_one, across), body)


def group_front_kernel(
    place, across, near, next_one, own, a_low, b_low, c_low, send, a_out, b_out, c_out
):
    n = a_low.shape[0]

    def body(maps):
        (a2, b2, _, c2, _), (a3, b3, _, c3, _) = (segment(one, n) for one in maps[2:])
        a = mm(a3, a2).astype(BF)
        c = mm_fine(a, c_low[...]) + (mm_fine(a3, c2) + c3)
        send[...] = c.astype(BF)
        c_out[...] = c
        a_out[...] = mm(a, a_low[...]).astype(BF)
        b_out[...] = mm(b_low[...], mm(b2, b3).astype(BF)).astype(BF)

    per_owner(place, (own, near, next_one, across), body)


def forward_one_kernel(incoming, a, c, send):
    send[...] = (mm(a[...], incoming[...]) + c[...]).astype(BF)


def turn_kernel(incoming, far, a, b, g, c, h, send, front_out, back_in):
    n = a.shape[0]
    front = incoming[...]
    ahead = mm(a[...], front) + c[...]
    back = mm_fine(unpack(far, n, n), ahead) + far[0:n, :].astype(F32)
    send[...] = (mm_fine(b[...], back) + (mm(g[...], front) + h[...])).astype(BF)
    front_out[...] = ahead.astype(BF)
    back_in[...] = back.astype(BF)


def backward_one_kernel(place, b, g, h, hop1, incoming, ahead, send):
    back = mm(b[...], incoming[...]) + (mm(g[...], hop1[...]) + h[...])
    send[...] = jnp.where(place[4] == 1, back.astype(BF), ahead[...])


def interfaces_kernel(place, across, near, next_one, own, hop1, hop2, hop3, back2, hop4, out):
    n = hop2.shape[0]
    rows = packed_rows(n)
    which = place[4]
    zero = jnp.zeros_like(hop2[...])
    first = jnp.where(
        which == 0, zero,
        jnp.where(which == 1, hop1[...], jnp.where(which == 2, hop2[...], hop4[...])),
    ).astype(F32)
    last = jnp.where(
        which == 0, hop4[...],
        jnp.where(which == 1, hop3[...], jnp.where(which == 2, back2[...], zero)),
    ).astype(F32)

    def body(maps):
        fronts, back = [first], last
        for one in maps[:-1]:
            shift = one[3 * rows : 3 * rows + n, :].astype(F32)
            fronts.append(mm_fine(unpack(one, 0, n), fronts[-1]) + shift)
        for j in reversed(range(GROUP)):
            out[j, 0:n, :] = fronts[j].astype(BF)
            out[j, n : 2 * n, :] = back.astype(BF)
            if j:
                shift = maps[j][3 * rows + n : 3 * rows + 2 * n, :].astype(F32)
                inner = mm_fine(unpack(maps[j], 2 * rows, n), fronts[j]) + shift
                back = mm_fine(unpack(maps[j], rows, n), back) + inner

    per_owner(place, (own, near, next_one, across), body)


def whole_call(kernel, outs, scalars, *operands, name, cost=SHORT):
    specs = [pl.BlockSpec(memory_space=pltpu.SMEM)] * len(scalars)
    specs += [pl.BlockSpec(memory_space=pltpu.VMEM)] * len(operands)
    return pl.pallas_call(
        kernel,
        in_specs=specs,
        out_specs=[pl.BlockSpec(memory_space=pltpu.VMEM)] * len(outs),
        out_shape=[jax.ShapeDtypeStruct(s, d) for s, d in outs],
        compiler_params=pltpu.CompilerParams(vmem_limit_bytes=VMEM_LIMIT),
        cost_estimate=cost,
        name=name,
    )(*scalars, *operands)


def finish_kernel(place, ends, first_ops, second_ops, c, y0, beside, tops, solved):
    n = c.shape[1]
    every = range(GROUP)
    fronts = [ends[p, 0:n, :] for p in every]
    backs = [ends[p, n : 2 * n, :] for p in every]
    x1 = [
        c[p] + mm(first_ops[p], jnp.concatenate([fronts[p], fronts[p], backs[p], backs[p]], axis=0))
        for p in every
    ]
    for p in every:
        top, rest = halves(x1[p])
        x0 = y0[p] + mm(
            second_ops[p], jnp.concatenate([fronts[p], fronts[p], top, top, rest], axis=0)
        )
        solved[p, 0] = x0.astype(BF)
        solved[p, 1] = top
        tops[p] = top
    even = lax.rem(place[1], 2) == 0
    for s in range(2):
        beside[s] = jnp.where(even, solved[0, s], solved[GROUP - 1, s])


def row_products(chosen, rows, solved, ends, partial):
    n = solved.shape[2]
    zero = jnp.zeros(solved.shape[2:], BF)

    def value(s, p):
        if p < 0 or p >= GROUP or s < 0:
            return zero
        return ends[p, n : 2 * n, :] if s == 2 else solved[p, s]

    for i, p in enumerate(chosen):
        for s in range(2):
            around = [value(s, p), value(s - 1, p), value(s + 1, p), value(s, p - 1), value(s, p + 1)]
            partial[i, s] = mm(rows[p, s], jnp.concatenate(around, axis=0))


def first_rows_kernel(place, rows, solved, ends, within, partial):
    even = lax.rem(place[1], 2) == 0
    row_products((0, 1), rows, solved, ends, partial)
    for s in range(2):
        within[s] = jnp.where(even, solved[GROUP - 1, s], solved[0, s])


def second_rows_kernel(slots, rows, solved, ends, precond, partial):
    row_products((2, 3), rows, solved, ends, partial)
    for s in range(2):
        for p in range(GROUP):
            precond[slots[s, p]] = solved[p, s]


def edge_jacobian_kernel(slots, place, beside, below, within, partial_a, partial_b, lowers, sides, jac):
    even = lax.rem(place[1], 2) == 0
    low = [jnp.where(even, beside[s], within[s]) for s in range(2)]
    high = [jnp.where(even, within[s], beside[s]) for s in range(2)]
    left = jnp.where(place[1] == 0, 0.0, 1.0).astype(F32)
    right = jnp.where(place[1] == place[2] - 1, 0.0, 1.0).astype(F32)
    start = jnp.where(place[0] == 0, 0.0, 1.0).astype(F32)
    for s in range(2):
        for p in range(GROUP):
            total = partial_a[p, s] if p < 2 else partial_b[p - 2, s]
            if s == 0:
                total = total + start * mm(lowers[p], below[p])
            if p == 0:
                total = total + left * mm(sides[s], low[s])
            if p == GROUP - 1:
                total = total + right * mm(sides[s + 2], high[s])
            jac[slots[s, p]] = total.astype(BF)


def local(right_side, diag_inv, diag_blk, lower_blk, upper_blk, cross_minus, cross_plus, elem_slot):
    n, cols = right_side.shape[2:]
    source, inverse, diagonal, lower, upper, minus, plus = (
        pltpu.with_memory_space_constraint(
            values.reshape((-1,) + values.shape[2:]), pltpu.HBM
        )
        for values in (
            right_side, diag_inv, diag_blk, lower_blk, upper_blk, cross_minus, cross_plus
        )
    )
    count = lax.axis_size("sweep")
    across = lax.axis_size("cross")
    sweep_at = lax.axis_index("sweep")
    place = jnp.stack(
        [
            sweep_at, lax.axis_index("cross"), jnp.int32(across),
            lax.rem(sweep_at, GROUP), lax.div(sweep_at, GROUP),
        ]
    ).astype(jnp.int32)
    groups = [list(range(g, g + GROUP)) for g in range(0, count, GROUP)]

    def swap(values, order):
        pairs = [(g * GROUP + k, order[g] * GROUP + k) for g in range(GROUP) for k in range(GROUP)]
        return lax.ppermute(values, "sweep", pairs)

    def to_peer(values, distance):
        return lax.ppermute(values, "sweep", [(i, i ^ distance) for i in range(count)])

    low_pair, high_pair, outer, inner = (1, 0, 2, 3), (0, 1, 3, 2), (1, 0, 3, 2), (0, 2, 1, 3)
    vec, vec32, mat = ((n, cols), BF), ((n, cols), F32), ((n, n), BF)
    maps = [None] * GROUP
    for distance in (3, 1, 2):
        piece = local_map(elem_slot, place, inverse, lower, upper, source, distance)
        maps[distance] = to_peer(piece, distance)
    maps[0], first_ops, second_ops, c_own, y_own, rows, lowers, sides = prepare(
        elem_slot, place, inverse, lower, upper, source, diagonal, minus, plus
    )
    pieces = (maps[3], maps[1], maps[2], maps[0])

    a_low, b_low, c_low, g, h, send_far = whole_call(
        group_back_kernel, [mat, mat, vec32, mat, vec32, ((n + packed_rows(n), cols), BF)],
        [place], *pieces, name="group_back",
    )
    far = swap(send_far, high_pair)
    send, a, b, c = whole_call(
        group_front_kernel, [vec, mat, mat, vec32], [place],
        *pieces, a_low, b_low, c_low, name="group_front",
    )
    hop1 = swap(send, low_pair)
    (send,) = whole_call(forward_one_kernel, [vec], [], hop1, a, c, name="forward_one")
    hop2 = swap(send, inner)
    send, ahead, back2 = whole_call(
        turn_kernel, [vec, vec, vec], [], hop2, far, a, b, g, c, h, name="turn"
    )
    hop3 = swap(send, inner)
    (send,) = whole_call(
        backward_one_kernel, [vec], [place], b, g, h, hop1, hop3, ahead, name="backward_one"
    )
    hop4 = swap(send, outer)
    (ends,) = whole_call(
        interfaces_kernel, [((GROUP, 2 * n, cols), BF)], [place],
        *pieces, hop1, hop2, hop3, back2, hop4, name="interfaces",
    )
    ends = lax.all_to_all(ends, "sweep", 0, 0, axis_index_groups=groups)

    pair = ((2, n, cols), BF)
    beside, tops, solved = whole_call(
        finish_kernel, [pair, ((GROUP, n, cols), BF), ((GROUP, 2, n, cols), BF)], [place],
        ends, first_ops, second_ops, c_own, y_own, name="finish",
    )
    aside = [(across - 1, across - 1), (0, 0)]
    for i in range(1, across - 1, 2):
        aside += [(i, i + 1), (i + 1, i)]
    beside = lax.ppermute(beside, "cross", aside)
    below = lax.ppermute(tops, "sweep", [(i, (i + 1) % count) for i in range(count)])
    part = ((2, 2, n, cols), F32)
    within, partial_a = whole_call(
        first_rows_kernel, [pair, part], [place], rows, solved, ends, name="first_rows"
    )
    within = lax.ppermute(within, "cross", [(i, i ^ 1) for i in range(across)])
    every = ((2 * GROUP, n, cols), BF)
    precond, partial_b = whole_call(
        second_rows_kernel, [every, part], [elem_slot], rows, solved, ends, name="second_rows"
    )
    (jac,) = whole_call(
        edge_jacobian_kernel, [every], [elem_slot, place],
        beside, below, within, partial_a, partial_b, lowers, sides, name="edge_jacobian",
    )
    return precond.reshape(right_side.shape), jac.reshape(right_side.shape)


def solution(mesh):
    blocks = P("sweep", "cross", None, None)
    in_specs = (blocks,) * 7 + (P("sweep", "cross"),)
    return jax.shard_map(
        local, mesh=mesh, in_specs=in_specs, out_specs=(blocks, blocks), check_vma=False
    )
```

```python
import functools

import jax
import jax.numpy as jnp
from jax import lax
from jax.experimental import pallas as pl
from jax.experimental.pallas import tpu as pltpu
from jax.sharding import PartitionSpec as P

BF = jnp.bfloat16
F32 = jnp.float32
GROUP = 4
VMEM_LIMIT = 28 << 20
LONG = pl.CostEstimate(flops=10**10, transcendentals=0, bytes_accessed=1024)
SHORT = pl.CostEstimate(flops=1024, transcendentals=0, bytes_accessed=1024)


def mm(a, b):
    return jnp.dot(a, b, preferred_element_type=F32)


def mm_fine(a, x):
    width = x.shape[1]
    top = x.astype(BF)
    rest = (x - top.astype(F32)).astype(BF)
    both = mm(a, jnp.concatenate([top, rest], axis=1))
    return both[:, :width] + both[:, width:]


def packed_rows(n):
    return 2 * n + n // 2


def pack(ref, base, mat):
    n = mat.shape[0]
    half = n // 2
    ref[base : base + n, :] = mat[:, 0:128]
    ref[base + n : base + 2 * n, :] = mat[:, 128:256]
    ref[base + 2 * n : base + 2 * n + half, 0:64] = mat[0:half, 256:320]
    ref[base + 2 * n : base + 2 * n + half, 64:128] = mat[half:n, 256:320]


def unpack(ref, base, n):
    half = n // 2
    tail = ref[base + 2 * n : base + 2 * n + half, :]
    last = jnp.concatenate([tail[:, 0:64], tail[:, 64:128]], axis=0)
    return jnp.concatenate(
        [ref[base : base + n, :], ref[base + n : base + 2 * n, :], last], axis=1
    )


def map_rows(n):
    return 3 * packed_rows(n) + 2 * n


def local_map_kernel(slots, place, d0, d1, l0, l1, u0, u1, r0, r1, out):
    n = d0.shape[0]
    rows = packed_rows(n)
    inv0, inv1 = d0[...], d1[...]
    e0 = mm(inv0, l0[...])
    e1 = mm(inv1, l1[...]).astype(BF)
    h0 = mm(inv0, u0[...]).astype(BF)
    h1 = mm(inv1, u1[...]).astype(BF)
    y0 = mm(inv0, r0[...])
    y1 = mm(inv1, r1[...])
    a = mm(e1, e0.astype(BF)).astype(BF)
    c = y1 - mm_fine(e1, y0)
    b = mm(h0, h1).astype(BF)
    g = -(e0 + mm(h0, a))
    h = y0 - mm_fine(h0, c)
    pack(out, 0, a)
    pack(out, rows, b)
    pack(out, 2 * rows, g.astype(BF))
    out[3 * rows : 3 * rows + n, :] = c.astype(BF)
    out[3 * rows + n : 3 * rows + 2 * n, :] = h.astype(BF)


def stored(slab, pencil, height, width):
    return pl.BlockSpec(
        (None, height, width), lambda i, sl, at: (sl[slab, pencil(at)], 0, 0)
    )


def constant(shape):
    return pl.BlockSpec(shape, lambda i, sl, at: (0,) * len(shape))


def element_call(kernel, in_specs, out_shape, slots, place, *operands, name, cost=SHORT):
    return pl.pallas_call(
        kernel,
        grid_spec=pltpu.PrefetchScalarGridSpec(
            num_scalar_prefetch=2,
            grid=(1,),
            in_specs=in_specs,
            out_specs=[constant(o.shape) for o in out_shape],
        ),
        out_shape=out_shape,
        compiler_params=pltpu.CompilerParams(vmem_limit_bytes=VMEM_LIMIT),
        cost_estimate=cost,
        name=name,
    )(slots, place, *operands)


def local_map(slots, place, diag_inv, lower, upper, source, distance):
    n, cols = source.shape[1:]

    def pencil(at):
        return lax.bitwise_xor(at[3], jnp.int32(distance))

    (out,) = element_call(
        local_map_kernel,
        [stored(s, pencil, n, n) for s in (0, 1, 0, 1, 0, 1)]
        + [stored(s, pencil, n, cols) for s in (0, 1)],
        [jax.ShapeDtypeStruct((map_rows(n), cols), BF)],
        slots, place, diag_inv, diag_inv, lower, lower, upper, upper, source, source,
        name="local_map",
    )
    return out


def halves(x):
    top = x.astype(BF)
    return top, (x - top.astype(F32)).astype(BF)


def prepare_kernel(slots, place, *refs):
    d0, d1, l0, l1, u0, u1, r0, r1 = refs[0:8]
    diags, minuses, pluses = refs[8:10], refs[10:12], refs[12:14]
    out, first_ops, second_ops, c_out, y_out, rows_out, lowers, sides = refs[14:]
    n = d0.shape[0]
    pencil = pl.program_id(0)
    for s in range(2):
        row = (diags[s], (l0, l1)[s], (u0, u1)[s], minuses[s], pluses[s])
        for t, block in enumerate(row):
            rows_out[s, :, t * n : (t + 1) * n] = block[...]
    lowers[...] = l0[...]

    @pl.when(pencil == 0)
    def _():
        for s in range(2):
            sides[s] = minuses[s][...]

    @pl.when(pencil == GROUP - 1)
    def _():
        for s in range(2):
            sides[s + 2] = pluses[s][...]

    rows = packed_rows(n)
    inv0, inv1 = d0[...], d1[...]
    e0 = mm(inv0, l0[...])
    e0_top, e0_rest = halves(e0)
    e1_top, e1_rest = halves(mm(inv1, l1[...]))
    h0_top, h0_rest = halves(mm(inv0, u0[...]))
    h1_top, h1_rest = halves(mm(inv1, u1[...]))
    y0 = mm(inv0, r0[...])
    a = mm(e1_top, e0_top) + (mm(e1_top, e0_rest) + mm(e1_rest, e0_top))
    c = mm(inv1, r1[...]) - (mm_fine(e1_top, y0) + mm(e1_rest, y0.astype(BF)))
    a_top, a_rest = halves(a)
    for t, part in enumerate((a_top, a_rest, -h1_top, -h1_rest)):
        first_ops[:, t * n : (t + 1) * n] = part
    for t, part in enumerate((-e0_top, -e0_rest, -h0_top, -h0_rest, -h0_top)):
        second_ops[:, t * n : (t + 1) * n] = part
    c_out[...] = c
    y_out[...] = y0

    @pl.when(pencil == place[3])
    def _():
        pack(out, 0, a_top)
        pack(out, rows, mm(h0_top, h1_top).astype(BF))
        pack(out, 2 * rows, (-(e0 + mm(h0_top, a_top))).astype(BF))
        out[3 * rows : 3 * rows + n, :] = c.astype(BF)
        out[3 * rows + n : 3 * rows + 2 * n, :] = (y0 - mm_fine(h0_top, c)).astype(BF)


def prepare(slots, place, diag_inv, lower, upper, source, diagonal, minus, plus):
    n, cols = source.shape[1:]

    def block(slab, width):
        return pl.BlockSpec((None, n, width), lambda p, sl, at: (sl[slab, p], 0, 0))

    def per(width):
        return pl.BlockSpec((None, n, width), lambda p, sl, at: (p, 0, 0))

    shape = jax.ShapeDtypeStruct
    return pl.pallas_call(
        prepare_kernel,
        grid_spec=pltpu.PrefetchScalarGridSpec(
            num_scalar_prefetch=2,
            grid=(GROUP,),
            in_specs=[block(s, n) for s in (0, 1) * 3]
            + [block(s, cols) for s in (0, 1)]
            + [block(s, n) for s in (0, 1) * 3],
            out_specs=[
                pl.BlockSpec((map_rows(n), cols), lambda p, sl, at: (0, 0)),
                per(4 * n), per(5 * n), per(cols), per(cols),
                pl.BlockSpec((None, 2, n, 5 * n), lambda p, sl, at: (p, 0, 0, 0)),
                per(n),
                pl.BlockSpec((4, n, n), lambda p, sl, at: (0, 0, 0)),
            ],
        ),
        out_shape=[
            shape((map_rows(n), cols), BF),
            shape((GROUP, n, 4 * n), BF),
            shape((GROUP, n, 5 * n), BF),
            shape((GROUP, n, cols), F32),
            shape((GROUP, n, cols), F32),
            shape((GROUP, 2, n, 5 * n), BF),
            shape((GROUP, n, n), BF),
            shape((4, n, n), BF),
        ],
        compiler_params=pltpu.CompilerParams(vmem_limit_bytes=VMEM_LIMIT),
        cost_estimate=SHORT,
        name="prepare",
    )(
        slots, place, diag_inv, diag_inv, lower, lower, upper, upper, source, source,
        diagonal, diagonal, minus, minus, plus, plus,
    )


def per_owner(place, pieces, body):
    for owned in range(GROUP):

        @pl.when(place[3] == owned)
        def _(owned=owned):
            body([pieces[owned ^ j] for j in range(GROUP)])


def segment(one, n):
    rows = packed_rows(n)
    return (
        unpack(one, 0, n),
        unpack(one, rows, n),
        unpack(one, 2 * rows, n),
        one[3 * rows : 3 * rows + n, :].astype(F32),
        one[3 * rows + n : 3 * rows + 2 * n, :].astype(F32),
    )


def group_back_kernel(
    place, across, near, next_one, own, a_low, b_low, c_low, g_out, h_out, send_far
):
    n = a_low.shape[0]

    def body(maps):
        (a0, b0, g0, c0, h0), (a1, b1, g1, c1, h1), (a2, b2, g2, c2, h2), (_, _, g3, _, h3) = (
            segment(one, n) for one in maps
        )
        a = mm(a1, a0).astype(BF)
        b = mm(b0, b1).astype(BF)
        c = mm_fine(a1, c0) + c1
        low_g = mm(b0, mm(g1, a0).astype(BF)) + g0.astype(F32)
        high_g = (mm(b2, mm(g3, a2).astype(BF)) + g2.astype(F32)).astype(BF)
        g = (mm(b, mm(high_g, a).astype(BF)) + low_g).astype(BF)
        low_h = mm_fine(b0, mm_fine(g1, c0) + h1) + h0
        high_h = mm_fine(b2, mm_fine(g3, c2) + h3) + h2
        h = mm_fine(b, mm_fine(high_g, c) + high_h) + low_h
        a_low[...] = a
        b_low[...] = b
        c_low[...] = c
        g_out[...] = g
        h_out[...] = h
        send_far[0:n, :] = h.astype(BF)
        pack(send_far, n, g)

    per_owner(place, (own, near, next_one, across), body)


def group_front_kernel(
    place, across, near, next_one, own, a_low, b_low, c_low, send, a_out, b_out, c_out
):
    n = a_low.shape[0]

    def body(maps):
        (a2, b2, _, c2, _), (a3, b3, _, c3, _) = (segment(one, n) for one in maps[2:])
        a = mm(a3, a2).astype(BF)
        c = mm_fine(a, c_low[...]) + (mm_fine(a3, c2) + c3)
        send[...] = c.astype(BF)
        c_out[...] = c
        a_out[...] = mm(a, a_low[...]).astype(BF)
        b_out[...] = mm(b_low[...], mm(b2, b3).astype(BF)).astype(BF)

    per_owner(place, (own, near, next_one, across), body)


def forward_one_kernel(incoming, a, c, send):
    send[...] = (mm(a[...], incoming[...]) + c[...]).astype(BF)


def turn_kernel(incoming, far, a, b, g, c, h, send, front_out, back_in):
    n = a.shape[0]
    front = incoming[...]
    ahead = mm(a[...], front) + c[...]
    back = mm_fine(unpack(far, n, n), ahead) + far[0:n, :].astype(F32)
    send[...] = (mm_fine(b[...], back) + (mm(g[...], front) + h[...])).astype(BF)
    front_out[...] = ahead.astype(BF)
    back_in[...] = back.astype(BF)


def backward_one_kernel(place, b, g, h, hop1, incoming, ahead, send):
    back = mm(b[...], incoming[...]) + (mm(g[...], hop1[...]) + h[...])
    send[...] = jnp.where(place[4] == 1, back.astype(BF), ahead[...])


def interfaces_kernel(place, across, near, next_one, own, hop1, hop2, hop3, back2, hop4, out):
    n = hop2.shape[0]
    rows = packed_rows(n)
    which = place[4]
    zero = jnp.zeros_like(hop2[...])
    first = jnp.where(
        which == 0, zero,
        jnp.where(which == 1, hop1[...], jnp.where(which == 2, hop2[...], hop4[...])),
    ).astype(F32)
    last = jnp.where(
        which == 0, hop4[...],
        jnp.where(which == 1, hop3[...], jnp.where(which == 2, back2[...], zero)),
    ).astype(F32)

    def body(maps):
        fronts, back = [first], last
        for one in maps[:-1]:
            shift = one[3 * rows : 3 * rows + n, :].astype(F32)
            fronts.append(mm_fine(unpack(one, 0, n), fronts[-1]) + shift)
        for j in reversed(range(GROUP)):
            out[j, 0:n, :] = fronts[j].astype(BF)
            out[j, n : 2 * n, :] = back.astype(BF)
            if j:
                shift = maps[j][3 * rows + n : 3 * rows + 2 * n, :].astype(F32)
                inner = mm_fine(unpack(maps[j], 2 * rows, n), fronts[j]) + shift
                back = mm_fine(unpack(maps[j], rows, n), back) + inner

    per_owner(place, (own, near, next_one, across), body)


def whole_call(kernel, outs, scalars, *operands, name, cost=SHORT):
    specs = [pl.BlockSpec(memory_space=pltpu.SMEM)] * len(scalars)
    specs += [pl.BlockSpec(memory_space=pltpu.VMEM)] * len(operands)
    return pl.pallas_call(
        kernel,
        in_specs=specs,
        out_specs=[pl.BlockSpec(memory_space=pltpu.VMEM)] * len(outs),
        out_shape=[jax.ShapeDtypeStruct(s, d) for s, d in outs],
        compiler_params=pltpu.CompilerParams(vmem_limit_bytes=VMEM_LIMIT),
        cost_estimate=cost,
        name=name,
    )(*scalars, *operands)


def finish_second_kernel(ends, first_ops, c, tops, rests):
    n = c.shape[1]
    for p in range(GROUP):
        front = ends[p, 0:n, :]
        back = ends[p, n : 2 * n, :]
        x1 = c[p] + mm(first_ops[p], jnp.concatenate([front, front, back, back], axis=0))
        tops[p], rests[p] = halves(x1)


def finish_first_kernel(place, ends, second_ops, y0, tops, rests, beside, firsts):
    n = y0.shape[1]
    for p in range(GROUP):
        front = ends[p, 0:n, :]
        top = tops[p]
        around = jnp.concatenate([front, front, top, top, rests[p]], axis=0)
        firsts[p] = (y0[p] + mm(second_ops[p], around)).astype(BF)
    even = lax.rem(place[1], 2) == 0
    for s, values in enumerate((firsts, tops)):
        beside[s] = jnp.where(even, values[0], values[GROUP - 1])


def row_products(chosen, rows, firsts, tops, ends, partial):
    n = tops.shape[1]
    zero = jnp.zeros(tops.shape[1:], BF)

    def value(s, p):
        if p < 0 or p >= GROUP or s < 0:
            return zero
        return ends[p, n : 2 * n, :] if s == 2 else (firsts, tops)[s][p]

    for i, p in enumerate(chosen):
        for s in range(2):
            around = [value(s, p), value(s - 1, p), value(s + 1, p), value(s, p - 1), value(s, p + 1)]
            partial[i, s] = mm(rows[p, s], jnp.concatenate(around, axis=0))


def first_rows_kernel(place, rows, firsts, tops, ends, within, partial):
    even = lax.rem(place[1], 2) == 0
    row_products((0, 1), rows, firsts, tops, ends, partial)
    for s, values in enumerate((firsts, tops)):
        within[s] = jnp.where(even, values[GROUP - 1], values[0])


def second_rows_kernel(slots, rows, firsts, tops, ends, precond, partial):
    row_products((2, 3), rows, firsts, tops, ends, partial)
    for s in range(2):
        for p in range(GROUP):
            precond[slots[s, p]] = (firsts, tops)[s][p]


def edge_jacobian_kernel(slots, place, beside, below, within, partial_a, partial_b, lowers, sides, jac):
    even = lax.rem(place[1], 2) == 0
    low = [jnp.where(even, beside[s], within[s]) for s in range(2)]
    high = [jnp.where(even, within[s], beside[s]) for s in range(2)]
    left = jnp.where(place[1] == 0, 0.0, 1.0).astype(F32)
    right = jnp.where(place[1] == place[2] - 1, 0.0, 1.0).astype(F32)
    start = jnp.where(place[0] == 0, 0.0, 1.0).astype(F32)
    for s in range(2):
        for p in range(GROUP):
            total = partial_a[p, s] if p < 2 else partial_b[p - 2, s]
            if s == 0:
                total = total + start * mm(lowers[p], below[p])
            if p == 0:
                total = total + left * mm(sides[s], low[s])
            if p == GROUP - 1:
                total = total + right * mm(sides[s + 2], high[s])
            jac[slots[s, p]] = total.astype(BF)


def local(right_side, diag_inv, diag_blk, lower_blk, upper_blk, cross_minus, cross_plus, elem_slot):
    n, cols = right_side.shape[2:]
    source, inverse, diagonal, lower, upper, minus, plus = (
        pltpu.with_memory_space_constraint(
            values.reshape((-1,) + values.shape[2:]), pltpu.HBM
        )
        for values in (
            right_side, diag_inv, diag_blk, lower_blk, upper_blk, cross_minus, cross_plus
        )
    )
    count = lax.axis_size("sweep")
    across = lax.axis_size("cross")
    sweep_at = lax.axis_index("sweep")
    place = jnp.stack(
        [
            sweep_at, lax.axis_index("cross"), jnp.int32(across),
            lax.rem(sweep_at, GROUP), lax.div(sweep_at, GROUP),
        ]
    ).astype(jnp.int32)
    groups = [list(range(g, g + GROUP)) for g in range(0, count, GROUP)]

    def hop(values, *moves):
        pairs = [(a * GROUP + k, b * GROUP + k) for a, b in moves for k in range(GROUP)]
        return lax.ppermute(values, "sweep", pairs)

    def to_peer(values, distance):
        return lax.ppermute(values, "sweep", [(i, i ^ distance) for i in range(count)])

    vec, vec32, mat = ((n, cols), BF), ((n, cols), F32), ((n, n), BF)
    maps = [None] * GROUP
    for distance in (3, 1, 2):
        piece = local_map(elem_slot, place, inverse, lower, upper, source, distance)
        maps[distance] = to_peer(piece, distance)
    maps[0], first_ops, second_ops, c_own, y_own, rows, lowers, sides = prepare(
        elem_slot, place, inverse, lower, upper, source, diagonal, minus, plus
    )
    pieces = (maps[3], maps[1], maps[2], maps[0])

    a_low, b_low, c_low, g, h, send_far = whole_call(
        group_back_kernel, [mat, mat, vec32, mat, vec32, ((n + packed_rows(n), cols), BF)],
        [place], *pieces, name="group_back",
    )
    far = hop(send_far, (3, 2))
    send, a, b, c = whole_call(
        group_front_kernel, [vec, mat, mat, vec32], [place],
        *pieces, a_low, b_low, c_low, name="group_front",
    )
    hop1 = hop(send, (0, 1))
    (send,) = whole_call(forward_one_kernel, [vec], [], hop1, a, c, name="forward_one")
    hop2 = hop(send, (1, 2))
    send, ahead, back2 = whole_call(
        turn_kernel, [vec, vec, vec], [], hop2, far, a, b, g, c, h, name="turn"
    )
    hop3 = hop(send, (2, 1))
    (send,) = whole_call(
        backward_one_kernel, [vec], [place], b, g, h, hop1, hop3, ahead, name="backward_one"
    )
    hop4 = hop(send, (1, 0), (2, 3))
    (ends,) = whole_call(
        interfaces_kernel, [((GROUP, 2 * n, cols), BF)], [place],
        *pieces, hop1, hop2, hop3, back2, hop4, name="interfaces",
    )
    ends = lax.all_to_all(ends, "sweep", 0, 0, axis_index_groups=groups)

    pair = ((2, n, cols), BF)
    four = ((GROUP, n, cols), BF)
    tops, rests = whole_call(
        finish_second_kernel, [four, four], [], ends, first_ops, c_own, name="finish_second"
    )
    below = lax.ppermute(tops, "sweep", [(i, (i + 1) % count) for i in range(count)])
    beside, firsts = whole_call(
        finish_first_kernel, [pair, four], [place],
        ends, second_ops, y_own, tops, rests, name="finish_first",
    )
    aside = []
    for i in range(1, across - 1, 2):
        aside += [(i, i + 1), (i + 1, i)]
    beside = lax.ppermute(beside, "cross", aside)
    part = ((2, 2, n, cols), F32)
    within, partial_a = whole_call(
        first_rows_kernel, [pair, part], [place], rows, firsts, tops, ends, name="first_rows"
    )
    within = lax.ppermute(within, "cross", [(i, i ^ 1) for i in range(across)])
    every = ((2 * GROUP, n, cols), BF)
    precond, partial_b = whole_call(
        second_rows_kernel, [every, part], [elem_slot], rows, firsts, tops, ends, name="second_rows"
    )
    (jac,) = whole_call(
        edge_jacobian_kernel, [every], [elem_slot, place],
        beside, below, within, partial_a, partial_b, lowers, sides, name="edge_jacobian",
    )
    return precond.reshape(right_side.shape), jac.reshape(right_side.shape)


def solution(mesh):
    blocks = P("sweep", "cross", None, None)
    in_specs = (blocks,) * 7 + (P("sweep", "cross"),)
    return jax.shard_map(
        local, mesh=mesh, in_specs=in_specs, out_specs=(blocks, blocks), check_vma=False
    )
```

```python
import functools

import jax
import jax.numpy as jnp
from jax import lax
from jax.experimental import pallas as pl
from jax.experimental.pallas import tpu as pltpu
from jax.sharding import PartitionSpec as P

BF = jnp.bfloat16
F32 = jnp.float32
GROUP = 4
VMEM_LIMIT = 28 << 20
LONG = pl.CostEstimate(flops=10**10, transcendentals=0, bytes_accessed=1024)
SHORT = pl.CostEstimate(flops=1024, transcendentals=0, bytes_accessed=1024)


def mm(a, b):
    return jnp.dot(a, b, preferred_element_type=F32)


def mm_fine(a, x):
    width = x.shape[1]
    top = x.astype(BF)
    rest = (x - top.astype(F32)).astype(BF)
    both = mm(a, jnp.concatenate([top, rest], axis=1))
    return both[:, :width] + both[:, width:]


def packed_rows(n):
    return 2 * n + n // 2


def pack(ref, base, mat):
    n = mat.shape[0]
    half = n // 2
    ref[base : base + n, :] = mat[:, 0:128]
    ref[base + n : base + 2 * n, :] = mat[:, 128:256]
    ref[base + 2 * n : base + 2 * n + half, 0:64] = mat[0:half, 256:320]
    ref[base + 2 * n : base + 2 * n + half, 64:128] = mat[half:n, 256:320]


def unpack(ref, base, n):
    half = n // 2
    tail = ref[base + 2 * n : base + 2 * n + half, :]
    last = jnp.concatenate([tail[:, 0:64], tail[:, 64:128]], axis=0)
    return jnp.concatenate(
        [ref[base : base + n, :], ref[base + n : base + 2 * n, :], last], axis=1
    )


def map_rows(n):
    return 3 * packed_rows(n) + 2 * n


def local_map_kernel(slots, place, d0, d1, l0, l1, u0, u1, r0, r1, out):
    n = d0.shape[0]
    rows = packed_rows(n)
    inv0, inv1 = d0[...], d1[...]
    e0 = mm(inv0, l0[...])
    e1 = mm(inv1, l1[...]).astype(BF)
    h0 = mm(inv0, u0[...]).astype(BF)
    h1 = mm(inv1, u1[...]).astype(BF)
    y0 = mm(inv0, r0[...])
    y1 = mm(inv1, r1[...])
    a = mm(e1, e0.astype(BF)).astype(BF)
    c = y1 - mm_fine(e1, y0)
    b = mm(h0, h1).astype(BF)
    g = -(e0 + mm(h0, a))
    h = y0 - mm_fine(h0, c)
    pack(out, 0, a)
    pack(out, rows, b)
    pack(out, 2 * rows, g.astype(BF))
    out[3 * rows : 3 * rows + n, :] = c.astype(BF)
    out[3 * rows + n : 3 * rows + 2 * n, :] = h.astype(BF)


def stored(slab, pencil, height, width):
    return pl.BlockSpec(
        (None, height, width), lambda i, sl, at: (sl[slab, pencil(at)], 0, 0)
    )


def constant(shape):
    return pl.BlockSpec(shape, lambda i, sl, at: (0,) * len(shape))


def element_call(kernel, in_specs, out_shape, slots, place, *operands, name, cost=SHORT):
    return pl.pallas_call(
        kernel,
        grid_spec=pltpu.PrefetchScalarGridSpec(
            num_scalar_prefetch=2,
            grid=(1,),
            in_specs=in_specs,
            out_specs=[constant(o.shape) for o in out_shape],
        ),
        out_shape=out_shape,
        compiler_params=pltpu.CompilerParams(vmem_limit_bytes=VMEM_LIMIT),
        cost_estimate=cost,
        name=name,
    )(slots, place, *operands)


def local_map(slots, place, diag_inv, lower, upper, source, distance):
    n, cols = source.shape[1:]

    def pencil(at):
        return lax.bitwise_xor(at[3], jnp.int32(distance))

    (out,) = element_call(
        local_map_kernel,
        [stored(s, pencil, n, n) for s in (0, 1, 0, 1, 0, 1)]
        + [stored(s, pencil, n, cols) for s in (0, 1)],
        [jax.ShapeDtypeStruct((map_rows(n), cols), BF)],
        slots, place, diag_inv, diag_inv, lower, lower, upper, upper, source, source,
        name="local_map",
    )
    return out


def halves(x):
    top = x.astype(BF)
    return top, (x - top.astype(F32)).astype(BF)


def prepare_kernel(slots, place, *refs):
    d0, d1, l0, l1, u0, u1, r0, r1 = refs[0:8]
    diags, minuses, pluses = refs[8:10], refs[10:12], refs[12:14]
    out, first_ops, second_ops, c_out, y_out, rows_out, lowers, sides = refs[14:]
    n = d0.shape[0]
    pencil = pl.program_id(0)
    for s in range(2):
        row = (diags[s], (l0, l1)[s], (u0, u1)[s], minuses[s], pluses[s])
        for t, block in enumerate(row):
            rows_out[s, :, t * n : (t + 1) * n] = block[...]
    lowers[...] = l0[...]

    @pl.when(pencil == 0)
    def _():
        for s in range(2):
            sides[s] = minuses[s][...]

    @pl.when(pencil == GROUP - 1)
    def _():
        for s in range(2):
            sides[s + 2] = pluses[s][...]

    rows = packed_rows(n)
    inv0, inv1 = d0[...], d1[...]
    e0 = mm(inv0, l0[...])
    e0_top, e0_rest = halves(e0)
    e1_top, e1_rest = halves(mm(inv1, l1[...]))
    h0_top, h0_rest = halves(mm(inv0, u0[...]))
    h1_top, h1_rest = halves(mm(inv1, u1[...]))
    y0 = mm(inv0, r0[...])
    a = mm(e1_top, e0_top) + (mm(e1_top, e0_rest) + mm(e1_rest, e0_top))
    c = mm(inv1, r1[...]) - (mm_fine(e1_top, y0) + mm(e1_rest, y0.astype(BF)))
    a_top, a_rest = halves(a)
    for t, part in enumerate((a_top, a_rest, -h1_top, -h1_rest)):
        first_ops[:, t * n : (t + 1) * n] = part
    for t, part in enumerate((-e0_top, -e0_rest, -h0_top, -h0_rest, -h0_top)):
        second_ops[:, t * n : (t + 1) * n] = part
    c_out[...] = c
    y_out[...] = y0

    @pl.when(pencil == place[3])
    def _():
        pack(out, 0, a_top)
        pack(out, rows, mm(h0_top, h1_top).astype(BF))
        pack(out, 2 * rows, (-(e0 + mm(h0_top, a_top))).astype(BF))
        out[3 * rows : 3 * rows + n, :] = c.astype(BF)
        out[3 * rows + n : 3 * rows + 2 * n, :] = (y0 - mm_fine(h0_top, c)).astype(BF)


def prepare(slots, place, diag_inv, lower, upper, source, diagonal, minus, plus):
    n, cols = source.shape[1:]

    def block(slab, width):
        return pl.BlockSpec((None, n, width), lambda p, sl, at: (sl[slab, p], 0, 0))

    def per(width):
        return pl.BlockSpec((None, n, width), lambda p, sl, at: (p, 0, 0))

    shape = jax.ShapeDtypeStruct
    return pl.pallas_call(
        prepare_kernel,
        grid_spec=pltpu.PrefetchScalarGridSpec(
            num_scalar_prefetch=2,
            grid=(GROUP,),
            in_specs=[block(s, n) for s in (0, 1) * 3]
            + [block(s, cols) for s in (0, 1)]
            + [block(s, n) for s in (0, 1) * 3],
            out_specs=[
                pl.BlockSpec((map_rows(n), cols), lambda p, sl, at: (0, 0)),
                per(4 * n), per(5 * n), per(cols), per(cols),
                pl.BlockSpec((None, 2, n, 5 * n), lambda p, sl, at: (p, 0, 0, 0)),
                per(n),
                pl.BlockSpec((4, n, n), lambda p, sl, at: (0, 0, 0)),
            ],
        ),
        out_shape=[
            shape((map_rows(n), cols), BF),
            shape((GROUP, n, 4 * n), BF),
            shape((GROUP, n, 5 * n), BF),
            shape((GROUP, n, cols), F32),
            shape((GROUP, n, cols), F32),
            shape((GROUP, 2, n, 5 * n), BF),
            shape((GROUP, n, n), BF),
            shape((4, n, n), BF),
        ],
        compiler_params=pltpu.CompilerParams(vmem_limit_bytes=VMEM_LIMIT),
        cost_estimate=SHORT,
        name="prepare",
    )(
        slots, place, diag_inv, diag_inv, lower, lower, upper, upper, source, source,
        diagonal, diagonal, minus, minus, plus, plus,
    )


def per_owner(place, pieces, body):
    for owned in range(GROUP):

        @pl.when(place[3] == owned)
        def _(owned=owned):
            body([pieces[owned ^ j] for j in range(GROUP)], owned)


def segment(one, n):
    rows = packed_rows(n)
    return (
        unpack(one, 0, n),
        unpack(one, rows, n),
        unpack(one, 2 * rows, n),
        one[3 * rows : 3 * rows + n, :].astype(F32),
        one[3 * rows + n : 3 * rows + 2 * n, :].astype(F32),
    )


def group_back_kernel(
    place, across, near, next_one, own, a_low, b_low, c_low, g_out, h_out, send_far
):
    n = a_low.shape[0]

    def body(maps, owned):
        (a0, b0, g0, c0, h0), (a1, b1, g1, c1, h1), (a2, b2, g2, c2, h2), (_, b3, g3, _, h3) = (
            segment(one, n) for one in maps
        )
        a = mm(a1, a0).astype(BF)
        b = mm(b0, b1).astype(BF)
        c = mm_fine(a1, c0) + c1
        low_g = mm(b0, mm(g1, a0).astype(BF)) + g0.astype(F32)
        high_g = (mm(b2, mm(g3, a2).astype(BF)) + g2.astype(F32)).astype(BF)
        g = (mm(b, mm(high_g, a).astype(BF)) + low_g).astype(BF)
        low_h = mm_fine(b0, mm_fine(g1, c0) + h1) + h0
        high_h = mm_fine(b2, mm_fine(g3, c2) + h3) + h2
        h = mm_fine(b, mm_fine(high_g, c) + high_h) + low_h
        a_low[...] = a
        b_low[...] = b
        c_low[...] = c
        g_out[...] = g
        h_out[...] = h
        send_far[0:n, :] = h.astype(BF)

        @pl.when(place[4] == 1)
        def _():
            pack(send_far, n, mm(b, mm(b2, b3).astype(BF)).astype(BF))

        @pl.when(place[4] != 1)
        def _():
            pack(send_far, n, g)

    per_owner(place, (own, near, next_one, across), body)


def group_front_kernel(
    place, across, near, next_one, own, a_low, b_low, c_low, send, a_out, b_out, c_out
):
    n = a_low.shape[0]

    def body(maps, owned):
        (a2, b2, _, c2, _), (a3, b3, _, c3, _) = (segment(one, n) for one in maps[2:])
        a = mm(a3, a2).astype(BF)
        c = mm_fine(a, c_low[...]) + (mm_fine(a3, c2) + c3)
        send[...] = c.astype(BF)
        c_out[...] = c
        a_out[...] = mm(a, a_low[...]).astype(BF)
        b_out[...] = mm(b_low[...], mm(b2, b3).astype(BF)).astype(BF)

    per_owner(place, (own, near, next_one, across), body)


def forward_one_kernel(incoming, a, c, g, h, send, inner):
    send[...] = (mm(a[...], incoming[...]) + c[...]).astype(BF)
    inner[...] = (mm(g[...], incoming[...]) + h[...]).astype(BF)


def turn_kernel(incoming, far, a, b, g, c, h, send, back_in):
    n = a.shape[0]
    front = incoming[...]
    ahead = mm(a[...], front) + c[...]
    back = mm_fine(unpack(far, n, n), ahead) + far[0:n, :].astype(F32)
    send[...] = (mm_fine(b[...], back) + (mm(g[...], front) + h[...])).astype(BF)
    back_in[...] = back.astype(BF)


def through_group(maps, first, n):
    rows = packed_rows(n)
    fronts, inner = [first], [None]
    for one in maps[:-1]:
        shift = one[3 * rows : 3 * rows + n, :].astype(F32)
        fronts.append(mm_fine(unpack(one, 0, n), fronts[-1]) + shift)
    for one, front in zip(maps[1:], fronts[1:]):
        shift = one[3 * rows + n : 3 * rows + 2 * n, :].astype(F32)
        inner.append(mm_fine(unpack(one, 2 * rows, n), front) + shift)
    return fronts, inner


def entering_kernel(place, across, near, next_one, own, hop1, hop2, fronts_out, inner_out, leaving):
    n = hop1.shape[0]
    rows = packed_rows(n)
    which = place[4]
    zero = jnp.zeros_like(hop1[...])
    first = jnp.where(which == 1, hop1[...], jnp.where(which == 2, hop2[...], zero)).astype(F32)

    def body(maps, owned):
        fronts, inner = through_group(maps, first, n)
        for j in range(GROUP):
            fronts_out[j] = fronts[j].astype(BF)
            if j:
                inner_out[j] = inner[j]
        shift = maps[-1][3 * rows : 3 * rows + n, :].astype(F32)
        leaving[...] = (mm_fine(unpack(maps[-1], 0, n), fronts[-1]) + shift).astype(BF)

    per_owner(place, (own, near, next_one, across), body)


def interfaces_kernel(
    place, across, near, next_one, own, far, inner_one, hop_three, hop_one, back_two, hop_zero,
    fronts_in, inner_in, out_near, out_next, out_across, out_own, inner_now,
):
    n = hop_one.shape[0]
    rows = packed_rows(n)
    which = place[4]
    outs = (out_own, out_near, out_next, out_across)
    zero = jnp.zeros_like(hop_one[...])
    through_one = mm(unpack(far, n, n), hop_zero[...]) + inner_one[...].astype(F32)
    last = jnp.where(
        which == 0, through_one.astype(BF),
        jnp.where(which == 1, hop_one[...], jnp.where(which == 2, back_two[...], zero)),
    ).astype(F32)

    def body(maps, owned):
        @pl.when(which == GROUP - 1)
        def _():
            fronts, inner = through_group(maps, hop_three[...].astype(F32), n)
            for j in range(GROUP):
                outs[owned ^ j][0:n, :] = fronts[j].astype(BF)
                if j:
                    inner_now[j] = inner[j]

        @pl.when(which != GROUP - 1)
        def _():
            for j in range(GROUP):
                outs[owned ^ j][0:n, :] = fronts_in[j]
                if j:
                    inner_now[j] = inner_in[j]

        back = last
        for j in reversed(range(GROUP)):
            outs[owned ^ j][n : 2 * n, :] = back.astype(BF)
            if j:
                back = mm_fine(unpack(maps[j], rows, n), back) + inner_now[j]

    per_owner(place, (own, near, next_one, across), body)


def whole_call(kernel, outs, scalars, *operands, name, cost=SHORT, scratch=()):
    specs = [pl.BlockSpec(memory_space=pltpu.SMEM)] * len(scalars)
    specs += [pl.BlockSpec(memory_space=pltpu.VMEM)] * len(operands)
    return pl.pallas_call(
        kernel,
        in_specs=specs,
        out_specs=[pl.BlockSpec(memory_space=pltpu.VMEM)] * len(outs),
        out_shape=[jax.ShapeDtypeStruct(s, d) for s, d in outs],
        scratch_shapes=scratch,
        compiler_params=pltpu.CompilerParams(vmem_limit_bytes=VMEM_LIMIT),
        cost_estimate=cost,
        name=name,
    )(*scalars, *operands)


def finish_second_kernel(
    place, near, next_one, across, own, first_ops, c, tops, rests, fronts, backs
):
    n = c.shape[1]

    def body(ends, owned):
        for p in range(GROUP):
            front = ends[p][0:n, :]
            back = ends[p][n : 2 * n, :]
            x1 = c[p] + mm(first_ops[p], jnp.concatenate([front, front, back, back], axis=0))
            tops[p], rests[p] = halves(x1)
            fronts[p] = front
            backs[p] = back

    per_owner(place, (own, near, next_one, across), body)


def finish_first_kernel(place, fronts, second_ops, y0, tops, rests, beside, firsts):
    n = y0.shape[1]
    for p in range(GROUP):
        front = fronts[p]
        top = tops[p]
        around = jnp.concatenate([front, front, top, top, rests[p]], axis=0)
        firsts[p] = (y0[p] + mm(second_ops[p], around)).astype(BF)
    even = lax.rem(place[1], 2) == 0
    for s, values in enumerate((firsts, tops)):
        beside[s] = jnp.where(even, values[0], values[GROUP - 1])


def row_products(chosen, rows, firsts, tops, backs, partial):
    n = tops.shape[1]
    zero = jnp.zeros(tops.shape[1:], BF)

    def value(s, p):
        if p < 0 or p >= GROUP or s < 0:
            return zero
        return backs[p] if s == 2 else (firsts, tops)[s][p]

    for i, p in enumerate(chosen):
        for s in range(2):
            around = [value(s, p), value(s - 1, p), value(s + 1, p), value(s, p - 1), value(s, p + 1)]
            partial[i, s] = mm(rows[p, s], jnp.concatenate(around, axis=0))


def first_rows_kernel(place, rows, firsts, tops, backs, within, partial):
    even = lax.rem(place[1], 2) == 0
    row_products((0, 1), rows, firsts, tops, backs, partial)
    for s, values in enumerate((firsts, tops)):
        within[s] = jnp.where(even, values[GROUP - 1], values[0])


def second_rows_kernel(slots, rows, firsts, tops, backs, precond, partial):
    row_products((2, 3), rows, firsts, tops, backs, partial)
    for s in range(2):
        for p in range(GROUP):
            precond[slots[s, p]] = (firsts, tops)[s][p]


def edge_jacobian_kernel(slots, place, beside, below, within, partial_a, partial_b, lowers, sides, jac):
    even = lax.rem(place[1], 2) == 0
    low = [jnp.where(even, beside[s], within[s]) for s in range(2)]
    high = [jnp.where(even, within[s], beside[s]) for s in range(2)]
    left = jnp.where(place[1] == 0, 0.0, 1.0).astype(F32)
    right = jnp.where(place[1] == place[2] - 1, 0.0, 1.0).astype(F32)
    start = jnp.where(place[0] == 0, 0.0, 1.0).astype(F32)
    for s in range(2):
        for p in range(GROUP):
            total = partial_a[p, s] if p < 2 else partial_b[p - 2, s]
            if s == 0:
                total = total + start * mm(lowers[p], below[p])
            if p == 0:
                total = total + left * mm(sides[s], low[s])
            if p == GROUP - 1:
                total = total + right * mm(sides[s + 2], high[s])
            jac[slots[s, p]] = total.astype(BF)


def local(right_side, diag_inv, diag_blk, lower_blk, upper_blk, cross_minus, cross_plus, elem_slot):
    n, cols = right_side.shape[2:]
    source, inverse, diagonal, lower, upper, minus, plus = (
        pltpu.with_memory_space_constraint(
            values.reshape((-1,) + values.shape[2:]), pltpu.HBM
        )
        for values in (
            right_side, diag_inv, diag_blk, lower_blk, upper_blk, cross_minus, cross_plus
        )
    )
    count = lax.axis_size("sweep")
    across = lax.axis_size("cross")
    sweep_at = lax.axis_index("sweep")
    place = jnp.stack(
        [
            sweep_at, lax.axis_index("cross"), jnp.int32(across),
            lax.rem(sweep_at, GROUP), lax.div(sweep_at, GROUP),
        ]
    ).astype(jnp.int32)
    def hop(values, *moves):
        pairs = [(a * GROUP + k, b * GROUP + k) for a, b in moves for k in range(GROUP)]
        return lax.ppermute(values, "sweep", pairs)

    def to_peer(values, distance):
        return lax.ppermute(values, "sweep", [(i, i ^ distance) for i in range(count)])

    vec, vec32, mat = ((n, cols), BF), ((n, cols), F32), ((n, n), BF)
    maps = [None] * GROUP
    for distance in (3, 1, 2):
        piece = local_map(elem_slot, place, inverse, lower, upper, source, distance)
        maps[distance] = to_peer(piece, distance)
    maps[0], first_ops, second_ops, c_own, y_own, rows, lowers, sides = prepare(
        elem_slot, place, inverse, lower, upper, source, diagonal, minus, plus
    )
    pieces = (maps[3], maps[1], maps[2], maps[0])

    a_low, b_low, c_low, g, h, send_far = whole_call(
        group_back_kernel, [mat, mat, vec32, mat, vec32, ((n + packed_rows(n), cols), BF)],
        [place], *pieces, name="group_back",
    )
    far = hop(send_far, (3, 2), (1, 0))
    send, a, b, c = whole_call(
        group_front_kernel, [vec, mat, mat, vec32], [place],
        *pieces, a_low, b_low, c_low, name="group_front",
    )
    hop1 = hop(send, (0, 1))
    send, inner_one = whole_call(
        forward_one_kernel, [vec, vec], [], hop1, a, c, g, h, name="forward_one"
    )
    hop2 = hop(send, (1, 2))
    inner_one = hop(inner_one, (1, 0))
    send, back_two = whole_call(
        turn_kernel, [vec, vec], [], hop2, far, a, b, g, c, h, name="turn"
    )
    hop_zero = hop(send, (2, 0))
    hop_one = hop(send, (2, 1))
    fronts, inner, ahead = whole_call(
        entering_kernel, [((GROUP, n, cols), BF), ((GROUP, n, cols), F32), vec], [place],
        *pieces, hop1, hop2, name="entering",
    )
    hop_three = hop(ahead, (2, 3))
    both = ((2 * n, cols), BF)
    ends = whole_call(
        interfaces_kernel, [both] * GROUP, [place], *pieces, far, inner_one,
        hop_three, hop_one, back_two, hop_zero, fronts, inner, name="interfaces",
        scratch=[pltpu.VMEM((GROUP, n, cols), F32)],
    )
    ends = [to_peer(values, distance) for distance, values in zip((1, 2, 3), ends)] + [ends[3]]

    pair = ((2, n, cols), BF)
    four = ((GROUP, n, cols), BF)
    tops, rests, fronts, backs = whole_call(
        finish_second_kernel, [four] * 4, [place], *ends, first_ops, c_own, name="finish_second"
    )
    below = lax.ppermute(tops, "sweep", [(i, (i + 1) % count) for i in range(count)])
    beside, firsts = whole_call(
        finish_first_kernel, [pair, four], [place],
        fronts, second_ops, y_own, tops, rests, name="finish_first",
    )
    aside = []
    for i in range(1, across - 1, 2):
        aside += [(i, i + 1), (i + 1, i)]
    beside = lax.ppermute(beside, "cross", aside)
    part = ((2, 2, n, cols), F32)
    within, partial_a = whole_call(
        first_rows_kernel, [pair, part], [place], rows, firsts, tops, backs, name="first_rows"
    )
    within = lax.ppermute(within, "cross", [(i, i ^ 1) for i in range(across)])
    every = ((2 * GROUP, n, cols), BF)
    precond, partial_b = whole_call(
        second_rows_kernel, [every, part], [elem_slot], rows, firsts, tops, backs, name="second_rows"
    )
    (jac,) = whole_call(
        edge_jacobian_kernel, [every], [elem_slot, place],
        beside, below, within, partial_a, partial_b, lowers, sides, name="edge_jacobian",
    )
    return precond.reshape(right_side.shape), jac.reshape(right_side.shape)


def solution(mesh):
    blocks = P("sweep", "cross", None, None)
    in_specs = (blocks,) * 7 + (P("sweep", "cross"),)
    return jax.shard_map(
        local, mesh=mesh, in_specs=in_specs, out_specs=(blocks, blocks), check_vma=False
    )
```

```python
import functools

import jax
import jax.numpy as jnp
from jax import lax
from jax.experimental import pallas as pl
from jax.experimental.pallas import tpu as pltpu
from jax.sharding import PartitionSpec as P

BF = jnp.bfloat16
F32 = jnp.float32
GROUP = 4
VMEM_LIMIT = 28 << 20
LONG = pl.CostEstimate(flops=10**10, transcendentals=0, bytes_accessed=1024)
SHORT = pl.CostEstimate(flops=1024, transcendentals=0, bytes_accessed=1024)


def mm(a, b):
    return jnp.dot(a, b, preferred_element_type=F32)


def mm_fine(a, x):
    width = x.shape[1]
    top = x.astype(BF)
    rest = (x - top.astype(F32)).astype(BF)
    both = mm(a, jnp.concatenate([top, rest], axis=1))
    return both[:, :width] + both[:, width:]


def packed_rows(n):
    return 2 * n + n // 2


def pack(ref, base, mat):
    n = mat.shape[0]
    half = n // 2
    ref[base : base + n, :] = mat[:, 0:128]
    ref[base + n : base + 2 * n, :] = mat[:, 128:256]
    ref[base + 2 * n : base + 2 * n + half, 0:64] = mat[0:half, 256:320]
    ref[base + 2 * n : base + 2 * n + half, 64:128] = mat[half:n, 256:320]


def unpack(ref, base, n):
    half = n // 2
    tail = ref[base + 2 * n : base + 2 * n + half, :]
    last = jnp.concatenate([tail[:, 0:64], tail[:, 64:128]], axis=0)
    return jnp.concatenate(
        [ref[base : base + n, :], ref[base + n : base + 2 * n, :], last], axis=1
    )


def map_rows(n):
    return 3 * packed_rows(n) + 2 * n


def local_map_kernel(slots, place, d0, d1, l0, l1, u0, u1, r0, r1, out):
    n = d0.shape[0]
    rows = packed_rows(n)
    inv0, inv1 = d0[...], d1[...]
    e0 = mm(inv0, l0[...])
    e1 = mm(inv1, l1[...]).astype(BF)
    h0 = mm(inv0, u0[...]).astype(BF)
    h1 = mm(inv1, u1[...]).astype(BF)
    y0 = mm(inv0, r0[...])
    y1 = mm(inv1, r1[...])
    a = mm(e1, e0.astype(BF)).astype(BF)
    c = y1 - mm_fine(e1, y0)
    b = mm(h0, h1).astype(BF)
    g = -(e0 + mm(h0, a))
    h = y0 - mm_fine(h0, c)
    pack(out, 0, a)
    pack(out, rows, b)
    pack(out, 2 * rows, g.astype(BF))
    out[3 * rows : 3 * rows + n, :] = c.astype(BF)
    out[3 * rows + n : 3 * rows + 2 * n, :] = h.astype(BF)


def stored(slab, pencil, height, width):
    return pl.BlockSpec(
        (None, height, width), lambda i, sl, at: (sl[slab, pencil(at)], 0, 0)
    )


def constant(shape):
    return pl.BlockSpec(shape, lambda i, sl, at: (0,) * len(shape))


def element_call(kernel, in_specs, out_shape, slots, place, *operands, name, cost=SHORT):
    return pl.pallas_call(
        kernel,
        grid_spec=pltpu.PrefetchScalarGridSpec(
            num_scalar_prefetch=2,
            grid=(1,),
            in_specs=in_specs,
            out_specs=[constant(o.shape) for o in out_shape],
        ),
        out_shape=out_shape,
        compiler_params=pltpu.CompilerParams(vmem_limit_bytes=VMEM_LIMIT),
        cost_estimate=cost,
        name=name,
    )(slots, place, *operands)


def local_map(slots, place, diag_inv, lower, upper, source, distance):
    n, cols = source.shape[1:]

    def pencil(at):
        return lax.bitwise_xor(at[3], jnp.int32(distance))

    (out,) = element_call(
        local_map_kernel,
        [stored(s, pencil, n, n) for s in (0, 1, 0, 1, 0, 1)]
        + [stored(s, pencil, n, cols) for s in (0, 1)],
        [jax.ShapeDtypeStruct((map_rows(n), cols), BF)],
        slots, place, diag_inv, diag_inv, lower, lower, upper, upper, source, source,
        name="local_map",
    )
    return out


def halves(x):
    top = x.astype(BF)
    return top, (x - top.astype(F32)).astype(BF)


def prepare_kernel(slots, place, *refs):
    d0, d1, l0, l1, u0, u1, r0, r1 = refs[0:8]
    diags, minuses, pluses = refs[8:10], refs[10:12], refs[12:14]
    out, first_ops, second_ops, c_out, y_out, rows_out, lowers, sides = refs[14:]
    n = d0.shape[0]
    pencil = pl.program_id(0)
    for s in range(2):
        row = (diags[s], (l0, l1)[s], (u0, u1)[s], minuses[s], pluses[s])
        for t, block in enumerate(row):
            rows_out[s, :, t * n : (t + 1) * n] = block[...]
    lowers[...] = l0[...]

    @pl.when(pencil == 0)
    def _():
        for s in range(2):
            sides[s] = minuses[s][...]

    @pl.when(pencil == GROUP - 1)
    def _():
        for s in range(2):
            sides[s + 2] = pluses[s][...]

    rows = packed_rows(n)
    inv0, inv1 = d0[...], d1[...]
    e0 = mm(inv0, l0[...])
    e0_top, e0_rest = halves(e0)
    e1_top, e1_rest = halves(mm(inv1, l1[...]))
    h0_top, h0_rest = halves(mm(inv0, u0[...]))
    h1_top, h1_rest = halves(mm(inv1, u1[...]))
    y0 = mm(inv0, r0[...])
    a = mm(e1_top, e0_top) + (mm(e1_top, e0_rest) + mm(e1_rest, e0_top))
    c = mm(inv1, r1[...]) - (mm_fine(e1_top, y0) + mm(e1_rest, y0.astype(BF)))
    a_top, a_rest = halves(a)
    for t, part in enumerate((a_top, a_rest, -h1_top, -h1_rest)):
        first_ops[:, t * n : (t + 1) * n] = part
    for t, part in enumerate((-e0_top, -e0_rest, -h0_top, -h0_rest, -h0_top)):
        second_ops[:, t * n : (t + 1) * n] = part
    c_out[...] = c
    y_out[...] = y0

    @pl.when(pencil == place[3])
    def _():
        pack(out, 0, a_top)
        pack(out, rows, mm(h0_top, h1_top).astype(BF))
        pack(out, 2 * rows, (-(e0 + mm(h0_top, a_top))).astype(BF))
        out[3 * rows : 3 * rows + n, :] = c.astype(BF)
        out[3 * rows + n : 3 * rows + 2 * n, :] = (y0 - mm_fine(h0_top, c)).astype(BF)


def prepare(slots, place, diag_inv, lower, upper, source, diagonal, minus, plus):
    n, cols = source.shape[1:]

    def block(slab, width):
        return pl.BlockSpec((None, n, width), lambda p, sl, at: (sl[slab, p], 0, 0))

    def per(width):
        return pl.BlockSpec((None, n, width), lambda p, sl, at: (p, 0, 0))

    shape = jax.ShapeDtypeStruct
    return pl.pallas_call(
        prepare_kernel,
        grid_spec=pltpu.PrefetchScalarGridSpec(
            num_scalar_prefetch=2,
            grid=(GROUP,),
            in_specs=[block(s, n) for s in (0, 1) * 3]
            + [block(s, cols) for s in (0, 1)]
            + [block(s, n) for s in (0, 1) * 3],
            out_specs=[
                pl.BlockSpec((map_rows(n), cols), lambda p, sl, at: (0, 0)),
                per(4 * n), per(5 * n), per(cols), per(cols),
                pl.BlockSpec((None, 2, n, 5 * n), lambda p, sl, at: (p, 0, 0, 0)),
                per(n),
                pl.BlockSpec((4, n, n), lambda p, sl, at: (0, 0, 0)),
            ],
        ),
        out_shape=[
            shape((map_rows(n), cols), BF),
            shape((GROUP, n, 4 * n), BF),
            shape((GROUP, n, 5 * n), BF),
            shape((GROUP, n, cols), F32),
            shape((GROUP, n, cols), F32),
            shape((GROUP, 2, n, 5 * n), BF),
            shape((GROUP, n, n), BF),
            shape((4, n, n), BF),
        ],
        compiler_params=pltpu.CompilerParams(vmem_limit_bytes=VMEM_LIMIT),
        cost_estimate=SHORT,
        name="prepare",
    )(
        slots, place, diag_inv, diag_inv, lower, lower, upper, upper, source, source,
        diagonal, diagonal, minus, minus, plus, plus,
    )


def per_owner(place, pieces, body):
    for owned in range(GROUP):

        @pl.when(place[3] == owned)
        def _(owned=owned):
            body([pieces[owned ^ j] for j in range(GROUP)], owned)


def segment(one, n):
    rows = packed_rows(n)
    return (
        unpack(one, 0, n),
        unpack(one, rows, n),
        unpack(one, 2 * rows, n),
        one[3 * rows : 3 * rows + n, :].astype(F32),
        one[3 * rows + n : 3 * rows + 2 * n, :].astype(F32),
    )


def group_back_kernel(
    place, across, near, next_one, own, a_low, b_out, c_low, g_out, h_out, send_far
):
    n = a_low.shape[0]

    def body(maps, owned):
        (a0, b0, g0, c0, h0), (a1, b1, g1, c1, h1), (a2, b2, g2, c2, h2), (_, b3, g3, _, h3) = (
            segment(one, n) for one in maps
        )
        a = mm(a1, a0).astype(BF)
        b = mm(b0, b1).astype(BF)
        c = mm_fine(a1, c0) + c1
        low_g = mm(b0, mm(g1, a0).astype(BF)) + g0.astype(F32)
        high_g = (mm(b2, mm(g3, a2).astype(BF)) + g2.astype(F32)).astype(BF)
        g = (mm(b, mm(high_g, a).astype(BF)) + low_g).astype(BF)
        low_h = mm_fine(b0, mm_fine(g1, c0) + h1) + h0
        high_h = mm_fine(b2, mm_fine(g3, c2) + h3) + h2
        h = mm_fine(b, mm_fine(high_g, c) + high_h) + low_h
        a_low[...] = a
        c_low[...] = c
        g_out[...] = g
        h_out[...] = h
        send_far[0:n, :] = h.astype(BF)
        through = mm(b, mm(b2, b3).astype(BF)).astype(BF)
        b_out[...] = through
        pack(send_far, n, jnp.where(place[4] == 1, through, g))

    per_owner(place, (own, near, next_one, across), body)


def group_front_kernel(
    place, across, near, next_one, own, a_low, c_low, send, a_out, c_out
):
    n = a_low.shape[0]

    def body(maps, owned):
        (a2, _, _, c2, _), (a3, _, _, c3, _) = (segment(one, n) for one in maps[2:])
        a = mm(a3, a2).astype(BF)
        c = mm_fine(a, c_low[...]) + (mm_fine(a3, c2) + c3)
        send[...] = c.astype(BF)
        c_out[...] = c
        a_out[...] = mm(a, a_low[...]).astype(BF)

    per_owner(place, (own, near, next_one, across), body)


def forward_one_kernel(incoming, a, c, g, h, send, inner):
    send[...] = (mm(a[...], incoming[...]) + c[...]).astype(BF)
    inner[...] = (mm(g[...], incoming[...]) + h[...]).astype(BF)


def turn_kernel(incoming, far, a, b, g, c, h, send, back_in):
    n = a.shape[0]
    front = incoming[...]
    ahead = mm(a[...], front) + c[...]
    back = mm_fine(unpack(far, n, n), ahead) + far[0:n, :].astype(F32)
    send[...] = (mm_fine(b[...], back) + (mm(g[...], front) + h[...])).astype(BF)
    back_in[...] = back.astype(BF)


def through_group(maps, first, n):
    rows = packed_rows(n)
    fronts, inner = [first], [None]
    for one in maps[:-1]:
        shift = one[3 * rows : 3 * rows + n, :].astype(F32)
        fronts.append(mm_fine(unpack(one, 0, n), fronts[-1]) + shift)
    for one, front in zip(maps[1:], fronts[1:]):
        shift = one[3 * rows + n : 3 * rows + 2 * n, :].astype(F32)
        inner.append(mm_fine(unpack(one, 2 * rows, n), front) + shift)
    return fronts, inner


def entering_kernel(
    place, across, near, next_one, own, hop1, hop2, fronts_out, inner_out, leaving, maps
):
    n = hop1.shape[0]
    rows = packed_rows(n)
    which = place[4]
    for distance, piece in enumerate((own, near, next_one, across)):
        maps[lax.bitwise_xor(place[3], jnp.int32(distance))] = piece[...]
    zero = jnp.zeros_like(hop1[...])
    first = jnp.where(which == 1, hop1[...], jnp.where(which == 2, hop2[...], zero)).astype(F32)
    ordered = [maps.at[j] for j in range(GROUP)]
    fronts, inner = through_group(ordered, first, n)
    for j in range(GROUP):
        fronts_out[j] = fronts[j].astype(BF)
        if j:
            inner_out[j] = inner[j]
    shift = ordered[-1][3 * rows : 3 * rows + n, :].astype(F32)
    leaving[...] = (mm_fine(unpack(ordered[-1], 0, n), fronts[-1]) + shift).astype(BF)


def interfaces_kernel(
    place, maps, far, inner_one, hop_three, hop_one, back_two, hop_zero,
    fronts_in, inner_in, out_near, out_next, out_across, out_own, fronts_now, inner_now, backs,
):
    n = hop_one.shape[0]
    rows = packed_rows(n)
    which = place[4]
    zero = jnp.zeros_like(hop_one[...])
    through_one = mm(unpack(far, n, n), hop_zero[...]) + inner_one[...].astype(F32)
    back = jnp.where(
        which == 0, through_one.astype(BF),
        jnp.where(which == 1, hop_one[...], jnp.where(which == 2, back_two[...], zero)),
    ).astype(F32)
    ordered = [maps.at[j] for j in range(GROUP)]

    @pl.when(which == GROUP - 1)
    def _():
        fronts, inner = through_group(ordered, hop_three[...].astype(F32), n)
        for j in range(GROUP):
            fronts_now[j] = fronts[j].astype(BF)
            if j:
                inner_now[j] = inner[j]

    @pl.when(which != GROUP - 1)
    def _():
        for j in range(GROUP):
            fronts_now[j] = fronts_in[j]
            if j:
                inner_now[j] = inner_in[j]

    for j in reversed(range(GROUP)):
        backs[j] = back.astype(BF)
        if j:
            back = mm_fine(unpack(ordered[j], rows, n), back) + inner_now[j]
    for distance, out in enumerate((out_own, out_near, out_next, out_across)):
        peer = lax.bitwise_xor(place[3], jnp.int32(distance))
        out[0:n, :] = fronts_now[peer]
        out[n : 2 * n, :] = backs[peer]


def whole_call(kernel, outs, scalars, *operands, name, cost=SHORT, scratch=()):
    specs = [pl.BlockSpec(memory_space=pltpu.SMEM)] * len(scalars)
    specs += [pl.BlockSpec(memory_space=pltpu.VMEM)] * len(operands)
    return pl.pallas_call(
        kernel,
        in_specs=specs,
        out_specs=[pl.BlockSpec(memory_space=pltpu.VMEM)] * len(outs),
        out_shape=[jax.ShapeDtypeStruct(s, d) for s, d in outs],
        scratch_shapes=scratch,
        compiler_params=pltpu.CompilerParams(vmem_limit_bytes=VMEM_LIMIT),
        cost_estimate=cost,
        name=name,
    )(*scalars, *operands)


def finish_second_kernel(
    place, near, next_one, across, own, first_ops, c, tops, rests, fronts, backs
):
    n = c.shape[1]
    for distance, piece in enumerate((own, near, next_one, across)):
        pencil = lax.bitwise_xor(place[3], jnp.int32(distance))
        fronts[pencil] = piece[0:n, :]
        backs[pencil] = piece[n : 2 * n, :]
    for p in range(GROUP):
        front = fronts[p]
        back = backs[p]
        x1 = c[p] + mm(first_ops[p], jnp.concatenate([front, front, back, back], axis=0))
        tops[p], rests[p] = halves(x1)


def finish_first_kernel(place, fronts, second_ops, y0, tops, rests, beside, firsts):
    n = y0.shape[1]
    for p in range(GROUP):
        front = fronts[p]
        top = tops[p]
        around = jnp.concatenate([front, front, top, top, rests[p]], axis=0)
        firsts[p] = (y0[p] + mm(second_ops[p], around)).astype(BF)
    even = lax.rem(place[1], 2) == 0
    for s, values in enumerate((firsts, tops)):
        beside[s] = jnp.where(even, values[0], values[GROUP - 1])


def row_products(chosen, rows, firsts, tops, backs, partial):
    n = tops.shape[1]
    zero = jnp.zeros(tops.shape[1:], BF)

    def value(s, p):
        if p < 0 or p >= GROUP or s < 0:
            return zero
        return backs[p] if s == 2 else (firsts, tops)[s][p]

    for i, p in enumerate(chosen):
        for s in range(2):
            around = [value(s, p), value(s - 1, p), value(s + 1, p), value(s, p - 1), value(s, p + 1)]
            partial[i, s] = mm(rows[p, s], jnp.concatenate(around, axis=0))


def first_rows_kernel(place, rows, firsts, tops, backs, within, partial):
    even = lax.rem(place[1], 2) == 0
    row_products((0, 1), rows, firsts, tops, backs, partial)
    for s, values in enumerate((firsts, tops)):
        within[s] = jnp.where(even, values[GROUP - 1], values[0])


def second_rows_kernel(slots, rows, firsts, tops, backs, precond, partial):
    row_products((2, 3), rows, firsts, tops, backs, partial)
    for s in range(2):
        for p in range(GROUP):
            precond[slots[s, p]] = (firsts, tops)[s][p]


def edge_jacobian_kernel(slots, place, beside, below, within, partial_a, partial_b, lowers, sides, jac):
    even = lax.rem(place[1], 2) == 0
    low = [jnp.where(even, beside[s], within[s]) for s in range(2)]
    high = [jnp.where(even, within[s], beside[s]) for s in range(2)]
    left = jnp.where(place[1] == 0, 0.0, 1.0).astype(F32)
    right = jnp.where(place[1] == place[2] - 1, 0.0, 1.0).astype(F32)
    start = jnp.where(place[0] == 0, 0.0, 1.0).astype(F32)
    for s in range(2):
        for p in range(GROUP):
            total = partial_a[p, s] if p < 2 else partial_b[p - 2, s]
            if s == 0:
                total = total + start * mm(lowers[p], below[p])
            if p == 0:
                total = total + left * mm(sides[s], low[s])
            if p == GROUP - 1:
                total = total + right * mm(sides[s + 2], high[s])
            jac[slots[s, p]] = total.astype(BF)


def local(right_side, diag_inv, diag_blk, lower_blk, upper_blk, cross_minus, cross_plus, elem_slot):
    n, cols = right_side.shape[2:]
    source, inverse, diagonal, lower, upper, minus, plus = (
        pltpu.with_memory_space_constraint(
            values.reshape((-1,) + values.shape[2:]), pltpu.HBM
        )
        for values in (
            right_side, diag_inv, diag_blk, lower_blk, upper_blk, cross_minus, cross_plus
        )
    )
    count = lax.axis_size("sweep")
    across = lax.axis_size("cross")
    sweep_at = lax.axis_index("sweep")
    place = jnp.stack(
        [
            sweep_at, lax.axis_index("cross"), jnp.int32(across),
            lax.rem(sweep_at, GROUP), lax.div(sweep_at, GROUP),
        ]
    ).astype(jnp.int32)
    def hop(values, *moves):
        pairs = [(a * GROUP + k, b * GROUP + k) for a, b in moves for k in range(GROUP)]
        return lax.ppermute(values, "sweep", pairs)

    def to_peer(values, distance):
        return lax.ppermute(values, "sweep", [(i, i ^ distance) for i in range(count)])

    vec, vec32, mat = ((n, cols), BF), ((n, cols), F32), ((n, n), BF)
    maps = [None] * GROUP
    for distance in (3, 1, 2):
        piece = local_map(elem_slot, place, inverse, lower, upper, source, distance)
        maps[distance] = to_peer(piece, distance)
    maps[0], first_ops, second_ops, c_own, y_own, rows, lowers, sides = prepare(
        elem_slot, place, inverse, lower, upper, source, diagonal, minus, plus
    )
    pieces = (maps[3], maps[1], maps[2], maps[0])

    a_low, b, c_low, g, h, send_far = whole_call(
        group_back_kernel, [mat, mat, vec32, mat, vec32, ((n + packed_rows(n), cols), BF)],
        [place], *pieces, name="group_back",
    )
    far = hop(send_far, (3, 2), (1, 0))
    send, a, c = whole_call(
        group_front_kernel, [vec, mat, vec32], [place],
        *pieces, a_low, c_low, name="group_front",
    )
    hop1 = hop(send, (0, 1))
    send, inner_one = whole_call(
        forward_one_kernel, [vec, vec], [], hop1, a, c, g, h, name="forward_one"
    )
    hop2 = hop(send, (1, 2))
    inner_one = hop(inner_one, (1, 0))
    send, back_two = whole_call(
        turn_kernel, [vec, vec], [], hop2, far, a, b, g, c, h, name="turn"
    )
    hop_zero = hop(send, (2, 0))
    hop_one = hop(send, (2, 1))
    fronts, inner, ahead, ordered = whole_call(
        entering_kernel,
        [
            ((GROUP, n, cols), BF), ((GROUP, n, cols), F32), vec,
            ((GROUP, map_rows(n), cols), BF),
        ],
        [place],
        *pieces, hop1, hop2, name="entering",
    )
    hop_three = hop(ahead, (2, 3))
    both = ((2 * n, cols), BF)
    ends = whole_call(
        interfaces_kernel, [both] * GROUP, [place], ordered, far, inner_one,
        hop_three, hop_one, back_two, hop_zero, fronts, inner, name="interfaces",
        scratch=[
            pltpu.VMEM((GROUP, n, cols), BF), pltpu.VMEM((GROUP, n, cols), F32),
            pltpu.VMEM((GROUP, n, cols), BF),
        ],
    )
    ends = [to_peer(values, distance) for distance, values in zip((1, 2, 3), ends)] + [ends[3]]

    pair = ((2, n, cols), BF)
    four = ((GROUP, n, cols), BF)
    tops, rests, fronts, backs = whole_call(
        finish_second_kernel, [four] * 4, [place], *ends, first_ops, c_own, name="finish_second"
    )
    below = lax.ppermute(tops, "sweep", [(i, (i + 1) % count) for i in range(count)])
    beside, firsts = whole_call(
        finish_first_kernel, [pair, four], [place],
        fronts, second_ops, y_own, tops, rests, name="finish_first",
    )
    aside = []
    for i in range(1, across - 1, 2):
        aside += [(i, i + 1), (i + 1, i)]
    beside = lax.ppermute(beside, "cross", aside)
    part = ((2, 2, n, cols), F32)
    within, partial_a = whole_call(
        first_rows_kernel, [pair, part], [place], rows, firsts, tops, backs, name="first_rows"
    )
    within = lax.ppermute(within, "cross", [(i, i ^ 1) for i in range(across)])
    every = ((2 * GROUP, n, cols), BF)
    precond, partial_b = whole_call(
        second_rows_kernel, [every, part], [elem_slot], rows, firsts, tops, backs, name="second_rows"
    )
    (jac,) = whole_call(
        edge_jacobian_kernel, [every], [elem_slot, place],
        beside, below, within, partial_a, partial_b, lowers, sides, name="edge_jacobian",
    )
    return precond.reshape(right_side.shape), jac.reshape(right_side.shape)


def solution(mesh):
    blocks = P("sweep", "cross", None, None)
    in_specs = (blocks,) * 7 + (P("sweep", "cross"),)
    return jax.shard_map(
        local, mesh=mesh, in_specs=in_specs, out_specs=(blocks, blocks), check_vma=False
    )
```

```python
import functools

import jax
import jax.numpy as jnp
from jax import lax
from jax.experimental import pallas as pl
from jax.experimental.pallas import tpu as pltpu
from jax.sharding import PartitionSpec as P

BF = jnp.bfloat16
F32 = jnp.float32
GROUP = 4
VMEM_LIMIT = 28 << 20
LONG = pl.CostEstimate(flops=10**10, transcendentals=0, bytes_accessed=1024)
SHORT = pl.CostEstimate(flops=1024, transcendentals=0, bytes_accessed=1024)


def mm(a, b):
    return jnp.dot(a, b, preferred_element_type=F32)


def mm_fine(a, x):
    width = x.shape[1]
    top = x.astype(BF)
    rest = (x - top.astype(F32)).astype(BF)
    both = mm(a, jnp.concatenate([top, rest], axis=1))
    return both[:, :width] + both[:, width:]


def packed_rows(n):
    return 2 * n + n // 2


def pack(ref, base, mat):
    n = mat.shape[0]
    half = n // 2
    ref[base : base + n, :] = mat[:, 0:128]
    ref[base + n : base + 2 * n, :] = mat[:, 128:256]
    ref[base + 2 * n : base + 2 * n + half, 0:64] = mat[0:half, 256:320]
    ref[base + 2 * n : base + 2 * n + half, 64:128] = mat[half:n, 256:320]


def unpack(ref, base, n):
    half = n // 2
    tail = ref[base + 2 * n : base + 2 * n + half, :]
    last = jnp.concatenate([tail[:, 0:64], tail[:, 64:128]], axis=0)
    return jnp.concatenate(
        [ref[base : base + n, :], ref[base + n : base + 2 * n, :], last], axis=1
    )


def map_rows(n):
    return 3 * packed_rows(n) + 2 * n


def local_map_kernel(slots, place, d0, d1, l0, l1, u0, u1, r0, r1, out):
    n = d0.shape[0]
    rows = packed_rows(n)
    inv0, inv1 = d0[...], d1[...]
    e0 = mm(inv0, l0[...])
    e1 = mm(inv1, l1[...]).astype(BF)
    h0 = mm(inv0, u0[...]).astype(BF)
    h1 = mm(inv1, u1[...]).astype(BF)
    y0 = mm(inv0, r0[...])
    y1 = mm(inv1, r1[...])
    a = mm(e1, e0.astype(BF)).astype(BF)
    c = y1 - mm_fine(e1, y0)
    b = mm(h0, h1).astype(BF)
    g = -(e0 + mm(h0, a))
    h = y0 - mm_fine(h0, c)
    pack(out, 0, a)
    pack(out, rows, b)
    pack(out, 2 * rows, g.astype(BF))
    out[3 * rows : 3 * rows + n, :] = c.astype(BF)
    out[3 * rows + n : 3 * rows + 2 * n, :] = h.astype(BF)


def stored(slab, pencil, height, width):
    return pl.BlockSpec(
        (None, height, width), lambda i, sl, at: (sl[slab, pencil(at)], 0, 0)
    )


def constant(shape):
    return pl.BlockSpec(shape, lambda i, sl, at: (0,) * len(shape))


def element_call(kernel, in_specs, out_shape, slots, place, *operands, name, cost=SHORT):
    return pl.pallas_call(
        kernel,
        grid_spec=pltpu.PrefetchScalarGridSpec(
            num_scalar_prefetch=2,
            grid=(1,),
            in_specs=in_specs,
            out_specs=[constant(o.shape) for o in out_shape],
        ),
        out_shape=out_shape,
        compiler_params=pltpu.CompilerParams(vmem_limit_bytes=VMEM_LIMIT),
        cost_estimate=cost,
        name=name,
    )(slots, place, *operands)


def local_map(slots, place, diag_inv, lower, upper, source, distance):
    n, cols = source.shape[1:]

    def pencil(at):
        return lax.bitwise_xor(at[3], jnp.int32(distance))

    (out,) = element_call(
        local_map_kernel,
        [stored(s, pencil, n, n) for s in (0, 1, 0, 1, 0, 1)]
        + [stored(s, pencil, n, cols) for s in (0, 1)],
        [jax.ShapeDtypeStruct((map_rows(n), cols), BF)],
        slots, place, diag_inv, diag_inv, lower, lower, upper, upper, source, source,
        name="local_map",
    )
    return out


def halves(x):
    top = x.astype(BF)
    return top, (x - top.astype(F32)).astype(BF)


def prepare_kernel(slots, place, *refs):
    d0, d1, l0, l1, u0, u1, r0, r1 = refs[0:8]
    diags, minuses, pluses = refs[8:10], refs[10:12], refs[12:14]
    out, first_ops, second_ops, c_out, y_out, rows_out, lowers, sides = refs[14:]
    n = d0.shape[0]
    pencil = pl.program_id(0)
    for s in range(2):
        row = (diags[s], (l0, l1)[s], (u0, u1)[s], minuses[s], pluses[s])
        for t, block in enumerate(row):
            rows_out[s, :, t * n : (t + 1) * n] = block[...]
    lowers[...] = l0[...]

    @pl.when(pencil == 0)
    def _():
        for s in range(2):
            sides[s] = minuses[s][...]

    @pl.when(pencil == GROUP - 1)
    def _():
        for s in range(2):
            sides[s + 2] = pluses[s][...]

    rows = packed_rows(n)
    inv0, inv1 = d0[...], d1[...]
    e0 = mm(inv0, l0[...])
    e0_top, e0_rest = halves(e0)
    e1_top, e1_rest = halves(mm(inv1, l1[...]))
    h0_top, h0_rest = halves(mm(inv0, u0[...]))
    h1_top, h1_rest = halves(mm(inv1, u1[...]))
    y0 = mm(inv0, r0[...])
    a = mm(e1_top, e0_top) + (mm(e1_top, e0_rest) + mm(e1_rest, e0_top))
    c = mm(inv1, r1[...]) - (mm_fine(e1_top, y0) + mm(e1_rest, y0.astype(BF)))
    a_top, a_rest = halves(a)
    for t, part in enumerate((a_top, a_rest, -h1_top, -h1_rest)):
        first_ops[:, t * n : (t + 1) * n] = part
    for t, part in enumerate((-e0_top, -e0_rest, -h0_top, -h0_rest, -h0_top)):
        second_ops[:, t * n : (t + 1) * n] = part
    c_out[...] = c
    y_out[...] = y0

    @pl.when(pencil == place[3])
    def _():
        pack(out, 0, a_top)
        pack(out, rows, mm(h0_top, h1_top).astype(BF))
        pack(out, 2 * rows, (-(e0 + mm(h0_top, a_top))).astype(BF))
        out[3 * rows : 3 * rows + n, :] = c.astype(BF)
        out[3 * rows + n : 3 * rows + 2 * n, :] = (y0 - mm_fine(h0_top, c)).astype(BF)


def prepare(slots, place, diag_inv, lower, upper, source, diagonal, minus, plus):
    n, cols = source.shape[1:]

    def block(slab, width):
        return pl.BlockSpec((None, n, width), lambda p, sl, at: (sl[slab, p], 0, 0))

    def per(width):
        return pl.BlockSpec((None, n, width), lambda p, sl, at: (p, 0, 0))

    shape = jax.ShapeDtypeStruct
    return pl.pallas_call(
        prepare_kernel,
        grid_spec=pltpu.PrefetchScalarGridSpec(
            num_scalar_prefetch=2,
            grid=(GROUP,),
            in_specs=[block(s, n) for s in (0, 1) * 3]
            + [block(s, cols) for s in (0, 1)]
            + [block(s, n) for s in (0, 1) * 3],
            out_specs=[
                pl.BlockSpec((map_rows(n), cols), lambda p, sl, at: (0, 0)),
                per(4 * n), per(5 * n), per(cols), per(cols),
                pl.BlockSpec((None, 2, n, 5 * n), lambda p, sl, at: (p, 0, 0, 0)),
                per(n),
                pl.BlockSpec((4, n, n), lambda p, sl, at: (0, 0, 0)),
            ],
        ),
        out_shape=[
            shape((map_rows(n), cols), BF),
            shape((GROUP, n, 4 * n), BF),
            shape((GROUP, n, 5 * n), BF),
            shape((GROUP, n, cols), F32),
            shape((GROUP, n, cols), F32),
            shape((GROUP, 2, n, 5 * n), BF),
            shape((GROUP, n, n), BF),
            shape((4, n, n), BF),
        ],
        compiler_params=pltpu.CompilerParams(vmem_limit_bytes=VMEM_LIMIT),
        cost_estimate=SHORT,
        name="prepare",
    )(
        slots, place, diag_inv, diag_inv, lower, lower, upper, upper, source, source,
        diagonal, diagonal, minus, minus, plus, plus,
    )


def per_owner(place, pieces, body):
    for owned in range(GROUP):

        @pl.when(place[3] == owned)
        def _(owned=owned):
            body([pieces[owned ^ j] for j in range(GROUP)], owned)


def segment(one, n):
    rows = packed_rows(n)
    return (
        unpack(one, 0, n),
        unpack(one, rows, n),
        unpack(one, 2 * rows, n),
        one[3 * rows : 3 * rows + n, :].astype(F32),
        one[3 * rows + n : 3 * rows + 2 * n, :].astype(F32),
    )


def group_back_kernel(
    place, across, near, next_one, own, a_low, b_out, c_low, g_out, h_out, send_far
):
    n = a_low.shape[0]

    def body(maps, owned):
        (a0, b0, g0, c0, h0), (a1, b1, g1, c1, h1), (a2, b2, g2, c2, h2), (_, b3, g3, _, h3) = (
            segment(one, n) for one in maps
        )
        a = mm(a1, a0).astype(BF)
        b = mm(b0, b1).astype(BF)
        c = mm_fine(a1, c0) + c1
        low_g = mm(b0, mm(g1, a0).astype(BF)) + g0.astype(F32)
        high_g = (mm(b2, mm(g3, a2).astype(BF)) + g2.astype(F32)).astype(BF)
        g = (mm(b, mm(high_g, a).astype(BF)) + low_g).astype(BF)
        low_h = mm_fine(b0, mm_fine(g1, c0) + h1) + h0
        high_h = mm_fine(b2, mm_fine(g3, c2) + h3) + h2
        h = mm_fine(b, mm_fine(high_g, c) + high_h) + low_h
        a_low[...] = a
        c_low[...] = c
        g_out[...] = g
        h_out[...] = h
        send_far[0:n, :] = h.astype(BF)
        through = mm(b, mm(b2, b3).astype(BF)).astype(BF)
        b_out[...] = through
        pack(send_far, n, jnp.where(place[4] == 1, through, g))

    per_owner(place, (own, near, next_one, across), body)


def group_front_kernel(
    place, across, near, next_one, own, a_low, c_low, send, a_out, c_out
):
    n = a_low.shape[0]

    def body(maps, owned):
        (a2, _, _, c2, _), (a3, _, _, c3, _) = (segment(one, n) for one in maps[2:])
        a = mm(a3, a2).astype(BF)
        c = mm_fine(a, c_low[...]) + (mm_fine(a3, c2) + c3)
        send[...] = c.astype(BF)
        c_out[...] = c
        a_out[...] = mm(a, a_low[...]).astype(BF)

    per_owner(place, (own, near, next_one, across), body)


def forward_one_kernel(incoming, a, c, g, h, send, inner):
    send[...] = (mm(a[...], incoming[...]) + c[...]).astype(BF)
    inner[...] = (mm(g[...], incoming[...]) + h[...]).astype(BF)


def turn_kernel(incoming, far, a, b, g, c, h, send, back_in):
    n = a.shape[0]
    front = incoming[...]
    ahead = mm(a[...], front) + c[...]
    back = mm_fine(unpack(far, n, n), ahead) + far[0:n, :].astype(F32)
    send[...] = (mm_fine(b[...], back) + (mm(g[...], front) + h[...])).astype(BF)
    back_in[...] = back.astype(BF)


def through_group(maps, first, n):
    rows = packed_rows(n)
    fronts, inner = [first], [None]
    for one in maps[:-1]:
        shift = one[3 * rows : 3 * rows + n, :].astype(F32)
        fronts.append(mm_fine(unpack(one, 0, n), fronts[-1]) + shift)
    for one, front in zip(maps[1:], fronts[1:]):
        shift = one[3 * rows + n : 3 * rows + 2 * n, :].astype(F32)
        inner.append(mm_fine(unpack(one, 2 * rows, n), front) + shift)
    return fronts, inner


def entering_kernel(
    place, across, near, next_one, own, hop1, hop2, fronts_out, inner_out, leaving, maps
):
    n = hop1.shape[0]
    rows = packed_rows(n)
    which = place[4]
    for distance, piece in enumerate((own, near, next_one, across)):
        maps[lax.bitwise_xor(place[3], jnp.int32(distance))] = piece[...]
    zero = jnp.zeros_like(hop1[...])
    first = jnp.where(which == 1, hop1[...], jnp.where(which == 2, hop2[...], zero)).astype(F32)
    ordered = [maps.at[j] for j in range(GROUP)]
    fronts, inner = through_group(ordered, first, n)
    for j in range(GROUP):
        fronts_out[j] = fronts[j].astype(BF)
        if j:
            inner_out[j] = inner[j]
    shift = ordered[-1][3 * rows : 3 * rows + n, :].astype(F32)
    leaving[...] = (mm_fine(unpack(ordered[-1], 0, n), fronts[-1]) + shift).astype(BF)


def interfaces_kernel(
    place, maps, far, inner_one, hop_three, hop_one, back_two, hop_zero,
    fronts_in, inner_in, out_near, out_next, out_across, out_own, fronts_now, inner_now, backs,
):
    n = hop_one.shape[0]
    rows = packed_rows(n)
    which = place[4]
    zero = jnp.zeros_like(hop_one[...])
    through_one = mm(unpack(far, n, n), hop_zero[...]) + inner_one[...].astype(F32)
    back = jnp.where(
        which == 0, through_one.astype(BF),
        jnp.where(which == 1, hop_one[...], jnp.where(which == 2, back_two[...], zero)),
    ).astype(F32)
    ordered = [maps.at[j] for j in range(GROUP)]

    @pl.when(which == GROUP - 1)
    def _():
        fronts, inner = through_group(ordered, hop_three[...].astype(F32), n)
        for j in range(GROUP):
            fronts_now[j] = fronts[j].astype(BF)
            if j:
                inner_now[j] = inner[j]

    @pl.when(which != GROUP - 1)
    def _():
        for j in range(GROUP):
            fronts_now[j] = fronts_in[j]
            if j:
                inner_now[j] = inner_in[j]

    for j in reversed(range(GROUP)):
        backs[j] = back.astype(BF)
        if j:
            back = mm_fine(unpack(ordered[j], rows, n), back) + inner_now[j]
    for distance, out in enumerate((out_own, out_near, out_next, out_across)):
        peer = lax.bitwise_xor(place[3], jnp.int32(distance))
        out[0:n, :] = fronts_now[peer]
        out[n : 2 * n, :] = backs[peer]


def whole_call(kernel, outs, scalars, *operands, name, cost=SHORT, scratch=()):
    specs = [pl.BlockSpec(memory_space=pltpu.SMEM)] * len(scalars)
    specs += [pl.BlockSpec(memory_space=pltpu.VMEM)] * len(operands)
    return pl.pallas_call(
        kernel,
        in_specs=specs,
        out_specs=[pl.BlockSpec(memory_space=pltpu.VMEM)] * len(outs),
        out_shape=[jax.ShapeDtypeStruct(s, d) for s, d in outs],
        scratch_shapes=scratch,
        compiler_params=pltpu.CompilerParams(vmem_limit_bytes=VMEM_LIMIT),
        cost_estimate=cost,
        name=name,
    )(*scalars, *operands)


def finish_second_kernel(
    place, near, next_one, across, own, first_ops, c, tops, rests, fronts, backs
):
    n = c.shape[1]
    for distance, piece in enumerate((own, near, next_one, across)):
        pencil = lax.bitwise_xor(place[3], jnp.int32(distance))
        fronts[pencil] = piece[0:n, :]
        backs[pencil] = piece[n : 2 * n, :]
    for p in range(GROUP):
        front = fronts[p]
        back = backs[p]
        x1 = c[p] + mm(first_ops[p], jnp.concatenate([front, front, back, back], axis=0))
        tops[p], rests[p] = halves(x1)


def finish_first_kernel(fronts, second_ops, y0, tops, rests, firsts):
    n = y0.shape[1]
    for p in range(GROUP):
        front = fronts[p]
        top = tops[p]
        around = jnp.concatenate([front, front, top, top, rests[p]], axis=0)
        firsts[p] = (y0[p] + mm(second_ops[p], around)).astype(BF)


def row_products(chosen, rows, firsts, tops, backs, partial):
    n = tops.shape[1]
    zero = jnp.zeros(tops.shape[1:], BF)

    def value(s, p):
        if p < 0 or p >= GROUP or s < 0:
            return zero
        return backs[p] if s == 2 else (firsts, tops)[s][p]

    for i, p in enumerate(chosen):
        for s in range(2):
            around = [value(s, p), value(s - 1, p), value(s + 1, p), value(s, p - 1), value(s, p + 1)]
            partial[i, s] = mm(rows[p, s], jnp.concatenate(around, axis=0))


def first_rows_kernel(place, rows, firsts, tops, backs, beside, within, partial):
    even = lax.rem(place[1], 2) == 0
    row_products((0, 1), rows, firsts, tops, backs, partial)
    for s, values in enumerate((firsts, tops)):
        within[s] = jnp.where(even, values[GROUP - 1], values[0])
        beside[s] = jnp.where(even, values[0], values[GROUP - 1])


def second_rows_kernel(slots, rows, firsts, tops, backs, precond, partial):
    row_products((2, 3), rows, firsts, tops, backs, partial)
    for s in range(2):
        for p in range(GROUP):
            precond[slots[s, p]] = (firsts, tops)[s][p]


def edge_jacobian_kernel(slots, place, beside, below, within, partial_a, partial_b, lowers, sides, jac):
    even = lax.rem(place[1], 2) == 0
    low = [jnp.where(even, beside[s], within[s]) for s in range(2)]
    high = [jnp.where(even, within[s], beside[s]) for s in range(2)]
    left = jnp.where(place[1] == 0, 0.0, 1.0).astype(F32)
    right = jnp.where(place[1] == place[2] - 1, 0.0, 1.0).astype(F32)
    start = jnp.where(place[0] == 0, 0.0, 1.0).astype(F32)
    for s in range(2):
        for p in range(GROUP):
            total = partial_a[p, s] if p < 2 else partial_b[p - 2, s]
            if s == 0:
                total = total + start * mm(lowers[p], below[p])
            if p == 0:
                total = total + left * mm(sides[s], low[s])
            if p == GROUP - 1:
                total = total + right * mm(sides[s + 2], high[s])
            jac[slots[s, p]] = total.astype(BF)


def local(right_side, diag_inv, diag_blk, lower_blk, upper_blk, cross_minus, cross_plus, elem_slot):
    n, cols = right_side.shape[2:]
    source, inverse, diagonal, lower, upper, minus, plus = (
        pltpu.with_memory_space_constraint(
            values.reshape((-1,) + values.shape[2:]), pltpu.HBM
        )
        for values in (
            right_side, diag_inv, diag_blk, lower_blk, upper_blk, cross_minus, cross_plus
        )
    )
    count = lax.axis_size("sweep")
    across = lax.axis_size("cross")
    sweep_at = lax.axis_index("sweep")
    place = jnp.stack(
        [
            sweep_at, lax.axis_index("cross"), jnp.int32(across),
            lax.rem(sweep_at, GROUP), lax.div(sweep_at, GROUP),
        ]
    ).astype(jnp.int32)
    def hop(values, *moves):
        pairs = [(a * GROUP + k, b * GROUP + k) for a, b in moves for k in range(GROUP)]
        return lax.ppermute(values, "sweep", pairs)

    def to_peer(values, distance):
        return lax.ppermute(values, "sweep", [(i, i ^ distance) for i in range(count)])

    vec, vec32, mat = ((n, cols), BF), ((n, cols), F32), ((n, n), BF)
    maps = [None] * GROUP
    for distance in (3, 1, 2):
        piece = local_map(elem_slot, place, inverse, lower, upper, source, distance)
        maps[distance] = to_peer(piece, distance)
    maps[0], first_ops, second_ops, c_own, y_own, rows, lowers, sides = prepare(
        elem_slot, place, inverse, lower, upper, source, diagonal, minus, plus
    )
    pieces = (maps[3], maps[1], maps[2], maps[0])

    a_low, b, c_low, g, h, send_far = whole_call(
        group_back_kernel, [mat, mat, vec32, mat, vec32, ((n + packed_rows(n), cols), BF)],
        [place], *pieces, name="group_back",
    )
    far = hop(send_far, (3, 2), (1, 0))
    send, a, c = whole_call(
        group_front_kernel, [vec, mat, vec32], [place],
        *pieces, a_low, c_low, name="group_front",
    )
    hop1 = hop(send, (0, 1))
    send, inner_one = whole_call(
        forward_one_kernel, [vec, vec], [], hop1, a, c, g, h, name="forward_one"
    )
    hop2 = hop(send, (1, 2))
    inner_one = hop(inner_one, (1, 0))
    send, back_two = whole_call(
        turn_kernel, [vec, vec], [], hop2, far, a, b, g, c, h, name="turn"
    )
    hop_zero = hop(send, (2, 0))
    hop_one = hop(send, (2, 1))
    fronts, inner, ahead, ordered = whole_call(
        entering_kernel,
        [
            ((GROUP, n, cols), BF), ((GROUP, n, cols), F32), vec,
            ((GROUP, map_rows(n), cols), BF),
        ],
        [place],
        *pieces, hop1, hop2, name="entering",
    )
    hop_three = hop(ahead, (2, 3))
    both = ((2 * n, cols), BF)
    ends = whole_call(
        interfaces_kernel, [both] * GROUP, [place], ordered, far, inner_one,
        hop_three, hop_one, back_two, hop_zero, fronts, inner, name="interfaces",
        scratch=[
            pltpu.VMEM((GROUP, n, cols), BF), pltpu.VMEM((GROUP, n, cols), F32),
            pltpu.VMEM((GROUP, n, cols), BF),
        ],
    )
    ends = [to_peer(values, distance) for distance, values in zip((1, 2, 3), ends)] + [ends[3]]

    pair = ((2, n, cols), BF)
    four = ((GROUP, n, cols), BF)
    tops, rests, fronts, backs = whole_call(
        finish_second_kernel, [four] * 4, [place], *ends, first_ops, c_own, name="finish_second"
    )
    below = lax.ppermute(tops, "sweep", [(i, (i + 1) % count) for i in range(count)])
    (firsts,) = whole_call(
        finish_first_kernel, [four], [],
        fronts, second_ops, y_own, tops, rests, name="finish_first",
    )
    part = ((2, 2, n, cols), F32)
    beside, within, partial_a = whole_call(
        first_rows_kernel, [pair, pair, part], [place], rows, firsts, tops, backs, name="first_rows"
    )
    aside = []
    for i in range(1, across - 1, 2):
        aside += [(i, i + 1), (i + 1, i)]
    beside = lax.ppermute(beside, "cross", aside)
    within = lax.ppermute(within, "cross", [(i, i ^ 1) for i in range(across)])
    every = ((2 * GROUP, n, cols), BF)
    precond, partial_b = whole_call(
        second_rows_kernel, [every, part], [elem_slot], rows, firsts, tops, backs, name="second_rows"
    )
    (jac,) = whole_call(
        edge_jacobian_kernel, [every], [elem_slot, place],
        beside, below, within, partial_a, partial_b, lowers, sides, name="edge_jacobian",
    )
    return precond.reshape(right_side.shape), jac.reshape(right_side.shape)


def solution(mesh):
    blocks = P("sweep", "cross", None, None)
    in_specs = (blocks,) * 7 + (P("sweep", "cross"),)
    return jax.shard_map(
        local, mesh=mesh, in_specs=in_specs, out_specs=(blocks, blocks), check_vma=False
    )
```
